128 devices in a mesh: rows: 2 (over core), head: 4 (over x), cluster: 16 (over y, z).
Axes of the slice: x: 4, y: 4, z: 4, core: 2. Of those that a mesh axis runs over, the one named last changes fastest.
Arguments:
- queries: bfloat16 [4, 512, 8192], P(None, ('rows', 'cluster'), 'head')
- new_keys: bfloat16 [4, 512, 1024], P(None, ('rows', 'cluster'), 'head'), may hold values from -6 to 6
- new_values: bfloat16 [4, 512, 1024], P(None, ('rows', 'cluster'), 'head'), may hold values from -6 to 6
- key_cache: bfloat16 [512, 8, 256, 128], P(('rows', 'cluster'), 'head'), may hold values from -6 to 6
- value_cache: bfloat16 [512, 8, 256, 128], P(('rows', 'cluster'), 'head'), may hold values from -6 to 6
- lengths: int32 [512], P(('rows', 'cluster')), may hold values from 1 to 256, as said below
- residual_in: bfloat16 [4, 512, 8192], P(None, 'rows', 'cluster')
- out_weight: bfloat16 [8192, 8192], P('head', 'cluster'), may hold values from -0.0625 to 0.0625
- norm_gain: float32 [8192], P('cluster'), may hold values from 0.5 to 1.5
- top_weight: bfloat16 [8192, 80], P('cluster')
- leaf_weight: bfloat16 [80, 8192, 1024], P('cluster', None, ('rows', 'head'))
- cluster_ids: int32 [4, 512, 1], replicated, may hold values from 0 to 79; in each aligned block of 256 rows (0 to 255, 256 to 511, ..., all dimensions but the last counted through in order) at most 12 rows name the same one
- targets: int32 [4, 512], replicated, may hold values from 0 to 1023
Outputs:
- log_prob: float32 [4, 512], P(None, ('rows', 'cluster'))
The draws below stay inside these ranges and needn't reach their ends.
Inputs may be any that keep to these rules, and one draw needn't show every extreme that they name: `cluster_ids`: in each step and each aligned block of 256 rows, no cluster is named by more than 12 rows, a bound that some block reaches. `lengths`: every device's 16 rows include one of length 256.
All inputs are finite; a program needn't handle non-finite values.
Results may differ from the reference program's by a relative error of at most 0.0011.
Values may be sent and summed in bfloat16 or wider, within the bound.
No kernel may reach another device: no remote copies, remote signals or barrier semaphores. Data moves between devices by JAX's collectives and lax.ppermute only.
A program may use at most 128 MiB of HBM per device.

```python
import math
from functools import partial
import jax
import jax.numpy as jnp
import numpy as np
from jax import lax

D = 8192
HEADS = 64
KV = 8
HD = 128
CLUSTERS = 80
LEAF = 1024
STEPS = 4
ROW_DEV = 16
CACHE = 256
RGROUP = 256
ROWS = 512
MOST = 12


def draw_queries(key, part):
    first = jax.random.fold_in(key, 0)
    shape = (STEPS, ROWS, HEADS * HD)
    return jnp.clip(jax.random.normal(first, shape, jnp.float32), -6.0, 6.0).astype(jnp.bfloat16)


def draw_lengths(key, part):
    first, second = jax.random.split(key)
    groups = ROWS // ROW_DEV
    drawn = jax.random.randint(first, (groups, ROW_DEV), 1, CACHE + 1)
    position = jax.random.randint(second, (groups, 1), 0, ROW_DEV)
    drawn = jnp.where(jnp.arange(ROW_DEV)[None, :] == position, CACHE, drawn)
    return drawn.reshape(ROWS).astype(jnp.int32)


def draw_residual_in(key, part):
    first = jax.random.fold_in(key, 0)
    shape = (STEPS, ROWS, D)
    column_scale = jnp.exp(math.log(3.0) * jnp.arange(D, dtype=jnp.float32) / D)
    base = jnp.clip(jax.random.normal(first, shape, jnp.float32), -6.0, 6.0)
    return (base * column_scale).astype(jnp.bfloat16)


def draw_top_weight(key, part):
    first = jax.random.fold_in(key, 0)
    base = jnp.clip(jax.random.normal(first, (D, CLUSTERS), jnp.float32), -6.0, 6.0) / math.sqrt(D)
    return (base * 3.0).astype(jnp.bfloat16)


def draw_leaf_weight(key, part):
    first = jax.random.fold_in(key, 0)
    base = jnp.clip(jax.random.normal(first, (CLUSTERS, D, LEAF), jnp.float32), -6.0, 6.0) / math.sqrt(D)
    return (base * 3.0).astype(jnp.bfloat16)


def set_ends(values, rng, low, largest):
    dims = values.shape
    index_at = [jax.random.randint(jax.random.fold_in(rng, axis), (), 0, dims[axis]) for axis in range(len(dims))]
    values = values.at[tuple(index_at)].set(low)
    longest = dims.index(max(dims))
    index_at[longest] = (index_at[longest] + 1) % dims[longest]
    return values.at[tuple(index_at)].set(largest)


def block_levels(rng, extent, cuts, low, largest):
    loudness = 1.0
    for dim, shards_of in cuts:
        steps = jax.random.uniform(jax.random.fold_in(jax.random.fold_in(rng, 6), dim), (shards_of,), jnp.float32, low / len(cuts), largest / len(cuts))
        loudness = loudness * jnp.repeat(jnp.exp(steps), extent[dim] // shards_of).reshape((-1,) + (1,) * (len(extent) - 1 - dim))
    return loudness


def deal_out(key, own, number, rows, number_of, top, most, skew):
    sequence = jax.random.permutation(key, number_of)
    crowded, usual = shares(number_of, rows * top, most, skew, True), shares(number_of, rows * top, most, skew, False)
    places = jnp.arange(number_of)

    def named(sizes, offset_by):
        used = int((sizes > 0).sum())
        fixed = max(1, used // 4)
        moved = fixed + (places - fixed + offset_by * (used - fixed)) % max(1, number_of - fixed)
        return jnp.zeros((number_of,), jnp.int32).at[sequence[jnp.where(places < fixed, places, moved)]].set(jnp.asarray(sizes, jnp.int32))

    sizes = jnp.where(number % 4 == 0, named(crowded, number // 4), named(usual, number - number // 4 - 1))
    mixed = jax.random.permutation(jax.random.fold_in(own, 3), number_of)
    giver, receiver = mixed[0:number_of // 2 * 2:2], mixed[1:number_of // 2 * 2:2]
    slack = jnp.minimum(sizes[giver] - 1, most - sizes[receiver]) // 2
    slack = jnp.where((giver == sequence[0]) | (receiver == sequence[0]) | (sizes[receiver] == 0), 0, jnp.maximum(slack, 0))
    moved = jax.random.randint(jax.random.fold_in(own, 4), (number_of // 2,), 0, 1 << 20) % (slack + 1)
    sizes = sizes.at[giver].add(-moved).at[receiver].add(moved)
    members = jnp.searchsorted(jnp.cumsum(sizes), jnp.arange(rows * top), side="right").astype(jnp.int32)
    grid = members.reshape(top, rows).T
    grid = grid[jax.random.permutation(jax.random.fold_in(own, 1), rows)]
    offset_by = jax.random.randint(jax.random.fold_in(own, 2), (rows, 1), 0, top)
    return jnp.take_along_axis(grid, (jnp.arange(top)[None, :] + offset_by) % top, axis=1)


def shares(amount, total, bound, lean, full):
    weights = [(1 << 20) // math.isqrt(standing ** lean) + 1 for standing in range(1, amount + 1)]
    largest = bound if full else min(bound, max(-(-total // amount), total * weights[0] // sum(weights)))
    least = 1 if total - largest >= amount - 1 else 0
    holding, spare = [largest] + [least] * (amount - 1), total - largest - least * (amount - 1)
    while spare > 0:
        candidates = [i for i in range(1, amount) if holding[i] < largest] or [i for i in range(1, amount) if holding[i] < bound]
        mass, remaining = sum([weights[i] for i in candidates]), spare
        for i in candidates:
            addition = min(bound - holding[i], max(1, remaining * weights[i] // mass), spare)
            holding[i] = holding[i] + addition
            spare = spare - addition
    return np.array(holding)


def scatter_about(rng, dims, scale, limit, pieces=(), kind=jnp.bfloat16):
    gain = block_levels(rng, dims, pieces, -0.22, 0.18) if pieces else 1.0
    entries = jax.random.normal(rng, dims, jnp.float32) * scale * gain
    return jnp.minimum(jnp.maximum(entries, -limit), limit).astype(kind)


def setup_inputs(seed: int = 0) -> dict:
    key_list = jax.random.split(jax.random.key(seed), 14)
    queries = draw_queries(jax.random.fold_in(key_list[13], 71), 0)
    new_keys = scatter_about(key_list[1], (STEPS, ROWS, KV * HD), 1.0, 6.0, ((1, 32), (2, 4)))
    new_values = scatter_about(key_list[2], (STEPS, ROWS, KV * HD), 1.0, 6.0, ((1, 32), (2, 4)))
    key_cache = scatter_about(key_list[3], (ROWS, KV, CACHE, HD), 1.0, 6.0, ((0, 32), (1, 4)))
    value_cache = scatter_about(key_list[4], (ROWS, KV, CACHE, HD), 1.0, 6.0, ((0, 32), (1, 4)))
    lengths = draw_lengths(jax.random.fold_in(key_list[13], 71), 0)
    residual_in = draw_residual_in(jax.random.fold_in(key_list[13], 71), 0)
    out_weight = scatter_about(key_list[7], (HEADS * HD, D), (HEADS * HD) ** -0.5, 0.0625, ((0, 4), (1, 16)))
    norm_gain = jnp.clip(1.0 + 0.1 * jax.random.normal(key_list[8], (D,), jnp.float32), 0.5, 1.5)
    top_weight = draw_top_weight(jax.random.fold_in(key_list[13], 71), 0)
    leaf_weight = draw_leaf_weight(jax.random.fold_in(key_list[13], 71), 0)
    cluster_ids_keys = jax.random.split(jax.random.fold_in(key_list[11], 1), STEPS * ROWS // RGROUP)
    cluster_ids_turns = jax.random.permutation(jax.random.fold_in(key_list[11], 3), STEPS * ROWS // RGROUP)
    cluster_ids = jax.vmap(lambda own, number: deal_out(jax.random.fold_in(key_list[11], 2), own, number, RGROUP, CLUSTERS, 1, MOST, 2))(cluster_ids_keys, cluster_ids_turns).reshape((STEPS, ROWS, 1))
    targets = set_ends(jax.random.randint(key_list[12], (STEPS, ROWS), 0, LEAF), jax.random.fold_in(key_list[12], 1), 0, LEAF - 1).astype(jnp.int32)
    return {"queries": queries, "new_keys": new_keys, "new_values": new_values, "key_cache": key_cache, "value_cache": value_cache, "lengths": lengths, "residual_in": residual_in, "out_weight": out_weight, "norm_gain": norm_gain, "top_weight": top_weight, "leaf_weight": leaf_weight, "cluster_ids": cluster_ids, "targets": targets}


def attend_row(packed, step_count):
    query, keys, values, fresh_keys, fresh_values, length = packed
    group = HEADS // KV
    scale = HD ** (-0.5)
    qf = query.reshape(KV, group, HD).astype(jnp.float32)
    kf = keys.astype(jnp.float32)
    vf = values.astype(jnp.float32)
    nkf = fresh_keys.reshape(step_count, KV, HD).astype(jnp.float32)
    nvf = fresh_values.reshape(step_count, KV, HD).astype(jnp.float32)
    cached = jnp.einsum('kgd,kpd->kgp', qf, kf) * scale
    valid = jnp.arange(CACHE) < length
    cached = jnp.where(valid[None, None, :], cached, -jnp.inf)
    recent = jnp.einsum('kgd,skd->kgs', qf, nkf) * scale
    peak = jnp.maximum(lax.optimization_barrier(jnp.max(cached, axis=-1)), lax.optimization_barrier(jnp.max(recent, axis=-1)))
    e_cached = jnp.exp(cached - peak[..., None])
    e_recent = jnp.exp(recent - peak[..., None])
    total = lax.optimization_barrier(jnp.sum(e_cached, axis=-1)) + lax.optimization_barrier(jnp.sum(e_recent, axis=-1))
    w_cached = (e_cached / total[..., None]).astype(jnp.bfloat16)
    w_recent = (e_recent / total[..., None]).astype(jnp.bfloat16)
    output = jnp.einsum('kgp,kpd->kgd', w_cached.astype(jnp.float32), vf)
    output = output + jnp.einsum('kgs,skd->kgd', w_recent.astype(jnp.float32), nvf)
    return output.astype(jnp.bfloat16).reshape(HEADS * HD)

def leaf_row(packed, leaf_weight):
    normed_row, cluster, target = packed
    weights = lax.dynamic_index_in_dim(leaf_weight, cluster, 0, keepdims=False)
    logits = jnp.dot(normed_row[None, :], weights, preferred_element_type=jnp.float32)[0]
    chosen = lax.dynamic_index_in_dim(logits, target, 0, keepdims=False)
    return chosen - jax.nn.logsumexp(logits)

def reference(queries, new_keys, new_values, key_cache, value_cache, lengths, residual_in, out_weight, norm_gain, top_weight, leaf_weight, cluster_ids, targets):
    results = []
    for step in range(STEPS):
        fresh_keys = jnp.moveaxis(new_keys[:step + 1], 1, 0)
        fresh_values = jnp.moveaxis(new_values[:step + 1], 1, 0)
        attended = lax.map(partial(attend_row, step_count=step + 1), (queries[step], key_cache, value_cache, fresh_keys, fresh_values, lengths))
        mixed = jnp.dot(attended, out_weight, preferred_element_type=jnp.float32)
        hidden = mixed + residual_in[step].astype(jnp.float32)
        inv_rms = lax.rsqrt(lax.optimization_barrier(jnp.sum(hidden * hidden, axis=1)) / D + 1e-05)
        gated = (hidden * norm_gain).astype(jnp.bfloat16)
        top_logits = jnp.dot(gated, top_weight, preferred_element_type=jnp.float32) * inv_rms[:, None]
        top_logprob = jax.nn.log_softmax(top_logits, axis=-1)
        ids = cluster_ids[step, :, 0]
        top_pick = jnp.take_along_axis(top_logprob, ids[:, None], axis=1)[:, 0]
        normed = (hidden * norm_gain * inv_rms[:, None]).astype(jnp.bfloat16)
        leaf_part = lax.map(partial(leaf_row, leaf_weight=leaf_weight), (normed, ids, targets[step]))
        results.append(top_pick + leaf_part)
    return jnp.stack(results, axis=0)
```

```python
import functools
import jax
import jax.numpy as jnp
from jax import lax
from jax.experimental import pallas as pl
from jax.experimental.pallas import tpu as pltpu
from jax.sharding import PartitionSpec as P


D = 8192
CLUSTERS = 80
STEPS = 4
LOCAL = 5
LEAF_COLS = 128
SIDE = 4
OFFS = (0, 1, 3, 2)
SMALL = 48
FULL = 64
F32 = jnp.float32
BF16 = jnp.bfloat16
VMEM = pl.BlockSpec(memory_space=pltpu.VMEM)
SMEM = pl.BlockSpec(memory_space=pltpu.SMEM)


def dot_nt(a, b):
    return lax.dot_general(a, b, (((1,), (1,)), ((), ())), preferred_element_type=F32)


def dot_nn(a, b):
    return lax.dot_general(a, b, (((1,), (0,)), ((), ())), preferred_element_type=F32)


def attend_kernel(len_ref, q_ref, nk_ref, nv_ref, k_ref, v_ref, oa_ref, ob_ref, q_scr, o_scr, q2_scr, o2_scr):
    step = pl.program_id(0)
    heads = 16
    scale = 128 ** (-0.5)

    @pl.when(step == 0)
    def _():
        for head in range(heads):
            part = q_ref[:, :, head * 128:(head + 1) * 128]
            q_scr[head] = part.reshape(64, 128).astype(F32)

    row0 = step * 4
    m_col = lax.broadcasted_iota(jnp.int32, (128, 64), 0)
    n_row = lax.broadcasted_iota(jnp.int32, (128, 64), 1)
    recent_ok = ((n_row & 15) == row0 + (m_col >> 5)) & ((n_row >> 4) <= (m_col & 3))
    lane = lax.broadcasted_iota(jnp.int32, (32, 256), 1)
    for kv in range(2):
        for rr in range(4):
            for g in range(8):
                q2_scr[rr * 32 + g * 4:rr * 32 + g * 4 + 4, :] = q_scr[kv * 8 + g, pl.ds(row0 + rr, 4, stride=16), :]
        q2 = q2_scr[...].astype(BF16)
        cached = []
        for rr in range(4):
            s = dot_nt(q2[rr * 32:(rr + 1) * 32], k_ref[rr, kv]) * scale
            cached.append(jnp.where(lane < len_ref[row0 + rr], s, -jnp.inf))
        cached = jnp.concatenate(cached, axis=0)
        nk = nk_ref[:, :, kv * 128:(kv + 1) * 128].reshape(64, 128)
        nv = nv_ref[:, :, kv * 128:(kv + 1) * 128].reshape(64, 128)
        recent = jnp.where(recent_ok, dot_nt(q2, nk) * scale, -jnp.inf)
        peak = jnp.maximum(jnp.max(cached, axis=1, keepdims=True), jnp.max(recent, axis=1, keepdims=True))
        ec = jnp.exp(cached - peak)
        er = jnp.exp(recent - peak)
        inv = 1.0 / (jnp.sum(ec, axis=1, keepdims=True) + jnp.sum(er, axis=1, keepdims=True))
        wc = (ec * inv).astype(BF16)
        wr = (er * inv).astype(BF16)
        out = []
        for rr in range(4):
            out.append(dot_nn(wc[rr * 32:(rr + 1) * 32], v_ref[rr, kv]))
        o2_scr[...] = jnp.concatenate(out, axis=0) + dot_nn(wr, nv)
        for rr in range(4):
            for g in range(8):
                o_scr[kv * 8 + g, pl.ds(row0 + rr, 4, stride=16), :] = o2_scr[rr * 32 + g * 4:rr * 32 + g * 4 + 4, :]

    @pl.when(step == pl.num_programs(0) - 1)
    def _():
        for head in range(heads):
            cols = slice(head * 128, (head + 1) * 128)
            oa_ref[:, :, cols] = o_scr[head, 0:32].reshape(2, 16, 128).astype(BF16)
            ob_ref[:, :, cols] = o_scr[head, 32:64].reshape(2, 16, 128).astype(BF16)


def attend(lengths, q, nk, nv, k, v):
    whole = lambda shape: pl.BlockSpec(shape, lambda i, *_: (0,) * len(shape))
    block = pl.BlockSpec((4, 2, 256, 128), lambda i, *_: (i, 0, 0, 0))
    out = jax.ShapeDtypeStruct((2, 16, 2048), BF16)
    return pl.pallas_call(
        attend_kernel,
        out_shape=(out, out),
        grid_spec=pltpu.PrefetchScalarGridSpec(
            num_scalar_prefetch=1,
            grid=(4,),
            in_specs=[whole((4, 16, 2048)), whole((4, 16, 256)), whole((4, 16, 256)), block, block],
            out_specs=(whole((2, 16, 2048)), whole((2, 16, 2048))),
            scratch_shapes=[
                pltpu.VMEM((16, 64, 128), F32),
                pltpu.VMEM((16, 64, 128), F32),
                pltpu.VMEM((128, 128), F32),
                pltpu.VMEM((128, 128), F32),
            ],
        ),
        cost_estimate=pl.CostEstimate(flops=300_000_000, bytes_accessed=5_000_000, transcendentals=400_000),
        name="attend",
    )(lengths, q, nk, nv, k, v)


def project_kernel(*refs):
    pieces = (refs[0:5], refs[5:10])
    w_ref, out_ref, lhs_scr = refs[10:]
    for s in range(4):
        own = pieces[s // 2]
        for i in range(4):
            for j in range(4):
                if i < 3:
                    rows = own[i][j, s % 2]
                else:
                    rows = own[3 + j // 2][j % 2, s % 2]
                k = i * 4 + j
                lhs_scr[s, k * 16:(k + 1) * 16, :] = rows
    for s in range(4):
        for n in range(2):
            cols = slice(n * 256, (n + 1) * 256)
            out_ref[s, :, cols] = dot_nn(lhs_scr[s], w_ref[:, cols]).astype(BF16)


def project(pieces_a, pieces_b, w):
    return pl.pallas_call(
        project_kernel,
        out_shape=jax.ShapeDtypeStruct((4, 256, 512), BF16),
        in_specs=[VMEM] * 11,
        out_specs=VMEM,
        scratch_shapes=[pltpu.VMEM((4, 256, 2048), BF16)],
        cost_estimate=pl.CostEstimate(flops=2_200_000_000, bytes_accessed=7_000_000, transcendentals=0),
        name="project",
    )(*pieces_a, *pieces_b, w)


def post_kernel(cap, place_ref, part_ref, res_ref, gain_ref, topw_ref, gp_ref, out_ref, top_ref):
    res = jnp.concatenate([res_ref[0, place_ref[k + 1]] for k in range(16)], axis=0).astype(F32)
    mixed = (part_ref[0].astype(F32) + part_ref[1].astype(F32)) + (part_ref[2].astype(F32) + part_ref[3].astype(F32))
    hidden = mixed + res
    squares = jnp.sum(hidden * hidden, axis=1, keepdims=True)
    gated = (hidden * gain_ref[...]).astype(BF16)
    top = dot_nn(gated, topw_ref[...])
    lane = lax.broadcasted_iota(jnp.int32, (256, 128), 1)
    wide = jnp.broadcast_to(squares, (256, 128))
    top = jnp.where(lane == CLUSTERS, wide, top)
    for k in range(16):
        top_ref[place_ref[k + 1]] = top[k * 16:(k + 1) * 16]
    dest = gp_ref[0:1, :]
    rank = gp_ref[1:2, :]
    rows = lax.broadcasted_iota(jnp.int32, (16, 256), 0)
    sq_row = wide.T[0:16]
    spread = jnp.where(rows == dest, sq_row, 0.0)
    hi = spread.astype(BF16)
    rest = spread - hi.astype(F32)
    mid = rest.astype(BF16)
    low = (rest - mid.astype(F32)).astype(BF16)
    by_rank = (lax.broadcasted_iota(jnp.int32, (128, 256), 0) == rank).astype(F32).astype(BF16)
    code = jnp.concatenate([dot_nt(hi, by_rank), dot_nt(mid, by_rank), dot_nt(low, by_rank), jnp.zeros((16, 128), F32)], axis=1).astype(BF16)
    slot = dest * cap + rank
    pick = (lax.broadcasted_iota(jnp.int32, (16 * cap, 256), 0) == slot).astype(F32).astype(BF16)
    srow = lax.broadcasted_iota(jnp.int32, (16 * cap, 16), 0)
    scol = lax.broadcasted_iota(jnp.int32, (16 * cap, 16), 1)
    last = (srow == scol * cap + cap - 1).astype(F32).astype(BF16)
    out_ref[...] = (dot_nn(pick, gated) + dot_nn(last, code)).astype(BF16)


def post(cap, place, parts, residual, gain, topw, gp):
    return pl.pallas_call(
        functools.partial(post_kernel, cap),
        out_shape=(jax.ShapeDtypeStruct((16 * cap, 512), BF16), jax.ShapeDtypeStruct((16, 16, 128), F32)),
        grid_spec=pltpu.PrefetchScalarGridSpec(
            num_scalar_prefetch=1,
            grid=(1,),
            in_specs=[
                pl.BlockSpec((4, 256, 512), lambda i, p: (0, 0, 0)),
                pl.BlockSpec((1, 16, 16, 512), lambda i, p: (p[0], 0, 0, 0)),
                pl.BlockSpec((1, 512), lambda i, p: (0, 0)),
                pl.BlockSpec((512, 128), lambda i, p: (0, 0)),
                pl.BlockSpec((2, 256), lambda i, p: (0, 0)),
            ],
            out_specs=(
                pl.BlockSpec((16 * cap, 512), lambda i, p: (0, 0)),
                pl.BlockSpec((16, 16, 128), lambda i, p: (0, 0, 0)),
            ),
        ),
        cost_estimate=pl.CostEstimate(flops=300_000_000, bytes_accessed=3_000_000, transcendentals=0),
        name="post",
    )(place, parts, residual, gain, topw, gp)


def leaf_kernel(cap, n_whole, n_split, place_ref, *refs):
    n = n_whole + n_split
    whole = refs[:n_whole]
    split = refs[n_whole:n_whole + 2 * n_split]
    code_ref, w_ref, out_ref, acc, sq_acc = refs[n_whole + 2 * n_split:]
    c = pl.program_id(0)

    @pl.when(c == 0)
    def _():
        acc[...] = jnp.zeros_like(acc)
        sq_acc[...] = jnp.zeros_like(sq_acc)

    pieces = [r[0] for r in whole]
    for k in range(n_split):
        pieces.append(jnp.where(c < 8, split[2 * k][0], split[2 * k + 1][0]))
    for k in range(n):
        tail = pieces[k][cap - 16:cap].astype(F32)[15:16]
        sq_acc[k:k + 1] += tail[:, 0:128] + tail[:, 128:256] + tail[:, 256:384]
    lhs = jnp.concatenate(pieces, axis=0)
    for first, width in ((0, 2), (2, 2), (4, 1)):
        rhs = [w_ref[first + k] for k in range(width)]
        rhs = rhs[0] if width == 1 else jnp.concatenate(rhs, axis=1)
        acc[:, first * 128:(first + width) * 128] += dot_nn(lhs, rhs)

    @pl.when(c == pl.num_programs(0) - 1)
    def _():
        out_ref[...] = jnp.zeros_like(out_ref)
        start = place_ref[8]
        r_i = lax.broadcasted_iota(jnp.int32, (cap, 128), 0)
        c_i = lax.broadcasted_iota(jnp.int32, (cap, 128), 1)
        diag = r_i == c_i
        for k in range(n):
            b = place_ref[k]
            code = code_ref[pl.ds(pl.multiple_of(b * cap, 16), cap), :]
            local = code >> 10
            target = (code & 1023) - start
            sq = jnp.sum(jnp.where(diag, jnp.broadcast_to(sq_acc[k:k + 1], (cap, 128)), 0.0), axis=1, keepdims=True)
            logits = jnp.zeros((cap, 128), F32)
            for j in range(LOCAL):
                logits = jnp.where(local == j, acc[k * cap:(k + 1) * cap, j * 128:(j + 1) * 128], logits)
            logits = logits * lax.rsqrt(sq / D + 1e-05)
            peak = jnp.max(logits, axis=1, keepdims=True)
            lse = peak + jnp.log(jnp.sum(jnp.exp(logits - peak), axis=1, keepdims=True))
            hit = jnp.sum(jnp.where(c_i == target, logits, 0.0), axis=1, keepdims=True)
            out_ref[pl.ds(b, 1), :] = jnp.sum(jnp.where(diag, lse, 0.0), axis=0, keepdims=True)
            out_ref[pl.ds(b + 8, 1), :] = jnp.sum(jnp.where(diag, hit, 0.0), axis=0, keepdims=True)


def leaf(cap, place, whole, split, code, w):
    n = len(whole) + len(split) // 2
    piece = pl.BlockSpec((1, cap, 512), lambda c, p: (c, 0, 0))
    first = pl.BlockSpec((1, cap, 512), lambda c, p: (jnp.minimum(c, 7), 0, 0))
    second = pl.BlockSpec((1, cap, 512), lambda c, p: (jnp.maximum(c - 8, 0), 0, 0))
    return pl.pallas_call(
        functools.partial(leaf_kernel, cap, len(whole), len(split) // 2),
        out_shape=jax.ShapeDtypeStruct((16, 128), F32),
        grid_spec=pltpu.PrefetchScalarGridSpec(
            num_scalar_prefetch=1,
            grid=(16,),
            in_specs=[piece] * len(whole) + [first, second] * (len(split) // 2) + [
                pl.BlockSpec((8 * cap, 1), lambda c, p: (0, 0)),
                pl.BlockSpec((LOCAL, 512, 128), lambda c, p: (0, c, 0)),
            ],
            out_specs=pl.BlockSpec((16, 128), lambda c, p: (0, 0)),
            scratch_shapes=[pltpu.VMEM((n * cap, LOCAL * 128), F32), pltpu.VMEM((8, 128), F32)],
        ),
        cost_estimate=pl.CostEstimate(flops=2 * n * cap * 8192 * 640, bytes_accessed=11_000_000, transcendentals=0),
        name="leaf",
    )(place, *whole, *split, code, w)


def from_z(x, d):
    return lax.ppermute(x, "cluster", [(c // 4 * 4 + (c + d) % 4, c) for c in range(16)])


def from_y(x, d):
    return lax.ppermute(x, "cluster", [((c // 4 + d) % 4 * 4 + c % 4, c) for c in range(16)])


def from_x(x, d):
    return lax.ppermute(x, "head", [((h + d) % 4, h) for h in range(4)])


def swap(x):
    return lax.ppermute(x, "rows", [(0, 1), (1, 0)])


def merge(a, b):
    peak = jnp.maximum(a, b)
    return peak + jnp.log(jnp.exp(a - peak) + jnp.exp(b - peak))


def tail(cap, parts, residual, gain, topw, place, gp, ids8, tg8, g8, p8, own_ids, leaf_weight):
    my_cluster = lax.axis_index("cluster")
    my_row = lax.axis_index("rows")
    my_head = lax.axis_index("head")
    land = (g8 == my_cluster)[:, None, :] & (p8[:, None, :] == jnp.arange(cap)[None, :, None])
    value = ids8 % LOCAL * 1024 + tg8
    code = jnp.sum(jnp.where(land, value[:, None, :], 0), axis=2).reshape(8 * cap, 1)
    outgoing, top = post(cap, place, parts, residual, gain, topw, gp)
    own = lax.all_to_all(outgoing.reshape(16, cap, 512), "cluster", 0, 0, tiled=True)
    plus, minus = from_x(own, 1), from_x(own, 3)
    own_p = swap(own)
    far_a, far_b = from_x(plus[:8], 1), from_x(minus[8:], 3)
    top = lax.all_to_all(top, "cluster", 0, 0, tiled=True)
    plus_p, minus_p = swap(plus), swap(minus)
    far_ap, far_bp = swap(far_a), swap(far_b)
    block = lambda flip, d: (my_row ^ flip) * 4 + (my_head + d) % 4
    start = (my_row * 4 + my_head) * LEAF_COLS
    near_place = jnp.stack([block(0, 0), block(0, 1), block(0, 3), block(1, 0), block(1, 1), block(1, 3), start, start, start])
    far_place = jnp.stack([block(0, 2), block(1, 2)] + [start] * 7)
    near = leaf(cap, near_place, [own, plus, minus, own_p, plus_p, minus_p], [], code, leaf_weight)
    far = leaf(cap, far_place, [], [far_a, far_b, far_ap, far_bp], code, leaf_weight)
    state = near + far

    tsum = jnp.sum(top, axis=0)
    inv = lax.rsqrt(tsum[:, CLUSTERS:CLUSTERS + 1] / D + 1e-05)
    logprob = jax.nn.log_softmax(tsum[:, :CLUSTERS] * inv, axis=-1)
    top_pick = jnp.sum(jnp.where(jnp.arange(CLUSTERS)[None, :] == own_ids[:, None], logprob, 0.0), axis=1)
    return state, top_pick


def shards(queries, new_keys, new_values, key_cache, value_cache, lengths, residual_in, out_weight, norm_gain, top_weight, leaf_weight, cluster_ids, targets):
    my_cluster = lax.axis_index("cluster")
    my_row = lax.axis_index("rows")
    my_head = lax.axis_index("head")
    my_y, my_z = my_cluster // SIDE, my_cluster % SIDE

    ids8 = cluster_ids[:, :, 0].reshape(STEPS, 2, 256).transpose(1, 0, 2).reshape(8, 256)
    tg8 = targets.reshape(STEPS, 2, 256).transpose(1, 0, 2).reshape(8, 256)
    g8 = ids8 // LOCAL
    index = jnp.arange(256)
    earlier = (g8[:, :, None] == g8[:, None, :]) & (index[None, None, :] < index[None, :, None])
    p8 = jnp.sum(earlier.astype(jnp.int32), axis=2)
    own_block = my_row * 4 + my_head
    offs = jnp.array(OFFS, jnp.int32)
    k = jnp.arange(16)
    major, minor = offs[k // 4], offs[k % 4]
    first = my_head < 2
    yy = (my_y + jnp.where(first, major, minor)) % 4
    zz = (my_z + jnp.where(first, minor, major)) % 4
    cabs = (yy * 4 + zz).astype(jnp.int32)
    place = jnp.concatenate([my_head[None].astype(jnp.int32), cabs])
    own_g = lax.dynamic_index_in_dim(g8, own_block, 0, False).reshape(16, 16)
    own_p = lax.dynamic_index_in_dim(p8, own_block, 0, False).reshape(16, 16)
    gp = jnp.stack([own_g[cabs].reshape(256), own_p[cabs].reshape(256)])
    own_ids = lax.dynamic_slice(ids8, (own_block, my_cluster * 16), (1, 16))[0]

    att_a, att_b = attend(lengths, queries, new_keys, new_values, key_cache, value_cache)
    za = [att_a] + [from_z(att_a, d) for d in OFFS[1:]]
    yb = [att_b] + [from_y(att_b, d) for d in OFFS[1:]]
    za, yb = jnp.stack(za), jnp.stack(yb)
    a1, a3, b1, b3 = from_y(za, 1), from_y(za, 3), from_z(yb, 1), from_z(yb, 3)
    a2a, a2b = from_y(a1[:2], 1), from_y(a3[2:], 3)
    b2a, b2b = from_z(b1[:2], 1), from_z(b3[2:], 3)
    partial_sums = project((za, a1, a3, a2a, a2b), (yb, b1, b3, b2a, b2b), out_weight)
    parts = lax.all_to_all(partial_sums, "head", 0, 0, tiled=True)

    topw = jnp.pad(top_weight, ((0, 0), (0, 128 - CLUSTERS)))
    args = (parts, residual_in.reshape(4, 16, 16, 512), norm_gain[None, :], topw, place, gp, ids8, tg8, g8, p8, own_ids, leaf_weight)
    state, top_pick = lax.cond(jnp.max(p8) < SMALL - 1, functools.partial(tail, SMALL), functools.partial(tail, FULL), *args)

    other = swap(state)
    state = jnp.concatenate([merge(state[:8], other[:8]), state[8:] + other[8:], jnp.pad(top_pick[None, :], ((0, 7), (0, 112)))], axis=0)
    heard = [state] + [from_x(state, d) for d in OFFS[1:]]
    lse = merge(merge(heard[0][:8], heard[1][:8]), merge(heard[2][:8], heard[3][:8]))
    picked = (heard[0][8:16] + heard[1][8:16]) + (heard[2][8:16] + heard[3][8:16])
    leaf_lp = picked - lse
    back = lax.all_to_all(jnp.broadcast_to(leaf_lp[None], (16, 8, 128)), "cluster", 0, 0, tiled=True)
    back = lax.dynamic_slice(back, (0, my_row * 4, 0), (16, 4, 128))
    g_rows = lax.dynamic_slice(g8, (my_row * 4, my_cluster * 16), (4, 16))
    p_rows = lax.dynamic_slice(p8, (my_row * 4, my_cluster * 16), (4, 16))
    hit = (g_rows[:, :, None, None] == jnp.arange(16)[None, None, :, None]) & (p_rows[:, :, None, None] == jnp.arange(128)[None, None, None, :])
    leaf_part = jnp.sum(jnp.where(hit, back.transpose(1, 0, 2)[:, None], 0.0), axis=(2, 3))
    tops = jnp.stack([s[16, :16] for s in heard])
    order = (jnp.arange(4)[:, None] - my_head) % 4 == offs[None, :]
    top_part = jnp.sum(jnp.where(order[:, :, None], tops[None], 0.0), axis=1)
    return leaf_part + top_part


def solution(mesh):
    placed = (
        P(None, ("rows", "cluster"), "head"),
        P(None, ("rows", "cluster"), "head"),
        P(None, ("rows", "cluster"), "head"),
        P(("rows", "cluster"), "head", None, None),
        P(("rows", "cluster"), "head", None, None),
        P(("rows", "cluster")),
        P(None, "rows", "cluster"),
        P("head", "cluster"),
        P("cluster"),
        P("cluster", None),
        P("cluster", None, ("rows", "head")),
        P(),
        P(),
    )
    return jax.shard_map(
        shards, mesh=mesh, in_specs=placed, out_specs=P(None, ("rows", "cluster")), check_vma=False
    )
```

```python
import functools
import jax
import jax.numpy as jnp
from jax import lax
from jax.experimental import pallas as pl
from jax.experimental.pallas import tpu as pltpu
from jax.sharding import PartitionSpec as P


D = 8192
CLUSTERS = 80
STEPS = 4
LOCAL = 5
LEAF_COLS = 128
SIDE = 4
OFFS = (0, 1, 3, 2)
SMALL = 40
FULL = 64
F32 = jnp.float32
BF16 = jnp.bfloat16
VMEM = pl.BlockSpec(memory_space=pltpu.VMEM)
SMEM = pl.BlockSpec(memory_space=pltpu.SMEM)


def dot_nt(a, b):
    return lax.dot_general(a, b, (((1,), (1,)), ((), ())), preferred_element_type=F32)


def dot_nn(a, b):
    return lax.dot_general(a, b, (((1,), (0,)), ((), ())), preferred_element_type=F32)


def attend_kernel(len_ref, q_ref, nk_ref, nv_ref, k_ref, v_ref, oa_ref, ob_ref, q_scr, o_scr, q2_scr, o2_scr):
    step = pl.program_id(0)
    heads = 16
    scale = 128 ** (-0.5)

    @pl.when(step == 0)
    def _():
        for head in range(heads):
            part = q_ref[:, :, head * 128:(head + 1) * 128]
            q_scr[head] = part.reshape(64, 128).astype(F32)

    row0 = step * 4
    m_col = lax.broadcasted_iota(jnp.int32, (128, 64), 0)
    n_row = lax.broadcasted_iota(jnp.int32, (128, 64), 1)
    recent_ok = ((n_row & 15) == row0 + (m_col >> 5)) & ((n_row >> 4) <= (m_col & 3))
    lane = lax.broadcasted_iota(jnp.int32, (32, 256), 1)
    for kv in range(2):
        for rr in range(4):
            for g in range(8):
                q2_scr[rr * 32 + g * 4:rr * 32 + g * 4 + 4, :] = q_scr[kv * 8 + g, pl.ds(row0 + rr, 4, stride=16), :]
        q2 = q2_scr[...].astype(BF16)
        cached = []
        for rr in range(4):
            s = dot_nt(q2[rr * 32:(rr + 1) * 32], k_ref[rr, kv]) * scale
            cached.append(jnp.where(lane < len_ref[row0 + rr], s, -jnp.inf))
        cached = jnp.concatenate(cached, axis=0)
        nk = nk_ref[:, :, kv * 128:(kv + 1) * 128].reshape(64, 128)
        nv = nv_ref[:, :, kv * 128:(kv + 1) * 128].reshape(64, 128)
        recent = jnp.where(recent_ok, dot_nt(q2, nk) * scale, -jnp.inf)
        peak = jnp.maximum(jnp.max(cached, axis=1, keepdims=True), jnp.max(recent, axis=1, keepdims=True))
        ec = jnp.exp(cached - peak)
        er = jnp.exp(recent - peak)
        inv = 1.0 / (jnp.sum(ec, axis=1, keepdims=True) + jnp.sum(er, axis=1, keepdims=True))
        wc = (ec * inv).astype(BF16)
        wr = (er * inv).astype(BF16)
        out = []
        for rr in range(4):
            out.append(dot_nn(wc[rr * 32:(rr + 1) * 32], v_ref[rr, kv]))
        o2_scr[...] = jnp.concatenate(out, axis=0) + dot_nn(wr, nv)
        for rr in range(4):
            for g in range(8):
                o_scr[kv * 8 + g, pl.ds(row0 + rr, 4, stride=16), :] = o2_scr[rr * 32 + g * 4:rr * 32 + g * 4 + 4, :]

    @pl.when(step == pl.num_programs(0) - 1)
    def _():
        for head in range(heads):
            cols = slice(head * 128, (head + 1) * 128)
            oa_ref[:, :, cols] = o_scr[head, 0:32].reshape(2, 16, 128).astype(BF16)
            ob_ref[:, :, cols] = o_scr[head, 32:64].reshape(2, 16, 128).astype(BF16)


def attend(lengths, q, nk, nv, k, v):
    whole = lambda shape: pl.BlockSpec(shape, lambda i, *_: (0,) * len(shape))
    block = pl.BlockSpec((4, 2, 256, 128), lambda i, *_: (i, 0, 0, 0))
    out = jax.ShapeDtypeStruct((2, 16, 2048), BF16)
    return pl.pallas_call(
        attend_kernel,
        out_shape=(out, out),
        grid_spec=pltpu.PrefetchScalarGridSpec(
            num_scalar_prefetch=1,
            grid=(4,),
            in_specs=[whole((4, 16, 2048)), whole((4, 16, 256)), whole((4, 16, 256)), block, block],
            out_specs=(whole((2, 16, 2048)), whole((2, 16, 2048))),
            scratch_shapes=[
                pltpu.VMEM((16, 64, 128), F32),
                pltpu.VMEM((16, 64, 128), F32),
                pltpu.VMEM((128, 128), F32),
                pltpu.VMEM((128, 128), F32),
            ],
        ),
        cost_estimate=pl.CostEstimate(flops=300_000_000, bytes_accessed=5_000_000, transcendentals=400_000),
        name="attend",
    )(lengths, q, nk, nv, k, v)


def project_first_kernel(*refs):
    pieces = (refs[0:4], refs[4:8])
    w_ref, lhs_ref, out_ref = refs[8:]
    for s in range(4):
        own = pieces[s // 2]
        for i in range(4):
            for j in range(4):
                k = i * 4 + j
                lhs_ref[s, k * 16:(k + 1) * 16, :] = own[i][j, s % 2]
    for s in range(4):
        out_ref[s] = dot_nn(lhs_ref[s], w_ref[:, 0:256]).astype(BF16)


def project_second_kernel(lhs_ref, w_ref, out_ref):
    for s in range(4):
        out_ref[s] = dot_nn(lhs_ref[s], w_ref[:, 256:512]).astype(BF16)


PROJECT_COST = pl.CostEstimate(flops=1_100_000_000, bytes_accessed=5_000_000, transcendentals=0)


def project_first(pieces_a, pieces_b, w):
    return pl.pallas_call(
        project_first_kernel,
        out_shape=(jax.ShapeDtypeStruct((4, 256, 2048), BF16), jax.ShapeDtypeStruct((4, 256, 256), BF16)),
        in_specs=[VMEM] * 9,
        out_specs=(VMEM, VMEM),
        cost_estimate=PROJECT_COST,
        name="project_first",
    )(*pieces_a, *pieces_b, w)


def project_second(lhs, w):
    return pl.pallas_call(
        project_second_kernel,
        out_shape=jax.ShapeDtypeStruct((4, 256, 256), BF16),
        in_specs=[VMEM] * 2,
        out_specs=VMEM,
        cost_estimate=PROJECT_COST,
        name="project_second",
    )(lhs, w)


def post_kernel(cap, second, place_ref, part_ref, res_ref, gain_ref, topw_ref, gp_ref, *refs):
    if second:
        first_top_ref, out_ref, top_ref = refs
    else:
        out_ref, top_ref = refs
    res = jnp.concatenate([res_ref[0, place_ref[k + 1]] for k in range(16)], axis=0).astype(F32)
    mixed = (part_ref[0].astype(F32) + part_ref[1].astype(F32)) + (part_ref[2].astype(F32) + part_ref[3].astype(F32))
    hidden = mixed + res
    squares = jnp.sum(hidden * hidden, axis=1, keepdims=True)
    gated = (hidden * gain_ref[...]).astype(BF16)
    top = dot_nn(gated, topw_ref[...])
    lane = lax.broadcasted_iota(jnp.int32, (256, 128), 1)
    wide = jnp.broadcast_to(squares, (256, 128))
    top = jnp.where(lane == CLUSTERS, wide, top)
    if second:
        top = top + first_top_ref[...]
        for k in range(16):
            top_ref[place_ref[k + 1]] = top[k * 16:(k + 1) * 16]
    else:
        top_ref[...] = top
    dest = gp_ref[0:1, :]
    rank = gp_ref[1:2, :]
    rows = lax.broadcasted_iota(jnp.int32, (16, 256), 0)
    sq_row = wide.T[0:16]
    spread = jnp.where(rows == dest, sq_row, 0.0)
    hi = spread.astype(BF16)
    low = (spread - hi.astype(F32)).astype(BF16)
    by_rank = (lax.broadcasted_iota(jnp.int32, (128, 256), 0) == rank).astype(F32).astype(BF16)
    code = jnp.concatenate([dot_nt(hi, by_rank), dot_nt(low, by_rank)], axis=1).astype(BF16)
    slot = dest * cap + rank
    pick = (lax.broadcasted_iota(jnp.int32, (16 * cap, 256), 0) == slot).astype(F32).astype(BF16)
    srow = lax.broadcasted_iota(jnp.int32, (16 * cap, 16), 0)
    scol = lax.broadcasted_iota(jnp.int32, (16 * cap, 16), 1)
    last = (srow == scol * cap + cap - 1).astype(F32).astype(BF16)
    out_ref[...] = (dot_nn(pick, gated) + dot_nn(last, code)).astype(BF16)


def post(cap, half, place, parts, residual, gain, topw, gp, first_top=()):
    top = (jax.ShapeDtypeStruct((16, 16, 128), F32), pl.BlockSpec((16, 16, 128), lambda i, p: (0, 0, 0)))
    if half == 0:
        top = (jax.ShapeDtypeStruct((256, 128), F32), pl.BlockSpec((256, 128), lambda i, p: (0, 0)))
    return pl.pallas_call(
        functools.partial(post_kernel, cap, half == 1),
        out_shape=(jax.ShapeDtypeStruct((16 * cap, 256), BF16), top[0]),
        grid_spec=pltpu.PrefetchScalarGridSpec(
            num_scalar_prefetch=1,
            grid=(1,),
            in_specs=[
                pl.BlockSpec((4, 256, 256), lambda i, p: (0, 0, 0)),
                pl.BlockSpec((1, 16, 16, 256), lambda i, p: (p[0], 0, 0, half)),
                pl.BlockSpec((1, 256), lambda i, p: (0, half)),
                pl.BlockSpec((256, 128), lambda i, p: (half, 0)),
                pl.BlockSpec((2, 256), lambda i, p: (0, 0)),
            ] + [pl.BlockSpec((256, 128), lambda i, p: (0, 0))] * len(first_top),
            out_specs=(pl.BlockSpec((16 * cap, 256), lambda i, p: (0, 0)), top[1]),
        ),
        cost_estimate=pl.CostEstimate(flops=150_000_000, bytes_accessed=1_500_000, transcendentals=0),
        name="post",
    )(place, parts, residual, gain, topw, gp, *first_top)


def stack_rows(cap, blocks):
    if cap % 16 == 0:
        return jnp.concatenate(blocks, axis=0)
    return jnp.concatenate([b.astype(F32) for b in blocks], axis=0).astype(BF16)


def leaf_accumulate(cap, half, pieces, w_ref, acc, sq_acc):
    for c0 in range(0, 16, 4):
        lhs = []
        for c in range(c0, c0 + 4):
            blocks = [ref[c] for ref in pieces]
            for k, block in enumerate(blocks):
                spare = block[cap - 8:cap].astype(F32)[7:8]
                sq_acc[k:k + 1] += spare[:, 0:128] + spare[:, 128:256]
            lhs.append(stack_rows(cap, blocks))
        lhs = jnp.concatenate(lhs, axis=1)
        for first, width in ((0, 2), (2, 2), (4, 1)):
            rhs = []
            for c in range(c0, c0 + 4):
                at = c * 512 + half * 256
                part = [w_ref[first + k, at:at + 256, :] for k in range(width)]
                rhs.append(part[0] if width == 1 else jnp.concatenate(part, axis=1))
            acc[:, first * 128:(first + width) * 128] += dot_nn(lhs, jnp.concatenate(rhs, axis=0))


def leaf_finish(cap, n, place_ref, code_ref, acc, sq_acc, out_ref):
    start = place_ref[n]
    r_i = lax.broadcasted_iota(jnp.int32, (cap, 128), 0)
    c_i = lax.broadcasted_iota(jnp.int32, (cap, 128), 1)
    diag = r_i == c_i
    for k in range(n):
        b = place_ref[k]
        code = code_ref[b][:cap]
        local = code >> 10
        target = (code & 1023) - start
        sq = jnp.sum(jnp.where(diag, jnp.broadcast_to(sq_acc[k:k + 1], (cap, 128)), 0.0), axis=1, keepdims=True)
        logits = jnp.zeros((cap, 128), F32)
        for j in range(LOCAL):
            logits = jnp.where(local == j, acc[k * cap:(k + 1) * cap, j * 128:(j + 1) * 128], logits)
        logits = logits * lax.rsqrt(sq / D + 1e-05)
        peak = jnp.max(logits, axis=1, keepdims=True)
        lse = peak + jnp.log(jnp.sum(jnp.exp(logits - peak), axis=1, keepdims=True))
        hit = jnp.sum(jnp.where(c_i == target, logits, 0.0), axis=1, keepdims=True)
        out_ref[pl.ds(b, 1), :] = jnp.sum(jnp.where(diag, lse, 0.0), axis=0, keepdims=True)
        out_ref[pl.ds(b + 8, 1), :] = jnp.sum(jnp.where(diag, hit, 0.0), axis=0, keepdims=True)


def near_first_kernel(cap, *refs):
    pieces, (w_ref, acc, sq_acc) = refs[:6], refs[6:]
    acc[...] = jnp.zeros_like(acc)
    sq_acc[...] = jnp.zeros_like(sq_acc)
    leaf_accumulate(cap, 0, pieces, w_ref, acc, sq_acc)


def near_second_kernel(cap, place_ref, *refs):
    pieces, (w_ref, code_ref, acc_in, sq_in, out_ref, acc, sq_acc) = refs[:6], refs[6:]
    acc[...] = acc_in[...]
    sq_acc[...] = sq_in[...]
    leaf_accumulate(cap, 1, pieces, w_ref, acc, sq_acc)
    out_ref[...] = jnp.zeros_like(out_ref)
    leaf_finish(cap, 6, place_ref, code_ref, acc, sq_acc, out_ref)


def far_kernel(cap, place_ref, *refs):
    first, second, (w_ref, code_ref, near_ref, out_ref, acc, sq_acc) = refs[:2], refs[2:4], refs[4:]
    acc[...] = jnp.zeros_like(acc)
    sq_acc[...] = jnp.zeros_like(sq_acc)
    leaf_accumulate(cap, 0, first, w_ref, acc, sq_acc)
    leaf_accumulate(cap, 1, second, w_ref, acc, sq_acc)
    out_ref[...] = near_ref[...]
    leaf_finish(cap, 2, place_ref, code_ref, acc, sq_acc, out_ref)


def leaf_cost(rows, depth):
    return pl.CostEstimate(flops=2 * rows * depth * 640, bytes_accessed=640 * depth * 2, transcendentals=0)


def near_first(cap, pieces, w):
    return pl.pallas_call(
        functools.partial(near_first_kernel, cap),
        out_shape=(jax.ShapeDtypeStruct((6 * cap, 640), F32), jax.ShapeDtypeStruct((8, 128), F32)),
        in_specs=[VMEM] * 7,
        out_specs=(VMEM, VMEM),
        cost_estimate=leaf_cost(6 * cap, 4096),
        name="near_first",
    )(*pieces, w)


def near_second(cap, place, pieces, w, code, acc, sq):
    return pl.pallas_call(
        functools.partial(near_second_kernel, cap),
        out_shape=jax.ShapeDtypeStruct((16, 128), F32),
        in_specs=[SMEM] + [VMEM] * 10,
        out_specs=VMEM,
        scratch_shapes=[pltpu.VMEM((6 * cap, 640), F32), pltpu.VMEM((8, 128), F32)],
        cost_estimate=leaf_cost(6 * cap, 4096),
        name="near_second",
    )(place, *pieces, w, code, acc, sq)


def far_leaf(cap, place, pieces, w, code, near):
    return pl.pallas_call(
        functools.partial(far_kernel, cap),
        out_shape=jax.ShapeDtypeStruct((16, 128), F32),
        in_specs=[SMEM] + [VMEM] * 7,
        out_specs=VMEM,
        scratch_shapes=[pltpu.VMEM((2 * cap, 640), F32), pltpu.VMEM((8, 128), F32)],
        cost_estimate=leaf_cost(2 * cap, 8192),
        name="far_leaf",
    )(place, *pieces, w, code, near)


def merge(a, b):
    peak = jnp.maximum(a, b)
    return peak + jnp.log(jnp.exp(a - peak) + jnp.exp(b - peak))


def message_kernel(place_ref, state_ref, other_ref, top_ref, ids_ref, out_ref):
    lse = merge(state_ref[0:8], other_ref[0:8])
    picked = state_ref[8:16] + other_ref[8:16]
    low = place_ref[0] == 0
    lse = jnp.where(low, lse[0:4], lse[4:8])
    picked = jnp.where(low, picked[0:4], picked[4:8])
    total = top_ref[0]
    for k in range(1, 16):
        total = total + top_ref[k]
    lane = lax.broadcasted_iota(jnp.int32, (16, 128), 1)
    row = lax.broadcasted_iota(jnp.int32, (16, 128), 0)
    logits = total * lax.rsqrt(total[:, CLUSTERS:CLUSTERS + 1] / D + 1e-05)
    logits = jnp.where(lane < CLUSTERS, logits, -jnp.inf)
    peak = jnp.max(logits, axis=1, keepdims=True)
    norm = peak + jnp.log(jnp.sum(jnp.exp(logits - peak), axis=1, keepdims=True))
    own = jnp.sum(jnp.where(lane == ids_ref[...], logits, 0.0), axis=1, keepdims=True) - norm
    top_row = jnp.sum(jnp.where(lane == row + 64, own, 0.0), axis=0, keepdims=True)
    whole = jnp.concatenate([lse, picked], axis=0)
    whole = jnp.where(lane[0:8] < 64, whole, top_row)
    out_ref[...] = jnp.broadcast_to(whole[None], out_ref.shape)


def final_kernel(place_ref, back_ref, g_ref, p_ref, out_ref):
    blocks = [back_ref[h * 16:(h + 1) * 16] for h in range(4)]
    peak = jnp.maximum(jnp.maximum(blocks[0], blocks[1]), jnp.maximum(blocks[2], blocks[3]))
    mass = jnp.exp(blocks[0] - peak)
    picked = blocks[0]
    for h in range(1, 4):
        mass = mass + jnp.exp(blocks[h] - peak)
        picked = picked + blocks[h]
    lse = peak + jnp.log(mass)
    lane = lax.broadcasted_iota(jnp.int32, (16, 128), 1)
    row = lax.broadcasted_iota(jnp.int32, (16, 128), 0)
    for s in range(4):
        g = jnp.broadcast_to(g_ref[s * 16:(s + 1) * 16], (16, 128))
        at = lane == p_ref[s * 16:(s + 1) * 16]
        found = jnp.where(lane == row + 64, back_ref[s * 16 + place_ref[1], 0:1], 0.0)
        for c in range(16):
            value = picked[c, 4 + s:5 + s] - lse[c, s:s + 1]
            found = found + jnp.where(at & (g == c), value, 0.0)
        column = jnp.sum(found, axis=1, keepdims=True)
        out_ref[s:s + 1, :] = jnp.sum(jnp.where(lane == row, column, 0.0), axis=0, keepdims=True)[:, 0:16]


def message(place, state, other, top, ids):
    return pl.pallas_call(
        message_kernel,
        out_shape=jax.ShapeDtypeStruct((64, 8, 128), F32),
        in_specs=[SMEM] + [VMEM] * 4,
        out_specs=VMEM,
        name="message",
    )(place, state, other, top, ids)


def final(place, back, g, p):
    return pl.pallas_call(
        final_kernel,
        out_shape=jax.ShapeDtypeStruct((4, 16), F32),
        in_specs=[SMEM] + [VMEM] * 3,
        out_specs=VMEM,
        name="final",
    )(place, back, g, p)


def cluster_permute(x, source):
    pairs = []
    for c in range(16):
        y, z = source(c // 4, c % 4)
        pairs.append((y % 4 * 4 + z % 4, c))
    return lax.ppermute(x, "cluster", pairs)


def from_x(x, d):
    return lax.ppermute(x, "head", [((h + d) % 4, h) for h in range(4)])


def swap(x):
    return lax.ppermute(x, "rows", [(0, 1), (1, 0)])


def gather_z(x):
    x = jnp.stack([x, cluster_permute(x, lambda y, z: (y, z ^ 1))])
    other = cluster_permute(x, lambda y, z: (y, 3 - z))
    return jnp.concatenate([x, other])


def gather_y(x):
    x = jnp.stack([x, cluster_permute(x, lambda y, z: (y ^ 1, z))])
    other = cluster_permute(x, lambda y, z: (3 - y, z))
    return jnp.concatenate([x, other])


def tail(cap, parts0, parts1, residual, gain, topw, place, near_place, far_place, end_place, gp, code, own_ids, g_rows, p_rows, leaf_weight):
    def spread(outgoing):
        own = lax.all_to_all(outgoing.reshape(16, cap, 256), "cluster", 0, 0, tiled=True)
        plus, minus = from_x(own, 1), from_x(own, 3)
        return own, plus, minus

    out0, top0 = post(cap, 0, place, parts0, residual, gain, topw, gp)
    own0, plus0, minus0 = spread(out0)
    out1, top = post(cap, 1, place, parts1, residual, gain, topw, gp, (top0,))
    own1, plus1, minus1 = spread(out1)
    top = lax.all_to_all(top, "cluster", 0, 0, tiled=True)
    far0 = from_x(plus0, 1)
    far1 = from_x(minus1, 3)
    acc, sq = near_first(cap, (own0, plus0, minus0, swap(own0), swap(plus0), swap(minus0)), leaf_weight)
    near = near_second(cap, near_place, (own1, plus1, minus1, swap(own1), swap(plus1), swap(minus1)), leaf_weight, code, acc, sq)
    state = far_leaf(cap, far_place, (far0, swap(far0), far1, swap(far1)), leaf_weight, code, near)
    note = message(end_place, state, swap(state), top, own_ids)
    back = lax.all_to_all(note, ("head", "cluster"), 0, 0, tiled=True)
    return final(end_place, back, g_rows, p_rows)


def shards(queries, new_keys, new_values, key_cache, value_cache, lengths, residual_in, out_weight, norm_gain, top_weight, leaf_weight, cluster_ids, targets):
    my_cluster = lax.axis_index("cluster").astype(jnp.int32)
    my_row = lax.axis_index("rows").astype(jnp.int32)
    my_head = lax.axis_index("head").astype(jnp.int32)
    my_y, my_z = my_cluster // SIDE, my_cluster % SIDE

    ids8 = cluster_ids[:, :, 0].reshape(STEPS, 2, 256).transpose(1, 0, 2).reshape(8, 256)
    tg8 = targets.reshape(STEPS, 2, 256).transpose(1, 0, 2).reshape(8, 256)
    g8 = ids8 // LOCAL
    index = jnp.arange(256)
    earlier = (g8[:, :, None] == g8[:, None, :]) & (index[None, None, :] < index[None, :, None])
    p8 = jnp.sum(earlier.astype(jnp.int32), axis=2)
    own_block = my_row * 4 + my_head
    k = jnp.arange(16)
    first = my_head < 2

    def near_side(m, t):
        m = jnp.where(t >= 2, 3 - m, m)
        return m ^ (t & 1)

    def far_side(m, t):
        return (m + jnp.array(OFFS, jnp.int32)[t]) % 4

    yy = jnp.where(first, far_side(my_y, k // 4), near_side(my_y, k % 4))
    zz = jnp.where(first, near_side(my_z, k % 4), far_side(my_z, k // 4))
    cabs = (yy * 4 + zz).astype(jnp.int32)
    place = jnp.concatenate([my_head[None], cabs])
    own_g = lax.dynamic_index_in_dim(g8, own_block, 0, False).reshape(16, 16)
    own_p = lax.dynamic_index_in_dim(p8, own_block, 0, False).reshape(16, 16)
    gp = jnp.stack([own_g[cabs].reshape(256), own_p[cabs].reshape(256)])
    own_ids = lax.dynamic_slice(ids8, (own_block, my_cluster * 16), (1, 16)).reshape(16, 1)
    g_rows = lax.dynamic_slice(g8, (my_row * 4, my_cluster * 16), (4, 16)).reshape(64, 1)
    p_rows = lax.dynamic_slice(p8, (my_row * 4, my_cluster * 16), (4, 16)).reshape(64, 1)
    land = (g8 == my_cluster)[:, None, :] & (p8[:, None, :] == jnp.arange(FULL)[None, :, None])
    value = ids8 % LOCAL * 1024 + tg8
    code = jnp.sum(jnp.where(land, value[:, None, :], 0), axis=2)[:, :, None]
    block = lambda flip, d: (my_row ^ flip) * 4 + (my_head + d) % 4
    start = (my_row * 4 + my_head) * LEAF_COLS
    near_place = jnp.stack([block(0, 0), block(0, 1), block(0, 3), block(1, 0), block(1, 1), block(1, 3), start])
    far_place = jnp.stack([block(0, 2), block(1, 2), start])
    end_place = jnp.stack([my_row, my_cluster])
    topw = jnp.pad(top_weight, ((0, 0), (0, 128 - CLUSTERS)))

    att_a, att_b = attend(lengths, queries, new_keys, new_values, key_cache, value_cache)
    za, yb = gather_z(att_a), gather_y(att_b)
    pieces_a = [za] + [cluster_permute(za, lambda y, z: (y + d, z)) for d in OFFS[1:]]
    pieces_b = [yb] + [cluster_permute(yb, lambda y, z: (y, z + d)) for d in OFFS[1:]]
    lhs, sums0 = project_first(pieces_a, pieces_b, out_weight)
    parts0 = lax.all_to_all(sums0, "head", 0, 0, tiled=True)
    sums1 = project_second(lhs, out_weight)
    parts1 = lax.all_to_all(sums1, "head", 0, 0, tiled=True)

    args = (parts0, parts1, residual_in.reshape(4, 16, 16, 512), norm_gain[None, :], topw, place, near_place, far_place, end_place, gp, code, own_ids, g_rows, p_rows, leaf_weight)
    return lax.cond(jnp.max(p8) < SMALL - 1, functools.partial(tail, SMALL), functools.partial(tail, FULL), *args)


def solution(mesh):
    placed = (
        P(None, ("rows", "cluster"), "head"),
        P(None, ("rows", "cluster"), "head"),
        P(None, ("rows", "cluster"), "head"),
        P(("rows", "cluster"), "head", None, None),
        P(("rows", "cluster"), "head", None, None),
        P(("rows", "cluster")),
        P(None, "rows", "cluster"),
        P("head", "cluster"),
        P("cluster"),
        P("cluster", None),
        P("cluster", None, ("rows", "head")),
        P(),
        P(),
    )
    return jax.shard_map(
        shards, mesh=mesh, in_specs=placed, out_specs=P(None, ("rows", "cluster")), check_vma=False
    )
```

```python
import functools
import jax
import jax.numpy as jnp
from jax import lax
from jax.experimental import pallas as pl
from jax.experimental.pallas import tpu as pltpu
from jax.sharding import PartitionSpec as P


D = 8192
CLUSTERS = 80
STEPS = 4
LOCAL = 5
LEAF_COLS = 128
SIDE = 4
OFFS = (0, 1, 3, 2)
SMALL = 40
FULL = 64
F32 = jnp.float32
BF16 = jnp.bfloat16
VMEM = pl.BlockSpec(memory_space=pltpu.VMEM)
SMEM = pl.BlockSpec(memory_space=pltpu.SMEM)


def dot_nt(a, b):
    return lax.dot_general(a, b, (((1,), (1,)), ((), ())), preferred_element_type=F32)


def dot_nn(a, b):
    return lax.dot_general(a, b, (((1,), (0,)), ((), ())), preferred_element_type=F32)


def attend_kernel(len_ref, q_ref, nk_ref, nv_ref, k_ref, v_ref, out_ref, q_scr, o_scr, q2_scr, o2_scr):
    step = pl.program_id(0)
    heads = 16
    scale = 128 ** (-0.5)

    @pl.when(step == 0)
    def _():
        for head in range(heads):
            part = q_ref[:, :, head * 128:(head + 1) * 128]
            q_scr[head] = part.reshape(64, 128).astype(F32)

    row0 = step * 4
    m_col = lax.broadcasted_iota(jnp.int32, (128, 64), 0)
    n_row = lax.broadcasted_iota(jnp.int32, (128, 64), 1)
    recent_ok = ((n_row & 15) == row0 + (m_col >> 5)) & ((n_row >> 4) <= (m_col & 3))
    lane = lax.broadcasted_iota(jnp.int32, (32, 256), 1)
    for kv in range(2):
        for rr in range(4):
            for g in range(8):
                q2_scr[kv, rr * 32 + g * 4:rr * 32 + g * 4 + 4, :] = q_scr[kv * 8 + g, pl.ds(row0 + rr, 4, stride=16), :]
        q2 = q2_scr[kv].astype(BF16)
        cached = []
        for rr in range(4):
            s = dot_nt(q2[rr * 32:(rr + 1) * 32], k_ref[rr, kv]) * scale
            cached.append(jnp.where(lane < len_ref[row0 + rr], s, -jnp.inf))
        cached = jnp.concatenate(cached, axis=0)
        nk = nk_ref[:, :, kv * 128:(kv + 1) * 128].reshape(64, 128)
        nv = nv_ref[:, :, kv * 128:(kv + 1) * 128].reshape(64, 128)
        recent = jnp.where(recent_ok, dot_nt(q2, nk) * scale, -jnp.inf)
        peak = jnp.maximum(jnp.max(cached, axis=1, keepdims=True), jnp.max(recent, axis=1, keepdims=True))
        ec = jnp.exp(cached - peak)
        er = jnp.exp(recent - peak)
        inv = 1.0 / (jnp.sum(ec, axis=1, keepdims=True) + jnp.sum(er, axis=1, keepdims=True))
        wc = (ec * inv).astype(BF16)
        wr = (er * inv).astype(BF16)
        out = []
        for rr in range(4):
            out.append(dot_nn(wc[rr * 32:(rr + 1) * 32], v_ref[rr, kv]))
        o2_scr[kv] = jnp.concatenate(out, axis=0) + dot_nn(wr, nv)
        for rr in range(4):
            for g in range(8):
                o_scr[kv * 8 + g, pl.ds(row0 + rr, 4, stride=16), :] = o2_scr[kv, rr * 32 + g * 4:rr * 32 + g * 4 + 4, :]

    @pl.when(step == pl.num_programs(0) - 1)
    def _():
        for head in range(heads):
            cols = slice(head * 128, (head + 1) * 128)
            out_ref[:, :, cols] = o_scr[head].reshape(4, 16, 128).astype(BF16)


def attend(lengths, q, nk, nv, k, v):
    whole = lambda shape: pl.BlockSpec(shape, lambda i, *_: (0,) * len(shape))
    block = pl.BlockSpec((4, 2, 256, 128), lambda i, *_: (i, 0, 0, 0))
    return pl.pallas_call(
        attend_kernel,
        out_shape=jax.ShapeDtypeStruct((4, 16, 2048), BF16),
        grid_spec=pltpu.PrefetchScalarGridSpec(
            num_scalar_prefetch=1,
            grid=(4,),
            in_specs=[whole((4, 16, 2048)), whole((4, 16, 256)), whole((4, 16, 256)), block, block],
            out_specs=whole((4, 16, 2048)),
            scratch_shapes=[
                pltpu.VMEM((16, 64, 128), F32),
                pltpu.VMEM((16, 64, 128), F32),
                pltpu.VMEM((2, 128, 128), F32),
                pltpu.VMEM((2, 128, 128), F32),
            ],
        ),
        cost_estimate=pl.CostEstimate(flops=300_000_000, bytes_accessed=5_000_000, transcendentals=400_000),
        name="attend",
    )(lengths, q, nk, nv, k, v)


NEAR = ((0, 0), (0, 1), (0, 2), (0, 3), (1, 0), (2, 0), (3, 0))
FAR = tuple((i, j) for i in range(1, 4) for j in range(1, 4))


def project_near_kernel(*refs):
    w_ref, out_ref, lhs = refs[7:]
    for k in range(7):
        for s in range(4):
            lhs[s * 112 + k * 16:s * 112 + (k + 1) * 16, :] = refs[k][s]
    for n in range(2):
        cols = slice(n * 256, (n + 1) * 256)
        rows = dot_nn(lhs[...], w_ref[:, cols]).astype(BF16)
        for s in range(4):
            out_ref[s, :, cols] = rows[s * 112:(s + 1) * 112]


def project_far_kernel(*refs):
    along_y, along_z = refs[0:3], refs[3:6]
    near_ref, w_ref, out_ref, lhs = refs[6:]
    for s in range(4):
        for k, (i, j) in enumerate(FAR):
            rows = along_y[i - 1][j - 1, s] if s < 2 else along_z[j - 1][i - 1, s - 2]
            lhs[s * 144 + k * 16:s * 144 + (k + 1) * 16, :] = rows
        out_ref[s, 0:112, :] = near_ref[s]
    for n in range(2):
        cols = slice(n * 256, (n + 1) * 256)
        rows = dot_nn(lhs[...], w_ref[:, cols]).astype(BF16)
        for s in range(4):
            out_ref[s, 112:256, cols] = rows[s * 144:(s + 1) * 144]


def pack_kernel(low, a_ref, b_ref, c_ref, out_ref):
    for k, ref in enumerate((a_ref, b_ref, c_ref)):
        out_ref[k] = ref[low:low + 2]


def pack(low, blocks):
    return pl.pallas_call(
        functools.partial(pack_kernel, low),
        out_shape=jax.ShapeDtypeStruct((3, 2, 16, 2048), BF16),
        in_specs=[VMEM] * 3,
        out_specs=VMEM,
        name="pack",
    )(*blocks)


def project_near(blocks, w):
    return pl.pallas_call(
        project_near_kernel,
        out_shape=jax.ShapeDtypeStruct((4, 112, 512), BF16),
        in_specs=[VMEM] * 8,
        out_specs=VMEM,
        scratch_shapes=[pltpu.VMEM((448, 2048), BF16)],
        cost_estimate=pl.CostEstimate(flops=940_000_000, bytes_accessed=4_000_000, transcendentals=0),
        name="project_near",
    )(*blocks, w)


def project_far(along_y, along_z, near, w):
    return pl.pallas_call(
        project_far_kernel,
        out_shape=jax.ShapeDtypeStruct((4, 256, 512), BF16),
        in_specs=[VMEM] * 8,
        out_specs=VMEM,
        scratch_shapes=[pltpu.VMEM((576, 2048), BF16)],
        cost_estimate=pl.CostEstimate(flops=1_200_000_000, bytes_accessed=5_000_000, transcendentals=0),
        name="project_far",
    )(*along_y, *along_z, near, w)


def post_kernel(cap, place_ref, part_ref, res_ref, gain_ref, topw_ref, gp_ref, out_ref, top_ref, top_scr):
    res = jnp.concatenate([res_ref[0, place_ref[k + 1]] for k in range(16)], axis=0).astype(F32)
    mixed = (part_ref[0].astype(F32) + part_ref[1].astype(F32)) + (part_ref[2].astype(F32) + part_ref[3].astype(F32))
    hidden = mixed + res
    squares = jnp.sum(hidden * hidden, axis=1, keepdims=True)
    gated = (hidden * gain_ref[...]).astype(BF16)
    wide = jnp.broadcast_to(squares, (256, 128))
    top_scr[...] = wide
    top_scr[:, 0:CLUSTERS] = dot_nt(gated, topw_ref[...])
    for k in range(16):
        top_ref[place_ref[k + 1]] = top_scr[k * 16:(k + 1) * 16]
    dest = gp_ref[0:1, :]
    rank = gp_ref[1:2, :]
    rows = lax.broadcasted_iota(jnp.int32, (16, 256), 0)
    sq_row = wide.T[0:16]
    spread = jnp.where(rows == dest, sq_row, 0.0)
    hi = spread.astype(BF16)
    rest = spread - hi.astype(F32)
    mid = rest.astype(BF16)
    low = (rest - mid.astype(F32)).astype(BF16)
    by_rank = (lax.broadcasted_iota(jnp.int32, (128, 256), 0) == rank).astype(F32).astype(BF16)
    code = jnp.concatenate([dot_nt(hi, by_rank), dot_nt(mid, by_rank), dot_nt(low, by_rank), jnp.zeros((16, 128), F32)], axis=1).astype(BF16)
    slot = dest * cap + rank
    pick = (lax.broadcasted_iota(jnp.int32, (16 * cap, 256), 0) == slot).astype(F32).astype(BF16)
    srow = lax.broadcasted_iota(jnp.int32, (16 * cap, 16), 0)
    scol = lax.broadcasted_iota(jnp.int32, (16 * cap, 16), 1)
    last = (srow == scol * cap + cap - 1).astype(F32).astype(BF16)
    out_ref[...] = (dot_nn(pick, gated) + dot_nn(last, code)).astype(BF16)


def post(cap, place, parts, residual, gain, topw, gp):
    return pl.pallas_call(
        functools.partial(post_kernel, cap),
        out_shape=(jax.ShapeDtypeStruct((16 * cap, 512), BF16), jax.ShapeDtypeStruct((16, 16, 128), F32)),
        grid_spec=pltpu.PrefetchScalarGridSpec(
            num_scalar_prefetch=1,
            grid=(1,),
            in_specs=[
                pl.BlockSpec((4, 256, 512), lambda i, p: (0, 0, 0)),
                pl.BlockSpec((1, 16, 16, 512), lambda i, p: (p[0], 0, 0, 0)),
                pl.BlockSpec((1, 512), lambda i, p: (0, 0)),
                pl.BlockSpec((CLUSTERS, 512), lambda i, p: (0, 0)),
                pl.BlockSpec((2, 256), lambda i, p: (0, 0)),
            ],
            out_specs=(
                pl.BlockSpec((16 * cap, 512), lambda i, p: (0, 0)),
                pl.BlockSpec((16, 16, 128), lambda i, p: (0, 0, 0)),
            ),
            scratch_shapes=[pltpu.VMEM((256, 128), F32)],
        ),
        cost_estimate=pl.CostEstimate(flops=300_000_000, bytes_accessed=3_000_000, transcendentals=0),
        name="post",
    )(place, parts, residual, gain, topw, gp)


def stack_rows(cap, blocks):
    if cap % 16 == 0:
        return jnp.concatenate(blocks, axis=0)
    return jnp.concatenate([b.astype(F32) for b in blocks], axis=0).astype(BF16)


def leaf_accumulate(cap, pieces, w_ref, acc, sq_acc):
    @pl.when(pl.program_id(0) == 0)
    def _():
        acc[...] = jnp.zeros_like(acc)
        sq_acc[...] = jnp.zeros_like(sq_acc)

    lhs = []
    for c in range(4):
        blocks = [ref[c] for ref in pieces]
        for k, block in enumerate(blocks):
            spare = block[cap - 8:cap].astype(F32)[7:8]
            sq_acc[k:k + 1] += spare[:, 0:128] + spare[:, 128:256] + spare[:, 256:384]
        lhs.append(stack_rows(cap, blocks))
    lhs = jnp.concatenate(lhs, axis=1)
    for first, width in ((0, 2), (2, 2), (4, 1)):
        part = [w_ref[first + k] for k in range(width)]
        rhs = part[0] if width == 1 else jnp.concatenate(part, axis=1)
        acc[:, first * 128:(first + width) * 128] += dot_nn(lhs, rhs)


def leaf_finish(cap, n, place_ref, code_ref, acc, sq_acc, write):
    start = place_ref[n]
    r_i = lax.broadcasted_iota(jnp.int32, (cap, 128), 0)
    c_i = lax.broadcasted_iota(jnp.int32, (cap, 128), 1)
    diag = r_i == c_i
    for k in range(n):
        b = place_ref[k]
        code = code_ref[b][:cap]
        local = code >> 10
        target = (code & 1023) - start
        sq = jnp.sum(jnp.where(diag, jnp.broadcast_to(sq_acc[k:k + 1], (cap, 128)), 0.0), axis=1, keepdims=True)
        logits = jnp.zeros((cap, 128), F32)
        for j in range(LOCAL):
            logits = jnp.where(local == j, acc[k * cap:(k + 1) * cap, j * 128:(j + 1) * 128], logits)
        logits = logits * lax.rsqrt(sq / D + 1e-05)
        peak = jnp.max(logits, axis=1, keepdims=True)
        lse = peak + jnp.log(jnp.sum(jnp.exp(logits - peak), axis=1, keepdims=True))
        hit = jnp.sum(jnp.where(c_i == target, logits, 0.0), axis=1, keepdims=True)
        write(b, jnp.sum(jnp.where(diag, lse, 0.0), axis=0, keepdims=True))
        write(b + 8, jnp.sum(jnp.where(diag, hit, 0.0), axis=0, keepdims=True))


def near_kernel(cap, place_ref, *refs):
    pieces, (code_ref, w_ref, out_ref, acc, sq_acc) = refs[:6], refs[6:]
    leaf_accumulate(cap, pieces, w_ref, acc, sq_acc)

    @pl.when(pl.program_id(0) == pl.num_programs(0) - 1)
    def _():
        out_ref[...] = jnp.zeros_like(out_ref)

        def write(at, row):
            out_ref[pl.ds(at, 1), :] = row

        leaf_finish(cap, 6, place_ref, code_ref, acc, sq_acc, write)


def far_kernel(cap, place_ref, *refs):
    pieces, (code_ref, near_ref, top_ref, w_ref, out_ref, acc, sq_acc, state) = refs[:2], refs[2:]
    leaf_accumulate(cap, pieces, w_ref, acc, sq_acc)

    @pl.when(pl.program_id(0) == pl.num_programs(0) - 1)
    def _():
        state[0:16, :] = near_ref[...]
        state[16:24, :] = top_ref[...]

        def write(at, row):
            state[pl.ds(at, 1), :] = row

        leaf_finish(cap, 2, place_ref, code_ref, acc, sq_acc, write)
        out_ref[...] = jnp.broadcast_to(state[...][None], out_ref.shape)


def leaf_call(cap, kernel, name, out_shape, place, pieces, small, w, scratch):
    n = len(pieces)
    fixed = lambda shape: pl.BlockSpec(shape, lambda c, p: (0,) * len(shape))
    return pl.pallas_call(
        functools.partial(kernel, cap),
        out_shape=jax.ShapeDtypeStruct(out_shape, F32),
        grid_spec=pltpu.PrefetchScalarGridSpec(
            num_scalar_prefetch=1,
            grid=(4,),
            in_specs=[pl.BlockSpec((4, cap, 512), lambda c, p: (c, 0, 0))] * n
            + [fixed(a.shape) for a in small]
            + [pl.BlockSpec((LOCAL, 2048, 128), lambda c, p: (0, c, 0))],
            out_specs=fixed(out_shape),
            scratch_shapes=[pltpu.VMEM((n * cap, LOCAL * 128), F32), pltpu.VMEM((8, 128), F32)] + scratch,
        ),
        cost_estimate=pl.CostEstimate(flops=2 * n * cap * 8192 * 640, bytes_accessed=11_000_000, transcendentals=0),
        name=name,
    )(place, *pieces, *small, w)


def top_kernel(top_ref, ids_ref, out_ref):
    total = top_ref[0]
    for k in range(1, 16):
        total = total + top_ref[k]
    lane = lax.broadcasted_iota(jnp.int32, (16, 128), 1)
    row = lax.broadcasted_iota(jnp.int32, (16, 128), 0)
    logits = total * lax.rsqrt(total[:, CLUSTERS:CLUSTERS + 1] / D + 1e-05)
    logits = jnp.where(lane < CLUSTERS, logits, -jnp.inf)
    peak = jnp.max(logits, axis=1, keepdims=True)
    norm = peak + jnp.log(jnp.sum(jnp.exp(logits - peak), axis=1, keepdims=True))
    own = jnp.sum(jnp.where(lane == ids_ref[...], logits, 0.0), axis=1, keepdims=True) - norm
    picked = jnp.sum(jnp.where(lane == row, own, 0.0), axis=0, keepdims=True)
    out_ref[...] = jnp.broadcast_to(picked, (8, 128))


def merge_kernel(place_ref, heard_ref, note_ref, top_ref):
    blocks = [heard_ref[d] for d in range(8)]
    peak = blocks[0][0:8]
    for d in range(1, 8):
        peak = jnp.maximum(peak, blocks[d][0:8])
    mass = jnp.exp(blocks[0][0:8] - peak)
    picked = blocks[0][8:16]
    for d in range(1, 8):
        mass = mass + jnp.exp(blocks[d][0:8] - peak)
        picked = picked + blocks[d][8:16]
    leaf = picked - (peak + jnp.log(mass))
    low = place_ref[0] == 0
    leaf = jnp.where(low, leaf, jnp.concatenate([leaf[4:8], leaf[0:4]], axis=0))
    note_ref[...] = jnp.broadcast_to(leaf[None], note_ref.shape)
    for s in range(4):
        top_ref[s:s + 1, :] = jnp.where(low, blocks[s][16:17], blocks[4 + s][16:17])


def final_kernel(back_ref, top_ref, g_ref, p_ref, out_ref):
    lane = lax.broadcasted_iota(jnp.int32, (16, 128), 1)
    row = lax.broadcasted_iota(jnp.int32, (16, 128), 0)
    for s in range(4):
        g = jnp.broadcast_to(g_ref[s * 16:(s + 1) * 16], (16, 128))
        at = lane == p_ref[s * 16:(s + 1) * 16]
        found = jnp.where(lane == row, top_ref[s:s + 1], 0.0)
        for c in range(16):
            found = found + jnp.where(at & (g == c), back_ref[c, s:s + 1], 0.0)
        column = jnp.sum(found, axis=1, keepdims=True)
        out_ref[s:s + 1, :] = jnp.sum(jnp.where(lane == row, column, 0.0), axis=0, keepdims=True)[:, 0:16]


def small_call(kernel, name, out_shape, *args, smem=0):
    many = isinstance(out_shape[0], tuple)
    shapes = out_shape if many else (out_shape,)
    shapes = tuple(jax.ShapeDtypeStruct(s, F32) for s in shapes)
    return pl.pallas_call(
        kernel,
        out_shape=shapes if many else shapes[0],
        in_specs=[SMEM] * smem + [VMEM] * (len(args) - smem),
        out_specs=(VMEM,) * len(shapes) if many else VMEM,
        name=name,
    )(*args)


def from_cluster(x, dy, dz):
    pairs = []
    for c in range(16):
        pairs.append(((c // 4 + dy) % 4 * 4 + (c % 4 + dz) % 4, c))
    return lax.ppermute(x, "cluster", pairs)


def from_x(x, d):
    return lax.ppermute(x, "head", [((h + d) % 4, h) for h in range(4)])


def swap(x):
    return lax.ppermute(x, "rows", [(0, 1), (1, 0)])


def tail(cap, parts, residual, gain, topw, places, gp, code, own_ids, g_rows, p_rows, leaf_weight):
    place, near_place, far_place, end_place = places
    outgoing, top = post(cap, place, parts, residual, gain, topw, gp)
    own = lax.all_to_all(outgoing.reshape(16, cap, 512), "cluster", 0, 0, tiled=True)
    plus, minus = from_x(own, 1), from_x(own, 3)
    top = lax.all_to_all(top, "cluster", 0, 0, tiled=True)
    plus, minus, top = lax.optimization_barrier((plus, minus, top))
    top_row = small_call(top_kernel, "top", (8, 128), top, own_ids)
    onward = jnp.where(end_place[0] == 0, plus, minus)
    pairs = [((h + 1) % 4, h) for h in range(4)] + [(4 + (h + 3) % 4, 4 + h) for h in range(4)]
    far = lax.ppermute(onward, ("rows", "head"), pairs)
    near = leaf_call(cap, near_kernel, "near", (16, 128), near_place, [own, plus, minus, swap(own), swap(plus), swap(minus)], [code], leaf_weight, [])
    far, near, top_row = lax.optimization_barrier((far, near, top_row))
    heard = leaf_call(cap, far_kernel, "far", (8, 24, 128), far_place, [far, swap(far)], [code, near, top_row], leaf_weight, [pltpu.VMEM((24, 128), F32)])
    heard = lax.all_to_all(heard, ("rows", "head"), 0, 0, tiled=True)
    note, tops = small_call(merge_kernel, "merge", ((16, 8, 128), (4, 128)), end_place, heard, smem=1)
    back = lax.all_to_all(note, "cluster", 0, 0, tiled=True)
    return small_call(final_kernel, "final", (4, 16), back, tops, g_rows, p_rows)


def shards(queries, new_keys, new_values, key_cache, value_cache, lengths, residual_in, out_weight, norm_gain, top_weight, leaf_weight, cluster_ids, targets):
    my_cluster = lax.axis_index("cluster").astype(jnp.int32)
    my_row = lax.axis_index("rows").astype(jnp.int32)
    my_head = lax.axis_index("head").astype(jnp.int32)
    my_y, my_z = my_cluster // SIDE, my_cluster % SIDE

    ids8 = cluster_ids[:, :, 0].reshape(STEPS, 2, 256).transpose(1, 0, 2).reshape(8, 256)
    tg8 = targets.reshape(STEPS, 2, 256).transpose(1, 0, 2).reshape(8, 256)
    g8 = ids8 // LOCAL
    index = jnp.arange(256)
    earlier = (g8[:, :, None] == g8[:, None, :]) & (index[None, None, :] < index[None, :, None])
    p8 = jnp.sum(earlier.astype(jnp.int32), axis=2)
    own_block = my_row * 4 + my_head
    order = NEAR + FAR
    dy = jnp.array([OFFS[i] for i, _ in order], jnp.int32)
    dz = jnp.array([OFFS[j] for _, j in order], jnp.int32)
    cabs = ((my_y + dy) & 3) * 4 + ((my_z + dz) & 3)
    place = jnp.concatenate([my_head[None], cabs])
    own_g = lax.dynamic_index_in_dim(g8, own_block, 0, False).reshape(16, 16)
    own_p = lax.dynamic_index_in_dim(p8, own_block, 0, False).reshape(16, 16)
    gp = jnp.stack([own_g[cabs].reshape(256), own_p[cabs].reshape(256)])
    own_ids = lax.dynamic_slice(ids8, (own_block, my_cluster * 16), (1, 16)).reshape(16, 1)
    g_rows = lax.dynamic_slice(g8, (my_row * 4, my_cluster * 16), (4, 16)).reshape(64, 1)
    p_rows = lax.dynamic_slice(p8, (my_row * 4, my_cluster * 16), (4, 16)).reshape(64, 1)
    land = (g8 == my_cluster)[:, None, :] & (p8[:, None, :] == jnp.arange(FULL)[None, :, None])
    value = ids8 % LOCAL * 1024 + tg8
    code = jnp.sum(jnp.where(land, value[:, None, :], 0), axis=2)[:, :, None]
    block = lambda flip, d: (my_row ^ flip) * 4 + ((my_head + d) & 3)
    start = (my_row * 4 + my_head) * LEAF_COLS
    near_place = jnp.stack([block(0, 0), block(0, 1), block(0, 3), block(1, 0), block(1, 1), block(1, 3), start])
    far_place = jnp.stack([block(0, 2), block(1, 2), start])
    end_place = jnp.stack([my_row, my_cluster])
    fits = jnp.max(p8) < SMALL - 1
    places = (place, near_place, far_place, end_place)
    places, gp, code, own_ids, g_rows, p_rows, fits = lax.optimization_barrier((places, gp, code, own_ids, g_rows, p_rows, fits))

    att = attend(lengths, queries, new_keys, new_values, key_cache, value_cache)
    along_z = [from_cluster(att, 0, d) for d in OFFS[1:]]
    along_y = [from_cluster(att, d, 0) for d in OFFS[1:]]
    row = pack(0, along_z)
    column = pack(2, along_y)
    far_y = [from_cluster(row, d, 0) for d in OFFS[1:]]
    far_z = [from_cluster(column, 0, d) for d in OFFS[1:]]
    sums = project_near([att, *along_z, *along_y], out_weight)
    sums = project_far(far_y, far_z, sums, out_weight)
    parts = lax.all_to_all(sums, "head", 0, 0, tiled=True)

    args = (parts, residual_in.reshape(4, 16, 16, 512), norm_gain[None, :], top_weight.T, places, gp, code, own_ids, g_rows, p_rows, leaf_weight)
    return lax.cond(fits, functools.partial(tail, SMALL), functools.partial(tail, FULL), *args)


def solution(mesh):
    placed = (
        P(None, ("rows", "cluster"), "head"),
        P(None, ("rows", "cluster"), "head"),
        P(None, ("rows", "cluster"), "head"),
        P(("rows", "cluster"), "head", None, None),
        P(("rows", "cluster"), "head", None, None),
        P(("rows", "cluster")),
        P(None, "rows", "cluster"),
        P("head", "cluster"),
        P("cluster"),
        P("cluster", None),
        P("cluster", None, ("rows", "head")),
        P(),
        P(),
    )
    return jax.shard_map(
        shards, mesh=mesh, in_specs=placed, out_specs=P(None, ("rows", "cluster")), check_vma=False
    )
```

```python
import functools
import jax
import jax.numpy as jnp
from jax import lax
from jax.experimental import pallas as pl
from jax.experimental.pallas import tpu as pltpu
from jax.sharding import PartitionSpec as P


D = 8192
CLUSTERS = 80
STEPS = 4
LOCAL = 5
LEAF_COLS = 128
SIDE = 4
OFFS = (0, 1, 3, 2)
SMALL = 40
FULL = 64
F32 = jnp.float32
BF16 = jnp.bfloat16
VMEM = pl.BlockSpec(memory_space=pltpu.VMEM)
SMEM = pl.BlockSpec(memory_space=pltpu.SMEM)


def dot_nt(a, b):
    return lax.dot_general(a, b, (((1,), (1,)), ((), ())), preferred_element_type=F32)


def dot_nn(a, b):
    return lax.dot_general(a, b, (((1,), (0,)), ((), ())), preferred_element_type=F32)


def attend_kernel(len_ref, q_ref, nk_ref, nv_ref, k_ref, v_ref, oa_ref, ob_ref, q_scr, o_scr, q2_scr, o2_scr):
    step = pl.program_id(0)
    heads = 16
    scale = 128 ** (-0.5)

    @pl.when(step == 0)
    def _():
        for head in range(heads):
            part = q_ref[:, :, head * 128:(head + 1) * 128]
            q_scr[head] = part.reshape(64, 128).astype(F32)

    row0 = step * 4
    m_col = lax.broadcasted_iota(jnp.int32, (128, 64), 0)
    n_row = lax.broadcasted_iota(jnp.int32, (128, 64), 1)
    recent_ok = ((n_row & 15) == row0 + (m_col >> 5)) & ((n_row >> 4) <= (m_col & 3))
    lane = lax.broadcasted_iota(jnp.int32, (32, 256), 1)
    for kv in range(2):
        for rr in range(4):
            for g in range(8):
                q2_scr[kv, rr * 32 + g * 4:rr * 32 + g * 4 + 4, :] = q_scr[kv * 8 + g, pl.ds(row0 + rr, 4, stride=16), :]
        q2 = q2_scr[kv].astype(BF16)
        cached = []
        for rr in range(4):
            s = dot_nt(q2[rr * 32:(rr + 1) * 32], k_ref[rr, kv]) * scale
            cached.append(jnp.where(lane < len_ref[row0 + rr], s, -jnp.inf))
        cached = jnp.concatenate(cached, axis=0)
        nk = nk_ref[:, :, kv * 128:(kv + 1) * 128].reshape(64, 128)
        nv = nv_ref[:, :, kv * 128:(kv + 1) * 128].reshape(64, 128)
        recent = jnp.where(recent_ok, dot_nt(q2, nk) * scale, -jnp.inf)
        peak = jnp.maximum(jnp.max(cached, axis=1, keepdims=True), jnp.max(recent, axis=1, keepdims=True))
        ec = jnp.exp(cached - peak)
        er = jnp.exp(recent - peak)
        inv = 1.0 / (jnp.sum(ec, axis=1, keepdims=True) + jnp.sum(er, axis=1, keepdims=True))
        wc = (ec * inv).astype(BF16)
        wr = (er * inv).astype(BF16)
        out = []
        for rr in range(4):
            out.append(dot_nn(wc[rr * 32:(rr + 1) * 32], v_ref[rr, kv]))
        o2_scr[kv] = jnp.concatenate(out, axis=0) + dot_nn(wr, nv)
        for rr in range(4):
            for g in range(8):
                o_scr[kv * 8 + g, pl.ds(row0 + rr, 4, stride=16), :] = o2_scr[kv, rr * 32 + g * 4:rr * 32 + g * 4 + 4, :]

    @pl.when(step == pl.num_programs(0) - 1)
    def _():
        for head in range(heads):
            cols = slice(head * 128, (head + 1) * 128)
            oa_ref[:, :, cols] = o_scr[head, 0:32].reshape(2, 16, 128).astype(BF16)
            ob_ref[:, :, cols] = o_scr[head, 32:64].reshape(2, 16, 128).astype(BF16)


def attend(lengths, q, nk, nv, k, v):
    whole = lambda shape: pl.BlockSpec(shape, lambda i, *_: (0,) * len(shape))
    block = pl.BlockSpec((4, 2, 256, 128), lambda i, *_: (i, 0, 0, 0))
    return pl.pallas_call(
        attend_kernel,
        out_shape=(jax.ShapeDtypeStruct((2, 16, 2048), BF16),) * 2,
        grid_spec=pltpu.PrefetchScalarGridSpec(
            num_scalar_prefetch=1,
            grid=(4,),
            in_specs=[whole((4, 16, 2048)), whole((4, 16, 256)), whole((4, 16, 256)), block, block],
            out_specs=(whole((2, 16, 2048)),) * 2,
            scratch_shapes=[
                pltpu.VMEM((16, 64, 128), F32),
                pltpu.VMEM((16, 64, 128), F32),
                pltpu.VMEM((2, 128, 128), F32),
                pltpu.VMEM((2, 128, 128), F32),
            ],
        ),
        cost_estimate=pl.CostEstimate(flops=300_000_000, bytes_accessed=5_000_000, transcendentals=400_000),
        name="attend",
    )(lengths, q, nk, nv, k, v)


def project_near_kernel(*refs):
    pieces = (refs[0:3], refs[3:6])
    w_ref, out_ref, lhs = refs[6:]
    for s in range(4):
        for i in range(3):
            for j in range(4):
                at = s * 192 + (i * 4 + j) * 16
                lhs[at:at + 16, :] = pieces[s // 2][i][j, s % 2]
    for n in range(2):
        cols = slice(n * 256, (n + 1) * 256)
        rows = dot_nn(lhs[...], w_ref[:, cols]).astype(BF16)
        for s in range(4):
            out_ref[s, :, cols] = rows[s * 192:(s + 1) * 192]


def project_far_kernel(a_ref, b_ref, near_ref, w_ref, out_ref, lhs):
    for s in range(4):
        for j in range(4):
            lhs[s * 64 + j * 16:s * 64 + (j + 1) * 16, :] = (a_ref, b_ref)[s // 2][j, s % 2]
        out_ref[s, 0:192, :] = near_ref[s]
    for n in range(2):
        cols = slice(n * 256, (n + 1) * 256)
        rows = dot_nn(lhs[...], w_ref[:, cols]).astype(BF16)
        for s in range(4):
            out_ref[s, 192:256, cols] = rows[s * 64:(s + 1) * 64]


def project_near(blocks, w):
    return pl.pallas_call(
        project_near_kernel,
        out_shape=jax.ShapeDtypeStruct((4, 192, 512), BF16),
        in_specs=[VMEM] * 7,
        out_specs=VMEM,
        scratch_shapes=[pltpu.VMEM((768, 2048), BF16)],
        cost_estimate=pl.CostEstimate(flops=1_600_000_000, bytes_accessed=6_000_000, transcendentals=0),
        name="project_near",
    )(*blocks, w)


def project_far(a, b, near, w):
    return pl.pallas_call(
        project_far_kernel,
        out_shape=jax.ShapeDtypeStruct((4, 256, 512), BF16),
        in_specs=[VMEM] * 4,
        out_specs=VMEM,
        scratch_shapes=[pltpu.VMEM((256, 2048), BF16)],
        cost_estimate=pl.CostEstimate(flops=540_000_000, bytes_accessed=4_000_000, transcendentals=0),
        name="project_far",
    )(a, b, near, w)


def post_kernel(cap, place_ref, part_ref, res_ref, gain_ref, topw_ref, gp_ref, out_ref, top_ref, top_scr):
    res = jnp.concatenate([res_ref[0, place_ref[k + 1]] for k in range(16)], axis=0).astype(F32)
    mixed = (part_ref[0].astype(F32) + part_ref[1].astype(F32)) + (part_ref[2].astype(F32) + part_ref[3].astype(F32))
    hidden = mixed + res
    squares = jnp.sum(hidden * hidden, axis=1, keepdims=True)
    gated = (hidden * gain_ref[...]).astype(BF16)
    wide = jnp.broadcast_to(squares, (256, 128))
    top_scr[...] = wide
    top_scr[:, 0:CLUSTERS] = dot_nt(gated, topw_ref[...])
    for k in range(16):
        top_ref[place_ref[k + 1]] = top_scr[k * 16:(k + 1) * 16]
    dest = gp_ref[0:1, :]
    rank = gp_ref[1:2, :]
    rows = lax.broadcasted_iota(jnp.int32, (16, 256), 0)
    sq_row = wide.T[0:16]
    spread = jnp.where(rows == dest, sq_row, 0.0)
    hi = spread.astype(BF16)
    rest = spread - hi.astype(F32)
    mid = rest.astype(BF16)
    low = (rest - mid.astype(F32)).astype(BF16)
    by_rank = (lax.broadcasted_iota(jnp.int32, (128, 256), 0) == rank).astype(F32).astype(BF16)
    code = jnp.concatenate([dot_nt(hi, by_rank), dot_nt(mid, by_rank), dot_nt(low, by_rank), jnp.zeros((16, 128), F32)], axis=1).astype(BF16)
    slot = dest * cap + rank
    pick = (lax.broadcasted_iota(jnp.int32, (16 * cap, 256), 0) == slot).astype(F32).astype(BF16)
    srow = lax.broadcasted_iota(jnp.int32, (16 * cap, 16), 0)
    scol = lax.broadcasted_iota(jnp.int32, (16 * cap, 16), 1)
    last = (srow == scol * cap + cap - 1).astype(F32).astype(BF16)
    out_ref[...] = (dot_nn(pick, gated) + dot_nn(last, code)).astype(BF16)


def post(cap, place, parts, residual, gain, topw, gp):
    return pl.pallas_call(
        functools.partial(post_kernel, cap),
        out_shape=(jax.ShapeDtypeStruct((16 * cap, 512), BF16), jax.ShapeDtypeStruct((16, 16, 128), F32)),
        grid_spec=pltpu.PrefetchScalarGridSpec(
            num_scalar_prefetch=1,
            grid=(1,),
            in_specs=[
                pl.BlockSpec((4, 256, 512), lambda i, p: (0, 0, 0)),
                pl.BlockSpec((1, 16, 16, 512), lambda i, p: (p[0], 0, 0, 0)),
                pl.BlockSpec((1, 512), lambda i, p: (0, 0)),
                pl.BlockSpec((CLUSTERS, 512), lambda i, p: (0, 0)),
                pl.BlockSpec((2, 256), lambda i, p: (0, 0)),
            ],
            out_specs=(
                pl.BlockSpec((16 * cap, 512), lambda i, p: (0, 0)),
                pl.BlockSpec((16, 16, 128), lambda i, p: (0, 0, 0)),
            ),
            scratch_shapes=[pltpu.VMEM((256, 128), F32)],
        ),
        cost_estimate=pl.CostEstimate(flops=300_000_000, bytes_accessed=3_000_000, transcendentals=0),
        name="post",
    )(place, parts, residual, gain, topw, gp)


def stack_rows(cap, blocks):
    if cap % 16 == 0:
        return jnp.concatenate(blocks, axis=0)
    return jnp.concatenate([b.astype(F32) for b in blocks], axis=0).astype(BF16)


def leaf_accumulate(cap, pieces, w_ref, acc, sq_acc):
    @pl.when(pl.program_id(0) == 0)
    def _():
        acc[...] = jnp.zeros_like(acc)
        sq_acc[...] = jnp.zeros_like(sq_acc)

    lhs = []
    for c in range(4):
        blocks = [ref[c] for ref in pieces]
        for k, block in enumerate(blocks):
            spare = block[cap - 8:cap].astype(F32)[7:8]
            sq_acc[k:k + 1] += spare[:, 0:128] + spare[:, 128:256] + spare[:, 256:384]
        lhs.append(stack_rows(cap, blocks))
    lhs = jnp.concatenate(lhs, axis=1)
    for first, width in ((0, 2), (2, 2), (4, 1)):
        part = [w_ref[first + k] for k in range(width)]
        rhs = part[0] if width == 1 else jnp.concatenate(part, axis=1)
        acc[:, first * 128:(first + width) * 128] += dot_nn(lhs, rhs)


def leaf_finish(cap, n, place_ref, code_ref, acc, sq_acc, out_ref):
    start = place_ref[n]
    r_i = lax.broadcasted_iota(jnp.int32, (cap, 128), 0)
    c_i = lax.broadcasted_iota(jnp.int32, (cap, 128), 1)
    diag = r_i == c_i
    shifted = r_i + 64 == c_i

    def column(row):
        return jnp.sum(jnp.where(diag, jnp.broadcast_to(row, (cap, 128)), 0.0), axis=1, keepdims=True)

    for k in range(n):
        b = place_ref[k]
        code = column(code_ref[pl.ds(b, 1), :]).astype(jnp.int32)
        local = code >> 10
        target = (code & 1023) - start
        logits = jnp.zeros((cap, 128), F32)
        for j in range(LOCAL):
            logits = jnp.where(local == j, acc[k * cap:(k + 1) * cap, j * 128:(j + 1) * 128], logits)
        logits = logits * lax.rsqrt(column(sq_acc[k:k + 1]) / D + 1e-05)
        peak = jnp.max(logits, axis=1, keepdims=True)
        lse = peak + jnp.log(jnp.sum(jnp.exp(logits - peak), axis=1, keepdims=True))
        hit = jnp.sum(jnp.where(c_i == target, logits, 0.0), axis=1, keepdims=True)
        row = jnp.where(diag, lse, 0.0) + jnp.where(shifted, hit, 0.0)
        out_ref[pl.ds(b, 1), :] = jnp.sum(row, axis=0, keepdims=True)


def top_rows(top_ref, ids):
    total = top_ref[0]
    for k in range(1, 16):
        total = total + top_ref[k]
    lane = lax.broadcasted_iota(jnp.int32, (16, 128), 1)
    row = lax.broadcasted_iota(jnp.int32, (16, 128), 0)
    own_id = jnp.sum(jnp.where(lane == row, jnp.broadcast_to(ids, (16, 128)), 0.0), axis=1, keepdims=True).astype(jnp.int32)
    logits = total * lax.rsqrt(total[:, CLUSTERS:CLUSTERS + 1] / D + 1e-05)
    logits = jnp.where(lane < CLUSTERS, logits, -jnp.inf)
    peak = jnp.max(logits, axis=1, keepdims=True)
    norm = peak + jnp.log(jnp.sum(jnp.exp(logits - peak), axis=1, keepdims=True))
    own = jnp.sum(jnp.where(lane == own_id, logits, 0.0), axis=1, keepdims=True) - norm
    return jnp.where(lane[0:8] == 62, own[0:8], own[8:16])


def near_kernel(cap, place_ref, *refs):
    pieces, (code_ref, w_ref, out_ref, acc, sq_acc) = refs[:6], refs[6:]
    leaf_accumulate(cap, pieces, w_ref, acc, sq_acc)

    @pl.when(pl.program_id(0) == pl.num_programs(0) - 1)
    def _():
        out_ref[...] = jnp.zeros_like(out_ref)
        leaf_finish(cap, 6, place_ref, code_ref, acc, sq_acc, out_ref)


def far_kernel(cap, place_ref, *refs):
    pieces, (code_ref, near_ref, top_ref, w_ref, out_ref, acc, sq_acc, state) = refs[:2], refs[2:]
    leaf_accumulate(cap, pieces, w_ref, acc, sq_acc)

    @pl.when(pl.program_id(0) == pl.num_programs(0) - 1)
    def _():
        state[...] = near_ref[...]
        leaf_finish(cap, 2, place_ref, code_ref, acc, sq_acc, state)
        lane = lax.broadcasted_iota(jnp.int32, (8, 128), 1)
        whole = jnp.where((lane == 62) | (lane == 63), top_rows(top_ref, code_ref[8:9, :]), state[...])
        out_ref[...] = jnp.broadcast_to(whole[None], out_ref.shape)


def leaf_call(cap, kernel, name, out_shape, place, pieces, small, w, scratch):
    n = len(pieces)
    fixed = lambda shape: pl.BlockSpec(shape, lambda c, p: (0,) * len(shape))
    return pl.pallas_call(
        functools.partial(kernel, cap),
        out_shape=jax.ShapeDtypeStruct(out_shape, F32),
        grid_spec=pltpu.PrefetchScalarGridSpec(
            num_scalar_prefetch=1,
            grid=(4,),
            in_specs=[pl.BlockSpec((4, cap, 512), lambda c, p: (c, 0, 0))] * n
            + [fixed(a.shape) for a in small]
            + [pl.BlockSpec((LOCAL, 2048, 128), lambda c, p: (0, c, 0))],
            out_specs=fixed(out_shape),
            scratch_shapes=[pltpu.VMEM((n * cap, LOCAL * 128), F32), pltpu.VMEM((8, 128), F32)] + scratch,
        ),
        cost_estimate=pl.CostEstimate(flops=2 * n * cap * 8192 * 640, bytes_accessed=11_000_000, transcendentals=0),
        name=name,
    )(place, *pieces, *small, w)


def merge_kernel(place_ref, heard_ref, note_ref):
    blocks = [heard_ref[d] for d in range(8)]
    peak = functools.reduce(jnp.maximum, blocks)
    mass = functools.reduce(jnp.add, [jnp.exp(b - peak) for b in blocks])
    picked = functools.reduce(jnp.add, blocks)
    leaf = pltpu.roll(picked, 64, 1) - (peak + jnp.log(mass))
    leaf = jnp.where(place_ref[0] == 0, leaf, jnp.concatenate([leaf[4:8], leaf[0:4]], axis=0))
    note_ref[...] = jnp.broadcast_to(leaf[None], note_ref.shape)


def final_kernel(place_ref, back_ref, heard_ref, gp_ref, out_ref):
    lane = lax.broadcasted_iota(jnp.int32, (16, 128), 1)
    row = lax.broadcasted_iota(jnp.int32, (16, 128), 0)

    def column(at):
        wide = jnp.broadcast_to(gp_ref[at:at + 1, :], (16, 128))
        return jnp.sum(jnp.where(lane == row, wide, 0.0), axis=1, keepdims=True).astype(jnp.int32)

    for s in range(4):
        g = jnp.broadcast_to(column(s), (16, 128))
        at = lane == column(4 + s)
        tops = heard_ref[place_ref[0] * 4 + s]
        found = jnp.where(lane == 62 + (row >> 3), jnp.concatenate([tops, tops], axis=0), 0.0)
        for c in range(16):
            found = found + jnp.where(at & (g == c), back_ref[c, s:s + 1], 0.0)
        total = jnp.sum(found, axis=1, keepdims=True)
        out_ref[s:s + 1, :] = jnp.sum(jnp.where(lane == row, total, 0.0), axis=0, keepdims=True)[:, 0:16]


def small_call(kernel, name, out_shape, *args, smem=0):
    many = isinstance(out_shape[0], tuple)
    shapes = out_shape if many else (out_shape,)
    shapes = tuple(jax.ShapeDtypeStruct(s, F32) for s in shapes)
    return pl.pallas_call(
        kernel,
        out_shape=shapes if many else shapes[0],
        in_specs=[SMEM] * smem + [VMEM] * (len(args) - smem),
        out_specs=(VMEM,) * len(shapes) if many else VMEM,
        name=name,
    )(*args)


def from_cluster(x, dy, dz):
    pairs = []
    for c in range(16):
        pairs.append(((c // 4 + dy) % 4 * 4 + (c % 4 + dz) % 4, c))
    return lax.ppermute(x, "cluster", pairs)


def from_split(x, dy, dz):
    pairs = []
    for c in range(16):
        for r in range(2):
            sign = 1 - 2 * r
            source = (c // 4 + sign * dy) % 4 * 4 + (c % 4 + sign * dz) % 4
            pairs.append((r * 16 + source, r * 16 + c))
    return lax.ppermute(x, ("rows", "cluster"), pairs)


def from_x(x, d):
    return lax.ppermute(x, "head", [((h + d) % 4, h) for h in range(4)])


def swap(x):
    return lax.ppermute(x, "rows", [(0, 1), (1, 0)])


def tail(cap, parts, residual, gain, topw, places, gp, code, gp_rows, leaf_weight):
    place, near_place, far_place, end_place = places
    outgoing, top = post(cap, place, parts, residual, gain, topw, gp)
    own = lax.all_to_all(outgoing.reshape(16, cap, 512), "cluster", 0, 0, tiled=True)
    plus, minus = from_x(own, 1), from_x(own, 3)
    top = lax.all_to_all(top, "cluster", 0, 0, tiled=True)
    plus, minus, top = lax.optimization_barrier((plus, minus, top))
    onward = jnp.where(end_place[0] == 0, plus, minus)
    pairs = [((h + 1) % 4, h) for h in range(4)] + [(4 + (h + 3) % 4, 4 + h) for h in range(4)]
    far = lax.ppermute(onward, ("rows", "head"), pairs)
    near = leaf_call(cap, near_kernel, "near", (8, 128), near_place, [own, plus, minus, swap(own), swap(plus), swap(minus)], [code], leaf_weight, [])
    far, near = lax.optimization_barrier((far, near))
    heard = leaf_call(cap, far_kernel, "far", (8, 8, 128), far_place, [far, swap(far)], [code, near, top], leaf_weight, [pltpu.VMEM((8, 128), F32)])
    heard = lax.all_to_all(heard, ("rows", "head"), 0, 0, tiled=True)
    note = small_call(merge_kernel, "merge", (16, 8, 128), end_place, heard, smem=1)
    back = lax.all_to_all(note, "cluster", 0, 0, tiled=True)
    return small_call(final_kernel, "final", (4, 16), end_place, back, heard, gp_rows, smem=1)


def shards(queries, new_keys, new_values, key_cache, value_cache, lengths, residual_in, out_weight, norm_gain, top_weight, leaf_weight, cluster_ids, targets):
    my_cluster = lax.axis_index("cluster").astype(jnp.int32)
    my_row = lax.axis_index("rows").astype(jnp.int32)
    my_head = lax.axis_index("head").astype(jnp.int32)
    my_y, my_z = my_cluster // SIDE, my_cluster % SIDE

    ids8 = cluster_ids[:, :, 0].reshape(STEPS, 2, 256).transpose(1, 0, 2).reshape(8, 256)
    tg8 = targets.reshape(STEPS, 2, 256).transpose(1, 0, 2).reshape(8, 256)
    g8 = ids8 // LOCAL
    index = jnp.arange(256)
    earlier = (g8[:, :, None] == g8[:, None, :]) & (index[None, None, :] < index[None, :, None])
    p8 = jnp.sum(earlier.astype(jnp.int32), axis=2)
    own_block = my_row * 4 + my_head
    offs = jnp.array(OFFS, jnp.int32)
    major, minor = jnp.repeat(offs, 4), jnp.tile(offs, 4)
    first = my_head < 2
    cabs = ((my_y + jnp.where(first, major, minor)) & 3) * 4 + ((my_z + jnp.where(first, minor, major)) & 3)
    place = jnp.concatenate([my_head[None], cabs])
    own_g = lax.dynamic_index_in_dim(g8, own_block, 0, False).reshape(16, 16)
    own_p = lax.dynamic_index_in_dim(p8, own_block, 0, False).reshape(16, 16)
    gp = jnp.stack([own_g[cabs].reshape(256), own_p[cabs].reshape(256)])
    own_ids = lax.dynamic_slice(ids8, (own_block, my_cluster * 16), (1, 16))
    g_rows = lax.dynamic_slice(g8, (my_row * 4, my_cluster * 16), (4, 16))
    p_rows = lax.dynamic_slice(p8, (my_row * 4, my_cluster * 16), (4, 16))
    gp_rows = jnp.pad(jnp.concatenate([g_rows, p_rows]), ((0, 0), (0, 112))).astype(F32)
    land = (g8 == my_cluster)[:, None, :] & (p8[:, None, :] == jnp.arange(128)[None, :, None])
    value = (ids8 % LOCAL * 1024 + tg8).astype(F32)
    code = jnp.sum(jnp.where(land, value[:, None, :], 0.0), axis=2)
    code = jnp.concatenate([code, jnp.pad(own_ids, ((0, 7), (0, 112))).astype(F32)])
    block = lambda flip, d: (my_row ^ flip) * 4 + ((my_head + d) & 3)
    start = (my_row * 4 + my_head) * LEAF_COLS
    near_place = jnp.stack([block(0, 0), block(0, 1), block(0, 3), block(1, 0), block(1, 1), block(1, 3), start])
    far_place = jnp.stack([block(0, 2), block(1, 2), start])
    end_place = jnp.stack([my_row, my_cluster])
    fits = jnp.max(p8) < SMALL - 1
    places = (place, near_place, far_place, end_place)
    places, gp, code, gp_rows, fits = lax.optimization_barrier((places, gp, code, gp_rows, fits))

    att_a, att_b = attend(lengths, queries, new_keys, new_values, key_cache, value_cache)
    za = jnp.stack([att_a] + [from_cluster(att_a, 0, d) for d in OFFS[1:]])
    yb = jnp.stack([att_b] + [from_cluster(att_b, d, 0) for d in OFFS[1:]])
    a1, a3 = from_cluster(za, 1, 0), from_cluster(za, 3, 0)
    b1, b3 = from_cluster(yb, 0, 1), from_cluster(yb, 0, 3)
    a2 = from_split(jnp.where(my_row == 0, a1, a3), 1, 0)
    b2 = from_split(jnp.where(my_row == 0, b1, b3), 0, 1)
    sums = project_near([za, a1, a3, yb, b1, b3], out_weight)
    sums = project_far(a2, b2, sums, out_weight)
    parts = lax.all_to_all(sums, "head", 0, 0, tiled=True)

    args = (parts, residual_in.reshape(4, 16, 16, 512), norm_gain[None, :], top_weight.T, places, gp, code, gp_rows, leaf_weight)
    return lax.cond(fits, functools.partial(tail, SMALL), functools.partial(tail, FULL), *args)


def solution(mesh):
    placed = (
        P(None, ("rows", "cluster"), "head"),
        P(None, ("rows", "cluster"), "head"),
        P(None, ("rows", "cluster"), "head"),
        P(("rows", "cluster"), "head", None, None),
        P(("rows", "cluster"), "head", None, None),
        P(("rows", "cluster")),
        P(None, "rows", "cluster"),
        P("head", "cluster"),
        P("cluster"),
        P("cluster", None),
        P("cluster", None, ("rows", "head")),
        P(),
        P(),
    )
    return jax.shard_map(
        shards, mesh=mesh, in_specs=placed, out_specs=P(None, ("rows", "cluster")), check_vma=False
    )
```

```python
import functools
import jax
import jax.numpy as jnp
from jax import lax
from jax.experimental import pallas as pl
from jax.experimental.pallas import tpu as pltpu
from jax.sharding import PartitionSpec as P


D = 8192
CLUSTERS = 80
STEPS = 4
LOCAL = 5
LEAF_COLS = 128
SIDE = 4
OFFS = (0, 1, 3, 2)
SIZES = (32, 40, 64)
F32 = jnp.float32
BF16 = jnp.bfloat16
VMEM = pl.BlockSpec(memory_space=pltpu.VMEM)
SMEM = pl.BlockSpec(memory_space=pltpu.SMEM)


def dot_nt(a, b):
    return lax.dot_general(a, b, (((1,), (1,)), ((), ())), preferred_element_type=F32)


def dot_nn(a, b):
    return lax.dot_general(a, b, (((1,), (0,)), ((), ())), preferred_element_type=F32)


def attend_kernel(len_ref, q_ref, nk_ref, nv_ref, k_ref, v_ref, oa_ref, ob_ref, q_scr, o_scr, q2_scr, o2_scr):
    step = pl.program_id(0)
    heads = 16
    scale = 128 ** (-0.5)

    @pl.when(step == 0)
    def _():
        for head in range(heads):
            part = q_ref[:, :, head * 128:(head + 1) * 128]
            q_scr[head] = part.reshape(64, 128).astype(F32)

    row0 = step * 4
    m_col = lax.broadcasted_iota(jnp.int32, (128, 64), 0)
    n_row = lax.broadcasted_iota(jnp.int32, (128, 64), 1)
    recent_ok = ((n_row & 15) == row0 + (m_col >> 5)) & ((n_row >> 4) <= (m_col & 3))
    lane = lax.broadcasted_iota(jnp.int32, (32, 256), 1)
    for kv in range(2):
        for rr in range(4):
            for g in range(8):
                q2_scr[kv, rr * 32 + g * 4:rr * 32 + g * 4 + 4, :] = q_scr[kv * 8 + g, pl.ds(row0 + rr, 4, stride=16), :]
        q2 = q2_scr[kv].astype(BF16)
        cached = []
        for rr in range(4):
            s = dot_nt(q2[rr * 32:(rr + 1) * 32], k_ref[rr, kv]) * scale
            cached.append(jnp.where(lane < len_ref[row0 + rr], s, -jnp.inf))
        cached = jnp.concatenate(cached, axis=0)
        nk = nk_ref[:, :, kv * 128:(kv + 1) * 128].reshape(64, 128)
        nv = nv_ref[:, :, kv * 128:(kv + 1) * 128].reshape(64, 128)
        recent = jnp.where(recent_ok, dot_nt(q2, nk) * scale, -jnp.inf)
        peak = jnp.maximum(jnp.max(cached, axis=1, keepdims=True), jnp.max(recent, axis=1, keepdims=True))
        ec = jnp.exp(cached - peak)
        er = jnp.exp(recent - peak)
        inv = 1.0 / (jnp.sum(ec, axis=1, keepdims=True) + jnp.sum(er, axis=1, keepdims=True))
        wc = (ec * inv).astype(BF16)
        wr = (er * inv).astype(BF16)
        out = []
        for rr in range(4):
            out.append(dot_nn(wc[rr * 32:(rr + 1) * 32], v_ref[rr, kv]))
        o2_scr[kv] = jnp.concatenate(out, axis=0) + dot_nn(wr, nv)
        for rr in range(4):
            for g in range(8):
                o_scr[kv * 8 + g, pl.ds(row0 + rr, 4, stride=16), :] = o2_scr[kv, rr * 32 + g * 4:rr * 32 + g * 4 + 4, :]

    @pl.when(step == pl.num_programs(0) - 1)
    def _():
        for head in range(heads):
            cols = slice(head * 128, (head + 1) * 128)
            oa_ref[:, :, cols] = o_scr[head, 0:32].reshape(2, 16, 128).astype(BF16)
            ob_ref[:, :, cols] = o_scr[head, 32:64].reshape(2, 16, 128).astype(BF16)


def attend(lengths, q, nk, nv, k, v):
    whole = lambda shape: pl.BlockSpec(shape, lambda i, *_: (0,) * len(shape))
    block = pl.BlockSpec((4, 2, 256, 128), lambda i, *_: (i, 0, 0, 0))
    return pl.pallas_call(
        attend_kernel,
        out_shape=(jax.ShapeDtypeStruct((2, 16, 2048), BF16),) * 2,
        grid_spec=pltpu.PrefetchScalarGridSpec(
            num_scalar_prefetch=1,
            grid=(4,),
            in_specs=[whole((4, 16, 2048)), whole((4, 16, 256)), whole((4, 16, 256)), block, block],
            out_specs=(whole((2, 16, 2048)),) * 2,
            scratch_shapes=[
                pltpu.VMEM((16, 64, 128), F32),
                pltpu.VMEM((16, 64, 128), F32),
                pltpu.VMEM((2, 128, 128), F32),
                pltpu.VMEM((2, 128, 128), F32),
            ],
        ),
        cost_estimate=pl.CostEstimate(flops=300_000_000, bytes_accessed=5_000_000, transcendentals=400_000),
        name="attend",
    )(lengths, q, nk, nv, k, v)


def project_near_kernel(*refs):
    pieces = (refs[0:3], refs[3:6])
    w_ref, out_ref, lhs = refs[6:]
    for s in range(4):
        for i in range(3):
            for j in range(4):
                at = s * 192 + (i * 4 + j) * 16
                lhs[at:at + 16, :] = pieces[s // 2][i][j, s % 2]
    for n in range(2):
        cols = slice(n * 256, (n + 1) * 256)
        rows = dot_nn(lhs[...], w_ref[:, cols]).astype(BF16)
        for s in range(4):
            out_ref[s, :, cols] = rows[s * 192:(s + 1) * 192]


def project_far_kernel(place_ref, a_ref, b_ref, near_ref, w_ref, *refs):
    outs, (lhs, all_rows) = refs[:4], refs[4:]
    for s in range(4):
        for j in range(4):
            lhs[s * 64 + j * 16:s * 64 + (j + 1) * 16, :] = (a_ref, b_ref)[s // 2][j, s % 2]
    for n in range(2):
        cols = slice(n * 256, (n + 1) * 256)
        rows = dot_nn(lhs[...], w_ref[:, cols]).astype(BF16)
        for s in range(4):
            all_rows[s, :, cols] = rows[s * 64:(s + 1) * 64]
    for out, d in zip(outs, OFFS):
        s = (place_ref[0] + d) & 3
        out[0:192, :] = near_ref[s]
        out[192:256, :] = all_rows[s]


def project_near(blocks, w):
    return pl.pallas_call(
        project_near_kernel,
        out_shape=jax.ShapeDtypeStruct((4, 192, 512), BF16),
        in_specs=[VMEM] * 7,
        out_specs=VMEM,
        scratch_shapes=[pltpu.VMEM((768, 2048), BF16)],
        cost_estimate=pl.CostEstimate(flops=1_600_000_000, bytes_accessed=6_000_000, transcendentals=0),
        name="project_near",
    )(*blocks, w)


def project_far(place, a, b, near, w):
    return pl.pallas_call(
        project_far_kernel,
        out_shape=(jax.ShapeDtypeStruct((256, 512), BF16),) * 4,
        in_specs=[SMEM] + [VMEM] * 4,
        out_specs=(VMEM,) * 4,
        scratch_shapes=[pltpu.VMEM((256, 2048), BF16), pltpu.VMEM((4, 64, 512), BF16)],
        cost_estimate=pl.CostEstimate(flops=540_000_000, bytes_accessed=4_000_000, transcendentals=0),
        name="project_far",
    )(place, a, b, near, w)


def post_kernel(cap, place_ref, pa_ref, pb_ref, pc_ref, pd_ref, res_ref, gain_ref, topw_ref, gp_ref, out_ref, top_ref, top_scr):
    res = jnp.concatenate([res_ref[0, place_ref[k + 1]] for k in range(16)], axis=0).astype(F32)
    mixed = (pa_ref[...].astype(F32) + pb_ref[...].astype(F32)) + (pc_ref[...].astype(F32) + pd_ref[...].astype(F32))
    hidden = mixed + res
    squares = jnp.sum(hidden * hidden, axis=1, keepdims=True)
    gated = (hidden * gain_ref[...]).astype(BF16)
    wide = jnp.broadcast_to(squares, (256, 128))
    top_scr[...] = wide
    top_scr[:, 0:CLUSTERS] = dot_nt(gated, topw_ref[...])
    for k in range(16):
        top_ref[place_ref[k + 1]] = top_scr[k * 16:(k + 1) * 16]
    dest = gp_ref[0:1, :]
    rank = gp_ref[1:2, :]
    rows = lax.broadcasted_iota(jnp.int32, (16, 256), 0)
    sq_row = wide.T[0:16]
    spread = jnp.where(rows == dest, sq_row, 0.0)
    hi = spread.astype(BF16)
    rest = spread - hi.astype(F32)
    mid = rest.astype(BF16)
    low = (rest - mid.astype(F32)).astype(BF16)
    by_rank = (lax.broadcasted_iota(jnp.int32, (128, 256), 0) == rank).astype(F32).astype(BF16)
    code = jnp.concatenate([dot_nt(hi, by_rank), dot_nt(mid, by_rank), dot_nt(low, by_rank), jnp.zeros((16, 128), F32)], axis=1).astype(BF16)
    slot = dest * cap + rank
    pick = (lax.broadcasted_iota(jnp.int32, (16 * cap, 256), 0) == slot).astype(F32).astype(BF16)
    srow = lax.broadcasted_iota(jnp.int32, (16 * cap, 16), 0)
    scol = lax.broadcasted_iota(jnp.int32, (16 * cap, 16), 1)
    last = (srow == scol * cap + cap - 1).astype(F32).astype(BF16)
    out_ref[...] = (dot_nn(pick, gated) + dot_nn(last, code)).astype(BF16)


def post(cap, place, parts, residual, gain, topw, gp):
    return pl.pallas_call(
        functools.partial(post_kernel, cap),
        out_shape=(jax.ShapeDtypeStruct((16 * cap, 512), BF16), jax.ShapeDtypeStruct((16, 16, 128), F32)),
        grid_spec=pltpu.PrefetchScalarGridSpec(
            num_scalar_prefetch=1,
            grid=(1,),
            in_specs=[
                *[pl.BlockSpec((256, 512), lambda i, p: (0, 0))] * 4,
                pl.BlockSpec((1, 16, 16, 512), lambda i, p: (p[0], 0, 0, 0)),
                pl.BlockSpec((1, 512), lambda i, p: (0, 0)),
                pl.BlockSpec((CLUSTERS, 512), lambda i, p: (0, 0)),
                pl.BlockSpec((2, 256), lambda i, p: (0, 0)),
            ],
            out_specs=(
                pl.BlockSpec((16 * cap, 512), lambda i, p: (0, 0)),
                pl.BlockSpec((16, 16, 128), lambda i, p: (0, 0, 0)),
            ),
            scratch_shapes=[pltpu.VMEM((256, 128), F32)],
        ),
        cost_estimate=pl.CostEstimate(flops=300_000_000, bytes_accessed=3_000_000, transcendentals=0),
        name="post",
    )(place, *parts, residual, gain, topw, gp)


def stack_rows(cap, blocks):
    if cap % 16 == 0:
        return jnp.concatenate(blocks, axis=0)
    return jnp.concatenate([b.astype(F32) for b in blocks], axis=0).astype(BF16)


def leaf_accumulate(cap, pieces, w_ref, acc, sq_acc):
    @pl.when(pl.program_id(0) == 0)
    def _():
        acc[...] = jnp.zeros_like(acc)
        sq_acc[...] = jnp.zeros_like(sq_acc)

    lhs = []
    for c in range(4):
        blocks = [ref[c] for ref in pieces]
        for k, block in enumerate(blocks):
            spare = block[cap - 8:cap].astype(F32)[7:8]
            sq_acc[k:k + 1] += spare[:, 0:128] + spare[:, 128:256] + spare[:, 256:384]
        lhs.append(stack_rows(cap, blocks))
    lhs = jnp.concatenate(lhs, axis=1)
    for first, width in ((0, 2), (2, 2), (4, 1)):
        part = [w_ref[first + k] for k in range(width)]
        rhs = part[0] if width == 1 else jnp.concatenate(part, axis=1)
        acc[:, first * 128:(first + width) * 128] += dot_nn(lhs, rhs)


def leaf_finish(cap, n, place_ref, code_ref, acc, sq_acc, out_ref):
    start = place_ref[n]
    r_i = lax.broadcasted_iota(jnp.int32, (cap, 128), 0)
    c_i = lax.broadcasted_iota(jnp.int32, (cap, 128), 1)
    diag = r_i == c_i
    shifted = r_i + 64 == c_i

    def column(row):
        return jnp.sum(jnp.where(diag, jnp.broadcast_to(row, (cap, 128)), 0.0), axis=1, keepdims=True)

    for k in range(n):
        b = place_ref[k]
        code = column(code_ref[pl.ds(b, 1), :]).astype(jnp.int32)
        local = code >> 10
        target = (code & 1023) - start
        logits = jnp.zeros((cap, 128), F32)
        for j in range(LOCAL):
            logits = jnp.where(local == j, acc[k * cap:(k + 1) * cap, j * 128:(j + 1) * 128], logits)
        logits = logits * lax.rsqrt(column(sq_acc[k:k + 1]) / D + 1e-05)
        peak = jnp.max(logits, axis=1, keepdims=True)
        lse = peak + jnp.log(jnp.sum(jnp.exp(logits - peak), axis=1, keepdims=True))
        hit = jnp.sum(jnp.where(c_i == target, logits, 0.0), axis=1, keepdims=True)
        row = jnp.where(diag, lse, 0.0) + jnp.where(shifted, hit, 0.0)
        out_ref[pl.ds(b, 1), :] = jnp.sum(row, axis=0, keepdims=True)


def top_rows(top_ref, ids):
    total = top_ref[0]
    for k in range(1, 16):
        total = total + top_ref[k]
    lane = lax.broadcasted_iota(jnp.int32, (16, 128), 1)
    row = lax.broadcasted_iota(jnp.int32, (16, 128), 0)
    own_id = jnp.sum(jnp.where(lane == row, jnp.broadcast_to(ids, (16, 128)), 0.0), axis=1, keepdims=True).astype(jnp.int32)
    logits = total * lax.rsqrt(total[:, CLUSTERS:CLUSTERS + 1] / D + 1e-05)
    logits = jnp.where(lane < CLUSTERS, logits, -jnp.inf)
    peak = jnp.max(logits, axis=1, keepdims=True)
    norm = peak + jnp.log(jnp.sum(jnp.exp(logits - peak), axis=1, keepdims=True))
    own = jnp.sum(jnp.where(lane == own_id, logits, 0.0), axis=1, keepdims=True) - norm
    return jnp.where(lane[0:8] == 62, own[0:8], own[8:16])


def near_kernel(cap, place_ref, *refs):
    pieces, (code_ref, w_ref, out_ref, acc, sq_acc) = refs[:6], refs[6:]
    leaf_accumulate(cap, pieces, w_ref, acc, sq_acc)

    @pl.when(pl.program_id(0) == pl.num_programs(0) - 1)
    def _():
        out_ref[...] = jnp.zeros_like(out_ref)
        leaf_finish(cap, 6, place_ref, code_ref, acc, sq_acc, out_ref)


def far_kernel(cap, place_ref, *refs):
    pieces, (code_ref, near_ref, top_ref, w_ref, out_ref, acc, sq_acc, state) = refs[:2], refs[2:]
    leaf_accumulate(cap, pieces, w_ref, acc, sq_acc)

    @pl.when(pl.program_id(0) == pl.num_programs(0) - 1)
    def _():
        state[...] = near_ref[...]
        leaf_finish(cap, 2, place_ref, code_ref, acc, sq_acc, state)
        lane = lax.broadcasted_iota(jnp.int32, (8, 128), 1)
        whole = jnp.where((lane == 62) | (lane == 63), top_rows(top_ref, code_ref[8:9, :]), state[...])
        out_ref[...] = jnp.broadcast_to(whole[None], out_ref.shape)


def leaf_call(cap, kernel, name, out_shape, place, pieces, small, w, scratch):
    n = len(pieces)
    fixed = lambda shape: pl.BlockSpec(shape, lambda c, p: (0,) * len(shape))
    return pl.pallas_call(
        functools.partial(kernel, cap),
        out_shape=jax.ShapeDtypeStruct(out_shape, F32),
        grid_spec=pltpu.PrefetchScalarGridSpec(
            num_scalar_prefetch=1,
            grid=(4,),
            in_specs=[pl.BlockSpec((4, cap, 512), lambda c, p: (c, 0, 0))] * n
            + [fixed(a.shape) for a in small]
            + [pl.BlockSpec((LOCAL, 2048, 128), lambda c, p: (0, c, 0))],
            out_specs=fixed(out_shape),
            scratch_shapes=[pltpu.VMEM((n * cap, LOCAL * 128), F32), pltpu.VMEM((8, 128), F32)] + scratch,
        ),
        cost_estimate=pl.CostEstimate(flops=2 * n * cap * 8192 * 640, bytes_accessed=11_000_000, transcendentals=0),
        name=name,
    )(place, *pieces, *small, w)


def merge_kernel(place_ref, heard_ref, note_ref):
    blocks = [heard_ref[d] for d in range(8)]
    peak = functools.reduce(jnp.maximum, blocks)
    mass = functools.reduce(jnp.add, [jnp.exp(b - peak) for b in blocks])
    picked = functools.reduce(jnp.add, blocks)
    leaf = pltpu.roll(picked, 64, 1) - (peak + jnp.log(mass))
    leaf = jnp.where(place_ref[0] == 0, leaf, jnp.concatenate([leaf[4:8], leaf[0:4]], axis=0))
    note_ref[...] = jnp.broadcast_to(leaf[None], note_ref.shape)


def final_kernel(place_ref, back_ref, heard_ref, gp_ref, out_ref):
    lane = lax.broadcasted_iota(jnp.int32, (16, 128), 1)
    row = lax.broadcasted_iota(jnp.int32, (16, 128), 0)

    def column(at):
        wide = jnp.broadcast_to(gp_ref[at:at + 1, :], (16, 128))
        return jnp.sum(jnp.where(lane == row, wide, 0.0), axis=1, keepdims=True).astype(jnp.int32)

    for s in range(4):
        g = jnp.broadcast_to(column(s), (16, 128))
        at = lane == column(4 + s)
        tops = heard_ref[place_ref[0] * 4 + s]
        found = jnp.where(lane == 62 + (row >> 3), jnp.concatenate([tops, tops], axis=0), 0.0)
        for c in range(16):
            found = found + jnp.where(at & (g == c), back_ref[c, s:s + 1], 0.0)
        total = jnp.sum(found, axis=1, keepdims=True)
        out_ref[s:s + 1, :] = jnp.sum(jnp.where(lane == row, total, 0.0), axis=0, keepdims=True)[:, 0:16]


def small_call(kernel, name, out_shape, *args, smem=0):
    many = isinstance(out_shape[0], tuple)
    shapes = out_shape if many else (out_shape,)
    shapes = tuple(jax.ShapeDtypeStruct(s, F32) for s in shapes)
    return pl.pallas_call(
        kernel,
        out_shape=shapes if many else shapes[0],
        in_specs=[SMEM] * smem + [VMEM] * (len(args) - smem),
        out_specs=(VMEM,) * len(shapes) if many else VMEM,
        name=name,
    )(*args)


def from_cluster(x, dy, dz):
    pairs = []
    for c in range(16):
        pairs.append(((c // 4 + dy) % 4 * 4 + (c % 4 + dz) % 4, c))
    return lax.ppermute(x, "cluster", pairs)


def from_split(x, dy, dz):
    pairs = []
    for c in range(16):
        for r in range(2):
            sign = 1 - 2 * r
            source = (c // 4 + sign * dy) % 4 * 4 + (c % 4 + sign * dz) % 4
            pairs.append((r * 16 + source, r * 16 + c))
    return lax.ppermute(x, ("rows", "cluster"), pairs)


def from_split_x(x, d):
    pairs = [(r * 4 + (h + (1 - 2 * r) * d) % 4, r * 4 + h) for r in range(2) for h in range(4)]
    return lax.ppermute(x, ("rows", "head"), pairs)


def to_x(x, d):
    return lax.ppermute(x, "head", [(h, (h + d) % 4) for h in range(4)])


def swap(x):
    return lax.ppermute(x, "rows", [(0, 1), (1, 0)])


def tail(cap, parts, residual, gain, topw, places, gp, code, gp_rows, leaf_weight):
    place, near_place, far_place, end_place = places
    outgoing, top = post(cap, place, parts, residual, gain, topw, gp)
    own = lax.all_to_all(outgoing.reshape(16, cap, 512), "cluster", 0, 0, tiled=True)
    first, second = from_split_x(own, 1), from_split_x(own, 3)
    top = lax.all_to_all(top, "cluster", 0, 0, tiled=True)
    first, second, top = lax.optimization_barrier((first, second, top))
    far = from_split_x(first, 1)
    near = leaf_call(cap, near_kernel, "near", (8, 128), near_place, [own, first, second, swap(own), swap(first), swap(second)], [code], leaf_weight, [])
    far, near = lax.optimization_barrier((far, near))
    heard = leaf_call(cap, far_kernel, "far", (8, 8, 128), far_place, [far, swap(far)], [code, near, top], leaf_weight, [pltpu.VMEM((8, 128), F32)])
    heard = lax.all_to_all(heard, ("rows", "head"), 0, 0, tiled=True)
    note = small_call(merge_kernel, "merge", (16, 8, 128), end_place, heard, smem=1)
    back = lax.all_to_all(note, "cluster", 0, 0, tiled=True)
    return small_call(final_kernel, "final", (4, 16), end_place, back, heard, gp_rows, smem=1)


def shards(queries, new_keys, new_values, key_cache, value_cache, lengths, residual_in, out_weight, norm_gain, top_weight, leaf_weight, cluster_ids, targets):
    my_cluster = lax.axis_index("cluster").astype(jnp.int32)
    my_row = lax.axis_index("rows").astype(jnp.int32)
    my_head = lax.axis_index("head").astype(jnp.int32)
    my_y, my_z = my_cluster // SIDE, my_cluster % SIDE

    ids8 = cluster_ids[:, :, 0].reshape(STEPS, 2, 256).transpose(1, 0, 2).reshape(8, 256)
    tg8 = targets.reshape(STEPS, 2, 256).transpose(1, 0, 2).reshape(8, 256)
    g8 = ids8 // LOCAL
    index = jnp.arange(256)
    earlier = (g8[:, :, None] == g8[:, None, :]) & (index[None, None, :] < index[None, :, None])
    p8 = jnp.sum(earlier.astype(jnp.int32), axis=2)
    own_block = my_row * 4 + my_head
    sign = 1 - 2 * my_row
    offs = jnp.array(OFFS, jnp.int32)
    major, minor = jnp.repeat(offs * sign, 4), jnp.tile(offs, 4)
    first = my_head < 2
    cabs = ((my_y + jnp.where(first, major, minor)) & 3) * 4 + ((my_z + jnp.where(first, minor, major)) & 3)
    place = jnp.concatenate([my_head[None], cabs])
    own_g = lax.dynamic_index_in_dim(g8, own_block, 0, False).reshape(16, 16)
    own_p = lax.dynamic_index_in_dim(p8, own_block, 0, False).reshape(16, 16)
    gp = jnp.stack([own_g[cabs].reshape(256), own_p[cabs].reshape(256)])
    own_ids = lax.dynamic_slice(ids8, (own_block, my_cluster * 16), (1, 16))
    g_rows = lax.dynamic_slice(g8, (my_row * 4, my_cluster * 16), (4, 16))
    p_rows = lax.dynamic_slice(p8, (my_row * 4, my_cluster * 16), (4, 16))
    gp_rows = jnp.pad(jnp.concatenate([g_rows, p_rows]), ((0, 0), (0, 112))).astype(F32)
    land = (g8 == my_cluster)[:, None, :] & (p8[:, None, :] == jnp.arange(128)[None, :, None])
    value = (ids8 % LOCAL * 1024 + tg8).astype(F32)
    code = jnp.sum(jnp.where(land, value[:, None, :], 0.0), axis=2)
    code = jnp.concatenate([code, jnp.pad(own_ids, ((0, 7), (0, 112))).astype(F32)])
    block = lambda flip, d: (my_row ^ flip) * 4 + ((my_head + d) & 3)
    start = (my_row * 4 + my_head) * LEAF_COLS
    near_place = jnp.stack([block(0, 0), block(0, sign), block(0, -sign), block(1, 0), block(1, -sign), block(1, sign), start])
    far_place = jnp.stack([block(0, 2), block(1, 2), start])
    end_place = jnp.stack([my_row, my_cluster])
    load = jnp.max(p8)
    level = sum((load >= size - 1).astype(jnp.int32) for size in SIZES[:-1])
    places = (place, near_place, far_place, end_place)
    places, gp, code, gp_rows, level = lax.optimization_barrier((places, gp, code, gp_rows, level))

    att_a, att_b = attend(lengths, queries, new_keys, new_values, key_cache, value_cache)
    za = jnp.stack([att_a] + [from_cluster(att_a, 0, d) for d in OFFS[1:]])
    yb = jnp.stack([att_b] + [from_cluster(att_b, d, 0) for d in OFFS[1:]])
    a1, a3 = from_split(za, 1, 0), from_split(za, 3, 0)
    b1, b3 = from_split(yb, 0, 1), from_split(yb, 0, 3)
    a2, b2 = from_split(a1, 1, 0), from_split(b1, 0, 1)
    sums = project_near([za, a1, a3, yb, b1, b3], out_weight)
    sums = project_far(place, a2, b2, sums, out_weight)
    parts = [sums[0]] + [to_x(sums[k], OFFS[k]) for k in (1, 2, 3)]

    args = (parts, residual_in.reshape(4, 16, 16, 512), norm_gain[None, :], top_weight.T, places, gp, code, gp_rows, leaf_weight)
    return lax.switch(level, [functools.partial(tail, size) for size in SIZES], *args)


def solution(mesh):
    placed = (
        P(None, ("rows", "cluster"), "head"),
        P(None, ("rows", "cluster"), "head"),
        P(None, ("rows", "cluster"), "head"),
        P(("rows", "cluster"), "head", None, None),
        P(("rows", "cluster"), "head", None, None),
        P(("rows", "cluster")),
        P(None, "rows", "cluster"),
        P("head", "cluster"),
        P("cluster"),
        P("cluster", None),
        P("cluster", None, ("rows", "head")),
        P(),
        P(),
    )
    return jax.shard_map(
        shards, mesh=mesh, in_specs=placed, out_specs=P(None, ("rows", "cluster")), check_vma=False
    )
```

```python
import functools
import jax
import jax.numpy as jnp
from jax import lax
from jax.experimental import pallas as pl
from jax.experimental.pallas import tpu as pltpu
from jax.sharding import PartitionSpec as P


D = 8192
CLUSTERS = 80
STEPS = 4
LOCAL = 5
LEAF_COLS = 128
SIDE = 4
OFFS = (0, 1, 3, 2)
SIZES = (32, 40, 64)
F32 = jnp.float32
BF16 = jnp.bfloat16
VMEM = pl.BlockSpec(memory_space=pltpu.VMEM)
SMEM = pl.BlockSpec(memory_space=pltpu.SMEM)


def dot_nt(a, b):
    return lax.dot_general(a, b, (((1,), (1,)), ((), ())), preferred_element_type=F32)


def dot_nn(a, b):
    return lax.dot_general(a, b, (((1,), (0,)), ((), ())), preferred_element_type=F32)


def attend_kernel(len_ref, q_ref, nk_ref, nv_ref, k_ref, v_ref, oa_ref, ob_ref, q_scr, o_scr, q2_scr, o2_scr):
    step = pl.program_id(0)
    heads = 16
    scale = 128 ** (-0.5)

    @pl.when(step == 0)
    def _():
        for head in range(heads):
            part = q_ref[:, :, head * 128:(head + 1) * 128]
            q_scr[head] = part.reshape(64, 128).astype(F32)

    row0 = step * 4
    m_col = lax.broadcasted_iota(jnp.int32, (128, 64), 0)
    n_row = lax.broadcasted_iota(jnp.int32, (128, 64), 1)
    recent_ok = ((n_row & 15) == row0 + (m_col >> 5)) & ((n_row >> 4) <= (m_col & 3))
    lane = lax.broadcasted_iota(jnp.int32, (32, 256), 1)
    for kv in range(2):
        for rr in range(4):
            for g in range(8):
                q2_scr[kv, rr * 32 + g * 4:rr * 32 + g * 4 + 4, :] = q_scr[kv * 8 + g, pl.ds(row0 + rr, 4, stride=16), :]
        q2 = q2_scr[kv].astype(BF16)
        cached = []
        for rr in range(4):
            s = dot_nt(q2[rr * 32:(rr + 1) * 32], k_ref[rr, kv]) * scale
            cached.append(jnp.where(lane < len_ref[row0 + rr], s, -jnp.inf))
        cached = jnp.concatenate(cached, axis=0)
        nk = nk_ref[:, :, kv * 128:(kv + 1) * 128].reshape(64, 128)
        nv = nv_ref[:, :, kv * 128:(kv + 1) * 128].reshape(64, 128)
        recent = jnp.where(recent_ok, dot_nt(q2, nk) * scale, -jnp.inf)
        peak = jnp.maximum(jnp.max(cached, axis=1, keepdims=True), jnp.max(recent, axis=1, keepdims=True))
        ec = jnp.exp(cached - peak)
        er = jnp.exp(recent - peak)
        inv = 1.0 / (jnp.sum(ec, axis=1, keepdims=True) + jnp.sum(er, axis=1, keepdims=True))
        wc = (ec * inv).astype(BF16)
        wr = (er * inv).astype(BF16)
        out = []
        for rr in range(4):
            out.append(dot_nn(wc[rr * 32:(rr + 1) * 32], v_ref[rr, kv]))
        o2_scr[kv] = jnp.concatenate(out, axis=0) + dot_nn(wr, nv)
        for rr in range(4):
            for g in range(8):
                o_scr[kv * 8 + g, pl.ds(row0 + rr, 4, stride=16), :] = o2_scr[kv, rr * 32 + g * 4:rr * 32 + g * 4 + 4, :]

    @pl.when(step == pl.num_programs(0) - 1)
    def _():
        for head in range(heads):
            cols = slice(head * 128, (head + 1) * 128)
            oa_ref[:, :, cols] = o_scr[head, 0:32].reshape(2, 16, 128).astype(BF16)
            ob_ref[:, :, cols] = o_scr[head, 32:64].reshape(2, 16, 128).astype(BF16)


def attend(lengths, q, nk, nv, k, v):
    whole = lambda shape: pl.BlockSpec(shape, lambda i, *_: (0,) * len(shape))
    block = pl.BlockSpec((4, 2, 256, 128), lambda i, *_: (i, 0, 0, 0))
    return pl.pallas_call(
        attend_kernel,
        out_shape=(jax.ShapeDtypeStruct((2, 16, 2048), BF16),) * 2,
        grid_spec=pltpu.PrefetchScalarGridSpec(
            num_scalar_prefetch=1,
            grid=(4,),
            in_specs=[whole((4, 16, 2048)), whole((4, 16, 256)), whole((4, 16, 256)), block, block],
            out_specs=(whole((2, 16, 2048)),) * 2,
            scratch_shapes=[
                pltpu.VMEM((16, 64, 128), F32),
                pltpu.VMEM((16, 64, 128), F32),
                pltpu.VMEM((2, 128, 128), F32),
                pltpu.VMEM((2, 128, 128), F32),
            ],
        ),
        cost_estimate=pl.CostEstimate(flops=300_000_000, bytes_accessed=5_000_000, transcendentals=400_000),
        name="attend",
    )(lengths, q, nk, nv, k, v)


def project_rows(pieces, lhs, w_ref, store):
    for s in range(4):
        for i in range(2):
            for j in range(4):
                at = s * 128 + (i * 4 + j) * 16
                lhs[at:at + 16, :] = pieces[s // 2][i][j, s % 2]
    for n in range(2):
        cols = slice(n * 256, (n + 1) * 256)
        rows = dot_nn(lhs[...], w_ref[:, cols]).astype(BF16)
        for s in range(4):
            store[s, :, cols] = rows[s * 128:(s + 1) * 128]


def project_near_kernel(a0, a1, b0, b1, w_ref, out_ref, lhs):
    project_rows(((a0, a1), (b0, b1)), lhs, w_ref, out_ref)


def project_far_kernel(place_ref, a2, a3, b2, b3, near_ref, w_ref, *refs):
    outs, (lhs, all_rows) = refs[:4], refs[4:]
    project_rows(((a2, a3), (b2, b3)), lhs, w_ref, all_rows)
    for out, d in zip(outs, OFFS):
        s = (place_ref[0] + d) & 3
        out[0:128, :] = near_ref[s]
        out[128:256, :] = all_rows[s]


PROJECT_COST = pl.CostEstimate(flops=1_100_000_000, bytes_accessed=6_000_000, transcendentals=0)


def project_near(pieces, w):
    return pl.pallas_call(
        project_near_kernel,
        out_shape=jax.ShapeDtypeStruct((4, 128, 512), BF16),
        in_specs=[VMEM] * 5,
        out_specs=VMEM,
        scratch_shapes=[pltpu.VMEM((512, 2048), BF16)],
        cost_estimate=PROJECT_COST,
        name="project_near",
    )(*pieces, w)


def project_far(place, pieces, near, w):
    return pl.pallas_call(
        project_far_kernel,
        out_shape=(jax.ShapeDtypeStruct((256, 512), BF16),) * 4,
        in_specs=[SMEM] + [VMEM] * 6,
        out_specs=(VMEM,) * 4,
        scratch_shapes=[pltpu.VMEM((512, 2048), BF16), pltpu.VMEM((4, 128, 512), BF16)],
        cost_estimate=PROJECT_COST,
        name="project_far",
    )(place, *pieces, near, w)


def post_kernel(cap, place_ref, pa_ref, pb_ref, pc_ref, pd_ref, res_ref, gain_ref, topw_ref, gp_ref, out_ref, top_ref, top_scr):
    res = jnp.concatenate([res_ref[0, place_ref[k + 1]] for k in range(16)], axis=0).astype(F32)
    mixed = (pa_ref[...].astype(F32) + pb_ref[...].astype(F32)) + (pc_ref[...].astype(F32) + pd_ref[...].astype(F32))
    hidden = mixed + res
    squares = jnp.sum(hidden * hidden, axis=1, keepdims=True)
    gated = (hidden * gain_ref[...]).astype(BF16)
    wide = jnp.broadcast_to(squares, (256, 128))
    top_scr[...] = wide
    top_scr[:, 0:CLUSTERS] = dot_nt(gated, topw_ref[...])
    for k in range(16):
        top_ref[place_ref[k + 1]] = top_scr[k * 16:(k + 1) * 16]
    dest = gp_ref[0:1, :]
    rank = gp_ref[1:2, :]
    rows = lax.broadcasted_iota(jnp.int32, (16, 256), 0)
    sq_row = wide.T[0:16]
    spread = jnp.where(rows == dest, sq_row, 0.0)
    hi = spread.astype(BF16)
    rest = spread - hi.astype(F32)
    mid = rest.astype(BF16)
    low = (rest - mid.astype(F32)).astype(BF16)
    by_rank = (lax.broadcasted_iota(jnp.int32, (128, 256), 0) == rank).astype(F32).astype(BF16)
    code = jnp.concatenate([dot_nt(hi, by_rank), dot_nt(mid, by_rank), dot_nt(low, by_rank), jnp.zeros((16, 128), F32)], axis=1).astype(BF16)
    slot = dest * cap + rank
    pick = (lax.broadcasted_iota(jnp.int32, (16 * cap, 256), 0) == slot).astype(F32).astype(BF16)
    srow = lax.broadcasted_iota(jnp.int32, (16 * cap, 16), 0)
    scol = lax.broadcasted_iota(jnp.int32, (16 * cap, 16), 1)
    last = (srow == scol * cap + cap - 1).astype(F32).astype(BF16)
    out_ref[...] = (dot_nn(pick, gated) + dot_nn(last, code)).astype(BF16)


def post(cap, place, parts, residual, gain, topw, gp):
    return pl.pallas_call(
        functools.partial(post_kernel, cap),
        out_shape=(jax.ShapeDtypeStruct((16 * cap, 512), BF16), jax.ShapeDtypeStruct((16, 16, 128), F32)),
        grid_spec=pltpu.PrefetchScalarGridSpec(
            num_scalar_prefetch=1,
            grid=(1,),
            in_specs=[
                *[pl.BlockSpec((256, 512), lambda i, p: (0, 0))] * 4,
                pl.BlockSpec((1, 16, 16, 512), lambda i, p: (p[0], 0, 0, 0)),
                pl.BlockSpec((1, 512), lambda i, p: (0, 0)),
                pl.BlockSpec((CLUSTERS, 512), lambda i, p: (0, 0)),
                pl.BlockSpec((2, 256), lambda i, p: (0, 0)),
            ],
            out_specs=(
                pl.BlockSpec((16 * cap, 512), lambda i, p: (0, 0)),
                pl.BlockSpec((16, 16, 128), lambda i, p: (0, 0, 0)),
            ),
            scratch_shapes=[pltpu.VMEM((256, 128), F32)],
        ),
        cost_estimate=pl.CostEstimate(flops=300_000_000, bytes_accessed=3_000_000, transcendentals=0),
        name="post",
    )(place, *parts, residual, gain, topw, gp)


def stack_rows(cap, blocks):
    if cap % 16 == 0:
        return jnp.concatenate(blocks, axis=0)
    return jnp.concatenate([b.astype(F32) for b in blocks], axis=0).astype(BF16)


def leaf_accumulate(cap, pieces, w_ref, acc, sq_acc):
    @pl.when(pl.program_id(0) == 0)
    def _():
        acc[...] = jnp.zeros_like(acc)
        sq_acc[...] = jnp.zeros_like(sq_acc)

    lhs = []
    for c in range(4):
        blocks = [ref[c] for ref in pieces]
        for k, block in enumerate(blocks):
            spare = block[cap - 8:cap].astype(F32)[7:8]
            sq_acc[k:k + 1] += spare[:, 0:128] + spare[:, 128:256] + spare[:, 256:384]
        lhs.append(stack_rows(cap, blocks))
    lhs = jnp.concatenate(lhs, axis=1)
    for first, width in ((0, 2), (2, 2), (4, 1)):
        part = [w_ref[first + k] for k in range(width)]
        rhs = part[0] if width == 1 else jnp.concatenate(part, axis=1)
        acc[:, first * 128:(first + width) * 128] += dot_nn(lhs, rhs)


def leaf_finish(cap, n, place_ref, code_ref, acc, sq_acc, out_ref):
    start = place_ref[n]
    r_i = lax.broadcasted_iota(jnp.int32, (cap, 128), 0)
    c_i = lax.broadcasted_iota(jnp.int32, (cap, 128), 1)
    diag = r_i == c_i
    shifted = r_i + 64 == c_i

    def column(row):
        return jnp.sum(jnp.where(diag, jnp.broadcast_to(row, (cap, 128)), 0.0), axis=1, keepdims=True)

    for k in range(n):
        b = place_ref[k]
        code = column(code_ref[pl.ds(b, 1), :]).astype(jnp.int32)
        local = code >> 10
        target = (code & 1023) - start
        logits = jnp.zeros((cap, 128), F32)
        for j in range(LOCAL):
            logits = jnp.where(local == j, acc[k * cap:(k + 1) * cap, j * 128:(j + 1) * 128], logits)
        logits = logits * lax.rsqrt(column(sq_acc[k:k + 1]) / D + 1e-05)
        peak = jnp.max(logits, axis=1, keepdims=True)
        lse = peak + jnp.log(jnp.sum(jnp.exp(logits - peak), axis=1, keepdims=True))
        hit = jnp.sum(jnp.where(c_i == target, logits, 0.0), axis=1, keepdims=True)
        row = jnp.where(diag, lse, 0.0) + jnp.where(shifted, hit, 0.0)
        out_ref[pl.ds(b, 1), :] = jnp.sum(row, axis=0, keepdims=True)


def top_rows(top_ref, ids):
    total = top_ref[0]
    for k in range(1, 16):
        total = total + top_ref[k]
    lane = lax.broadcasted_iota(jnp.int32, (16, 128), 1)
    row = lax.broadcasted_iota(jnp.int32, (16, 128), 0)
    own_id = jnp.sum(jnp.where(lane == row, jnp.broadcast_to(ids, (16, 128)), 0.0), axis=1, keepdims=True).astype(jnp.int32)
    logits = total * lax.rsqrt(total[:, CLUSTERS:CLUSTERS + 1] / D + 1e-05)
    logits = jnp.where(lane < CLUSTERS, logits, -jnp.inf)
    peak = jnp.max(logits, axis=1, keepdims=True)
    norm = peak + jnp.log(jnp.sum(jnp.exp(logits - peak), axis=1, keepdims=True))
    own = jnp.sum(jnp.where(lane == own_id, logits, 0.0), axis=1, keepdims=True) - norm
    small = lane[0:4]
    rows = jnp.zeros((4, 128), F32)
    for j in range(4):
        rows = jnp.where(small == 60 + j, own[4 * j:4 * j + 4], rows)
    return rows


def near_kernel(cap, place_ref, *refs):
    pieces, (code_ref, w_ref, out_ref, acc, sq_acc) = refs[:6], refs[6:]
    leaf_accumulate(cap, pieces, w_ref, acc, sq_acc)

    @pl.when(pl.program_id(0) == pl.num_programs(0) - 1)
    def _():
        out_ref[...] = jnp.zeros_like(out_ref)
        leaf_finish(cap, 6, place_ref, code_ref, acc, sq_acc, out_ref)


def far_kernel(cap, place_ref, *refs):
    pieces, (code_ref, near_ref, top_ref, w_ref, out_ref, acc, sq_acc, state) = refs[:2], refs[2:]
    leaf_accumulate(cap, pieces, w_ref, acc, sq_acc)

    @pl.when(pl.program_id(0) == pl.num_programs(0) - 1)
    def _():
        state[...] = near_ref[...]
        leaf_finish(cap, 2, place_ref, code_ref, acc, sq_acc, state)
        lane = lax.broadcasted_iota(jnp.int32, (4, 128), 1)
        top = top_rows(top_ref, code_ref[8:9, :])
        for r in range(2):
            rows = jnp.where((lane >= 60) & (lane < 64), top, state[r * 4:r * 4 + 4, :])
            out_ref[r * 64:(r + 1) * 64] = jnp.broadcast_to(rows[None], (64, 4, 128))


def leaf_call(cap, kernel, name, out_shape, place, pieces, small, w, scratch):
    n = len(pieces)
    fixed = lambda shape: pl.BlockSpec(shape, lambda c, p: (0,) * len(shape))
    return pl.pallas_call(
        functools.partial(kernel, cap),
        out_shape=jax.ShapeDtypeStruct(out_shape, F32),
        grid_spec=pltpu.PrefetchScalarGridSpec(
            num_scalar_prefetch=1,
            grid=(4,),
            in_specs=[pl.BlockSpec((4, cap, 512), lambda c, p: (c, 0, 0))] * n
            + [fixed(a.shape) for a in small]
            + [pl.BlockSpec((LOCAL, 2048, 128), lambda c, p: (0, c, 0))],
            out_specs=fixed(out_shape),
            scratch_shapes=[pltpu.VMEM((n * cap, LOCAL * 128), F32), pltpu.VMEM((8, 128), F32)] + scratch,
        ),
        cost_estimate=pl.CostEstimate(flops=2 * n * cap * 8192 * 640, bytes_accessed=11_000_000, transcendentals=0),
        name=name,
    )(place, *pieces, *small, w)


def final_kernel(place_ref, heard_ref, gp_ref, out_ref):
    blocks = [heard_ref[d * 16:(d + 1) * 16] for d in range(8)]
    peak = functools.reduce(jnp.maximum, blocks)
    mass = functools.reduce(jnp.add, [jnp.exp(b - peak) for b in blocks])
    picked = functools.reduce(jnp.add, blocks)
    leaf = pltpu.roll(picked, 64, 2) - (peak + jnp.log(mass))
    lane = lax.broadcasted_iota(jnp.int32, (16, 128), 1)
    row = lax.broadcasted_iota(jnp.int32, (16, 128), 0)

    def column(at):
        wide = jnp.broadcast_to(gp_ref[at:at + 1, :], (16, 128))
        return jnp.sum(jnp.where(lane == row, wide, 0.0), axis=1, keepdims=True).astype(jnp.int32)

    for s in range(4):
        g = jnp.broadcast_to(column(s), (16, 128))
        at = lane == column(4 + s)
        tops = heard_ref[place_ref[0] * 64 + s * 16 + place_ref[1]]
        found = jnp.where(lane == 60 + (row >> 2), jnp.concatenate([tops] * 4, axis=0), 0.0)
        for c in range(16):
            found = found + jnp.where(at & (g == c), leaf[c, s:s + 1], 0.0)
        total = jnp.sum(found, axis=1, keepdims=True)
        out_ref[s:s + 1, :] = jnp.sum(jnp.where(lane == row, total, 0.0), axis=0, keepdims=True)[:, 0:16]


def small_call(kernel, name, out_shape, *args, smem=0):
    many = isinstance(out_shape[0], tuple)
    shapes = out_shape if many else (out_shape,)
    shapes = tuple(jax.ShapeDtypeStruct(s, F32) for s in shapes)
    return pl.pallas_call(
        kernel,
        out_shape=shapes if many else shapes[0],
        in_specs=[SMEM] * smem + [VMEM] * (len(args) - smem),
        out_specs=(VMEM,) * len(shapes) if many else VMEM,
        name=name,
    )(*args)


def from_cluster(x, dy, dz):
    pairs = []
    for c in range(16):
        pairs.append(((c // 4 + dy) % 4 * 4 + (c % 4 + dz) % 4, c))
    return lax.ppermute(x, "cluster", pairs)


def from_split(x, dy, dz):
    pairs = []
    for c in range(16):
        for r in range(2):
            sign = 1 - 2 * r
            source = (c // 4 + sign * dy) % 4 * 4 + (c % 4 + sign * dz) % 4
            pairs.append((r * 16 + source, r * 16 + c))
    return lax.ppermute(x, ("rows", "cluster"), pairs)


def from_split_x(x, d):
    pairs = [(r * 4 + (h + (1 - 2 * r) * d) % 4, r * 4 + h) for r in range(2) for h in range(4)]
    return lax.ppermute(x, ("rows", "head"), pairs)


def to_x(x, d):
    return lax.ppermute(x, "head", [(h, (h + d) % 4) for h in range(4)])


def swap(x):
    return lax.ppermute(x, "rows", [(0, 1), (1, 0)])


def tail(cap, parts, residual, gain, topw, places, gp, code, gp_rows, leaf_weight):
    place, near_place, far_place, end_place = places
    outgoing, top = post(cap, place, parts, residual, gain, topw, gp)
    own = lax.all_to_all(outgoing.reshape(16, cap, 512), "cluster", 0, 0, tiled=True)
    first, second = from_split_x(own, 1), from_split_x(own, 3)
    top = lax.all_to_all(top, "cluster", 0, 0, tiled=True)
    first, second, top = lax.optimization_barrier((first, second, top))
    far = from_split_x(first, 1)
    near = leaf_call(cap, near_kernel, "near", (8, 128), near_place, [own, first, second, swap(own), swap(first), swap(second)], [code], leaf_weight, [])
    far, near = lax.optimization_barrier((far, near))
    heard = leaf_call(cap, far_kernel, "far", (128, 4, 128), far_place, [far, swap(far)], [code, near, top], leaf_weight, [pltpu.VMEM((8, 128), F32)])
    heard = lax.all_to_all(heard, ("rows", "head", "cluster"), 0, 0, tiled=True)
    return small_call(final_kernel, "final", (4, 16), end_place, heard, gp_rows, smem=1)


def shards(queries, new_keys, new_values, key_cache, value_cache, lengths, residual_in, out_weight, norm_gain, top_weight, leaf_weight, cluster_ids, targets):
    my_cluster = lax.axis_index("cluster").astype(jnp.int32)
    my_row = lax.axis_index("rows").astype(jnp.int32)
    my_head = lax.axis_index("head").astype(jnp.int32)
    my_y, my_z = my_cluster // SIDE, my_cluster % SIDE

    ids8 = cluster_ids[:, :, 0].reshape(STEPS, 2, 256).transpose(1, 0, 2).reshape(8, 256)
    tg8 = targets.reshape(STEPS, 2, 256).transpose(1, 0, 2).reshape(8, 256)
    g8 = ids8 // LOCAL
    index = jnp.arange(256)
    earlier = (g8[:, :, None] == g8[:, None, :]) & (index[None, None, :] < index[None, :, None])
    p8 = jnp.sum(earlier.astype(jnp.int32), axis=2)
    own_block = my_row * 4 + my_head
    sign = 1 - 2 * my_row
    offs = jnp.array(OFFS, jnp.int32)
    major, minor = jnp.repeat(offs * sign, 4), jnp.tile(offs, 4)
    first = my_head < 2
    cabs = ((my_y + jnp.where(first, major, minor)) & 3) * 4 + ((my_z + jnp.where(first, minor, major)) & 3)
    place = jnp.concatenate([my_head[None], cabs])
    own_g = lax.dynamic_index_in_dim(g8, own_block, 0, False).reshape(16, 16)
    own_p = lax.dynamic_index_in_dim(p8, own_block, 0, False).reshape(16, 16)
    gp = jnp.stack([own_g[cabs].reshape(256), own_p[cabs].reshape(256)])
    own_ids = lax.dynamic_slice(ids8, (own_block, my_cluster * 16), (1, 16))
    g_rows = lax.dynamic_slice(g8, (my_row * 4, my_cluster * 16), (4, 16))
    p_rows = lax.dynamic_slice(p8, (my_row * 4, my_cluster * 16), (4, 16))
    gp_rows = jnp.pad(jnp.concatenate([g_rows, p_rows]), ((0, 0), (0, 112))).astype(F32)
    land = (g8 == my_cluster)[:, None, :] & (p8[:, None, :] == jnp.arange(128)[None, :, None])
    value = (ids8 % LOCAL * 1024 + tg8).astype(F32)
    code = jnp.sum(jnp.where(land, value[:, None, :], 0.0), axis=2)
    code = jnp.concatenate([code, jnp.pad(own_ids, ((0, 7), (0, 112))).astype(F32)])
    block = lambda flip, d: (my_row ^ flip) * 4 + ((my_head + d) & 3)
    start = (my_row * 4 + my_head) * LEAF_COLS
    near_place = jnp.stack([block(0, 0), block(0, sign), block(0, -sign), block(1, 0), block(1, -sign), block(1, sign), start])
    far_place = jnp.stack([block(0, 2), block(1, 2), start])
    end_place = jnp.stack([my_row, my_cluster])
    load = jnp.max(p8)
    level = sum((load >= size - 1).astype(jnp.int32) for size in SIZES[:-1])
    places = (place, near_place, far_place, end_place)
    places, gp, code, gp_rows, level = lax.optimization_barrier((places, gp, code, gp_rows, level))

    att_a, att_b = attend(lengths, queries, new_keys, new_values, key_cache, value_cache)
    za = jnp.stack([att_a] + [from_cluster(att_a, 0, d) for d in OFFS[1:]])
    yb = jnp.stack([att_b] + [from_cluster(att_b, d, 0) for d in OFFS[1:]])
    a1, a3 = from_split(za, 1, 0), from_split(za, 3, 0)
    b1, b3 = from_split(yb, 0, 1), from_split(yb, 0, 3)
    a2, b2 = from_split(a1, 1, 0), from_split(b1, 0, 1)
    sums = project_near([za, a1, yb, b1], out_weight)
    sums = project_far(place, [a3, a2, b3, b2], sums, out_weight)
    parts = [sums[0]] + [to_x(sums[k], OFFS[k]) for k in (1, 2, 3)]

    args = (parts, residual_in.reshape(4, 16, 16, 512), norm_gain[None, :], top_weight.T, places, gp, code, gp_rows, leaf_weight)
    return lax.switch(level, [functools.partial(tail, size) for size in SIZES], *args)


def solution(mesh):
    placed = (
        P(None, ("rows", "cluster"), "head"),
        P(None, ("rows", "cluster"), "head"),
        P(None, ("rows", "cluster"), "head"),
        P(("rows", "cluster"), "head", None, None),
        P(("rows", "cluster"), "head", None, None),
        P(("rows", "cluster")),
        P(None, "rows", "cluster"),
        P("head", "cluster"),
        P("cluster"),
        P("cluster", None),
        P("cluster", None, ("rows", "head")),
        P(),
        P(),
    )
    return jax.shard_map(
        shards, mesh=mesh, in_specs=placed, out_specs=P(None, ("rows", "cluster")), check_vma=False
    )
```

```python
import functools
import jax
import jax.numpy as jnp
from jax import lax
from jax.experimental import pallas as pl
from jax.experimental.pallas import tpu as pltpu
from jax.sharding import PartitionSpec as P


D = 8192
CLUSTERS = 80
STEPS = 4
LOCAL = 5
LEAF_COLS = 128
SIDE = 4
OFFS = (0, 1, 3, 2)
SIZES = (32, 40, 64)
F32 = jnp.float32
BF16 = jnp.bfloat16
VMEM = pl.BlockSpec(memory_space=pltpu.VMEM)
SMEM = pl.BlockSpec(memory_space=pltpu.SMEM)


def dot_nt(a, b):
    return lax.dot_general(a, b, (((1,), (1,)), ((), ())), preferred_element_type=F32)


def dot_nn(a, b):
    return lax.dot_general(a, b, (((1,), (0,)), ((), ())), preferred_element_type=F32)


def attend_kernel(len_ref, q_ref, nk_ref, nv_ref, k_ref, v_ref, oa_ref, ob_ref, q_scr, o_scr, q2_scr, o2_scr):
    step = pl.program_id(0)
    heads = 16
    scale = 128 ** (-0.5)

    @pl.when(step == 0)
    def _():
        for head in range(heads):
            part = q_ref[:, :, head * 128:(head + 1) * 128]
            q_scr[head] = part.reshape(64, 128).astype(F32)

    row0 = step * 4
    m_col = lax.broadcasted_iota(jnp.int32, (128, 64), 0)
    n_row = lax.broadcasted_iota(jnp.int32, (128, 64), 1)
    recent_ok = ((n_row & 15) == row0 + (m_col >> 5)) & ((n_row >> 4) <= (m_col & 3))
    lane = lax.broadcasted_iota(jnp.int32, (32, 256), 1)
    for kv in range(2):
        for rr in range(4):
            for g in range(8):
                q2_scr[kv, rr * 32 + g * 4:rr * 32 + g * 4 + 4, :] = q_scr[kv * 8 + g, pl.ds(row0 + rr, 4, stride=16), :]
        q2 = q2_scr[kv].astype(BF16)
        cached = []
        for rr in range(4):
            s = dot_nt(q2[rr * 32:(rr + 1) * 32], k_ref[rr, kv]) * scale
            cached.append(jnp.where(lane < len_ref[row0 + rr], s, -jnp.inf))
        cached = jnp.concatenate(cached, axis=0)
        nk = nk_ref[:, :, kv * 128:(kv + 1) * 128].reshape(64, 128)
        nv = nv_ref[:, :, kv * 128:(kv + 1) * 128].reshape(64, 128)
        recent = jnp.where(recent_ok, dot_nt(q2, nk) * scale, -jnp.inf)
        peak = jnp.maximum(jnp.max(cached, axis=1, keepdims=True), jnp.max(recent, axis=1, keepdims=True))
        ec = jnp.exp(cached - peak)
        er = jnp.exp(recent - peak)
        inv = 1.0 / (jnp.sum(ec, axis=1, keepdims=True) + jnp.sum(er, axis=1, keepdims=True))
        wc = (ec * inv).astype(BF16)
        wr = (er * inv).astype(BF16)
        out = []
        for rr in range(4):
            out.append(dot_nn(wc[rr * 32:(rr + 1) * 32], v_ref[rr, kv]))
        o2_scr[kv] = jnp.concatenate(out, axis=0) + dot_nn(wr, nv)
        for rr in range(4):
            for g in range(8):
                o_scr[kv * 8 + g, pl.ds(row0 + rr, 4, stride=16), :] = o2_scr[kv, rr * 32 + g * 4:rr * 32 + g * 4 + 4, :]

    @pl.when(step == pl.num_programs(0) - 1)
    def _():
        for head in range(heads):
            cols = slice(head * 128, (head + 1) * 128)
            oa_ref[:, :, cols] = o_scr[head, 0:32].reshape(2, 16, 128).astype(BF16)
            ob_ref[:, :, cols] = o_scr[head, 32:64].reshape(2, 16, 128).astype(BF16)


def attend(lengths, q, nk, nv, k, v):
    whole = lambda shape: pl.BlockSpec(shape, lambda i, *_: (0,) * len(shape))
    block = pl.BlockSpec((4, 2, 256, 128), lambda i, *_: (i, 0, 0, 0))
    return pl.pallas_call(
        attend_kernel,
        out_shape=(jax.ShapeDtypeStruct((2, 16, 2048), BF16),) * 2,
        grid_spec=pltpu.PrefetchScalarGridSpec(
            num_scalar_prefetch=1,
            grid=(4,),
            in_specs=[whole((4, 16, 2048)), whole((4, 16, 256)), whole((4, 16, 256)), block, block],
            out_specs=(whole((2, 16, 2048)),) * 2,
            scratch_shapes=[
                pltpu.VMEM((16, 64, 128), F32),
                pltpu.VMEM((16, 64, 128), F32),
                pltpu.VMEM((2, 128, 128), F32),
                pltpu.VMEM((2, 128, 128), F32),
            ],
        ),
        cost_estimate=pl.CostEstimate(flops=300_000_000, bytes_accessed=5_000_000, transcendentals=400_000),
        name="attend",
    )(lengths, q, nk, nv, k, v)


def project_rows(pieces, lhs, w_ref, store):
    for s in range(4):
        for i in range(2):
            for j in range(4):
                at = s * 128 + (i * 4 + j) * 16
                lhs[at:at + 16, :] = pieces[s // 2][i][j, s % 2]
    for n in range(2):
        cols = slice(n * 256, (n + 1) * 256)
        rows = dot_nn(lhs[...], w_ref[:, cols]).astype(BF16)
        for s in range(4):
            store[s, :, cols] = rows[s * 128:(s + 1) * 128]


def project_kernel(place_ref, a0, a1, b0, b1, w_ref, *refs):
    outs, (lhs, all_rows) = refs[:4], refs[4:]
    project_rows(((a0, a1), (b0, b1)), lhs, w_ref, all_rows)
    for out, d in zip(outs, OFFS):
        out[...] = all_rows[(place_ref[0] + d) & 3]


def project(name, place, pieces, w):
    return pl.pallas_call(
        project_kernel,
        out_shape=(jax.ShapeDtypeStruct((128, 512), BF16),) * 4,
        in_specs=[SMEM] + [VMEM] * 5,
        out_specs=(VMEM,) * 4,
        scratch_shapes=[pltpu.VMEM((512, 2048), BF16), pltpu.VMEM((4, 128, 512), BF16)],
        cost_estimate=pl.CostEstimate(flops=1_100_000_000, bytes_accessed=6_000_000, transcendentals=0),
        name=name,
    )(place, *pieces, w)


def post_kernel(cap, place_ref, *refs):
    parts, (res_ref, gain_ref, topw_ref, gp_ref, out_ref, top_ref, top_scr) = refs[:8], refs[8:]
    res = jnp.concatenate([res_ref[0, place_ref[k + 1]] for k in range(16)], axis=0).astype(F32)
    wide_parts = [p[...].astype(F32) for p in parts]
    near = (wide_parts[0] + wide_parts[1]) + (wide_parts[2] + wide_parts[3])
    far = (wide_parts[4] + wide_parts[5]) + (wide_parts[6] + wide_parts[7])
    mixed = jnp.concatenate([near, far], axis=0)
    hidden = mixed + res
    squares = jnp.sum(hidden * hidden, axis=1, keepdims=True)
    gated = (hidden * gain_ref[...]).astype(BF16)
    wide = jnp.broadcast_to(squares, (256, 128))
    top_scr[...] = wide
    top_scr[:, 0:CLUSTERS] = dot_nt(gated, topw_ref[...])
    for k in range(16):
        top_ref[place_ref[k + 1]] = top_scr[k * 16:(k + 1) * 16]
    dest = gp_ref[0:1, :]
    rank = gp_ref[1:2, :]
    rows = lax.broadcasted_iota(jnp.int32, (16, 256), 0)
    sq_row = wide.T[0:16]
    spread = jnp.where(rows == dest, sq_row, 0.0)
    hi = spread.astype(BF16)
    rest = spread - hi.astype(F32)
    mid = rest.astype(BF16)
    low = (rest - mid.astype(F32)).astype(BF16)
    by_rank = (lax.broadcasted_iota(jnp.int32, (128, 256), 0) == rank).astype(F32).astype(BF16)
    code = jnp.concatenate([dot_nt(hi, by_rank), dot_nt(mid, by_rank), dot_nt(low, by_rank), jnp.zeros((16, 128), F32)], axis=1).astype(BF16)
    slot = dest * cap + rank
    pick = (lax.broadcasted_iota(jnp.int32, (16 * cap, 256), 0) == slot).astype(F32).astype(BF16)
    srow = lax.broadcasted_iota(jnp.int32, (16 * cap, 16), 0)
    scol = lax.broadcasted_iota(jnp.int32, (16 * cap, 16), 1)
    last = (srow == scol * cap + cap - 1).astype(F32).astype(BF16)
    out_ref[...] = (dot_nn(pick, gated) + dot_nn(last, code)).astype(BF16)


def post(cap, place, parts, residual, gain, topw, gp):
    return pl.pallas_call(
        functools.partial(post_kernel, cap),
        out_shape=(jax.ShapeDtypeStruct((16 * cap, 512), BF16), jax.ShapeDtypeStruct((16, 16, 128), F32)),
        grid_spec=pltpu.PrefetchScalarGridSpec(
            num_scalar_prefetch=1,
            grid=(1,),
            in_specs=[
                *[pl.BlockSpec((128, 512), lambda i, p: (0, 0))] * 8,
                pl.BlockSpec((1, 16, 16, 512), lambda i, p: (p[0], 0, 0, 0)),
                pl.BlockSpec((1, 512), lambda i, p: (0, 0)),
                pl.BlockSpec((CLUSTERS, 512), lambda i, p: (0, 0)),
                pl.BlockSpec((2, 256), lambda i, p: (0, 0)),
            ],
            out_specs=(
                pl.BlockSpec((16 * cap, 512), lambda i, p: (0, 0)),
                pl.BlockSpec((16, 16, 128), lambda i, p: (0, 0, 0)),
            ),
            scratch_shapes=[pltpu.VMEM((256, 128), F32)],
        ),
        cost_estimate=pl.CostEstimate(flops=300_000_000, bytes_accessed=3_000_000, transcendentals=0),
        name="post",
    )(place, *parts, residual, gain, topw, gp)


def stack_rows(cap, blocks):
    if cap % 16 == 0:
        return jnp.concatenate(blocks, axis=0)
    return jnp.concatenate([b.astype(F32) for b in blocks], axis=0).astype(BF16)


def leaf_accumulate(cap, pieces, w_ref, acc, sq_acc):
    @pl.when(pl.program_id(0) == 0)
    def _():
        acc[...] = jnp.zeros_like(acc)
        sq_acc[...] = jnp.zeros_like(sq_acc)

    lhs = []
    for c in range(4):
        blocks = [ref[c] for ref in pieces]
        for k, block in enumerate(blocks):
            spare = block[cap - 8:cap].astype(F32)[7:8]
            sq_acc[k:k + 1] += spare[:, 0:128] + spare[:, 128:256] + spare[:, 256:384]
        lhs.append(stack_rows(cap, blocks))
    lhs = jnp.concatenate(lhs, axis=1)
    for first, width in ((0, 2), (2, 2), (4, 1)):
        part = [w_ref[first + k] for k in range(width)]
        rhs = part[0] if width == 1 else jnp.concatenate(part, axis=1)
        acc[:, first * 128:(first + width) * 128] += dot_nn(lhs, rhs)


def leaf_finish(cap, n, place_ref, code_ref, acc, sq_acc, out_ref):
    start = place_ref[n]
    r_i = lax.broadcasted_iota(jnp.int32, (cap, 128), 0)
    c_i = lax.broadcasted_iota(jnp.int32, (cap, 128), 1)
    diag = r_i == c_i
    shifted = r_i + 64 == c_i

    def column(row):
        return jnp.sum(jnp.where(diag, jnp.broadcast_to(row, (cap, 128)), 0.0), axis=1, keepdims=True)

    for k in range(n):
        b = place_ref[k]
        code = column(code_ref[pl.ds(b, 1), :]).astype(jnp.int32)
        local = code >> 10
        target = (code & 1023) - start
        logits = jnp.zeros((cap, 128), F32)
        for j in range(LOCAL):
            logits = jnp.where(local == j, acc[k * cap:(k + 1) * cap, j * 128:(j + 1) * 128], logits)
        logits = logits * lax.rsqrt(column(sq_acc[k:k + 1]) / D + 1e-05)
        peak = jnp.max(logits, axis=1, keepdims=True)
        lse = peak + jnp.log(jnp.sum(jnp.exp(logits - peak), axis=1, keepdims=True))
        hit = jnp.sum(jnp.where(c_i == target, logits, 0.0), axis=1, keepdims=True)
        row = jnp.where(diag, lse, 0.0) + jnp.where(shifted, hit, 0.0)
        out_ref[pl.ds(b, 1), :] = jnp.sum(row, axis=0, keepdims=True)


def top_rows(top_ref, ids):
    total = top_ref[0]
    for k in range(1, 16):
        total = total + top_ref[k]
    lane = lax.broadcasted_iota(jnp.int32, (16, 128), 1)
    row = lax.broadcasted_iota(jnp.int32, (16, 128), 0)
    own_id = jnp.sum(jnp.where(lane == row, jnp.broadcast_to(ids, (16, 128)), 0.0), axis=1, keepdims=True).astype(jnp.int32)
    logits = total * lax.rsqrt(total[:, CLUSTERS:CLUSTERS + 1] / D + 1e-05)
    logits = jnp.where(lane < CLUSTERS, logits, -jnp.inf)
    peak = jnp.max(logits, axis=1, keepdims=True)
    norm = peak + jnp.log(jnp.sum(jnp.exp(logits - peak), axis=1, keepdims=True))
    own = jnp.sum(jnp.where(lane == own_id, logits, 0.0), axis=1, keepdims=True) - norm
    small = lane[0:4]
    rows = jnp.zeros((4, 128), F32)
    for j in range(4):
        rows = jnp.where(small == 60 + j, own[4 * j:4 * j + 4], rows)
    return rows


def near_kernel(cap, place_ref, *refs):
    pieces, (code_ref, w_ref, out_ref, acc, sq_acc) = refs[:6], refs[6:]
    leaf_accumulate(cap, pieces, w_ref, acc, sq_acc)

    @pl.when(pl.program_id(0) == pl.num_programs(0) - 1)
    def _():
        out_ref[...] = jnp.zeros_like(out_ref)
        leaf_finish(cap, 6, place_ref, code_ref, acc, sq_acc, out_ref)


def far_kernel(cap, place_ref, *refs):
    pieces, (code_ref, near_ref, top_ref, w_ref, out_ref, acc, sq_acc, state) = refs[:2], refs[2:]
    leaf_accumulate(cap, pieces, w_ref, acc, sq_acc)

    @pl.when(pl.program_id(0) == pl.num_programs(0) - 1)
    def _():
        state[...] = near_ref[...]
        leaf_finish(cap, 2, place_ref, code_ref, acc, sq_acc, state)
        lane = lax.broadcasted_iota(jnp.int32, (4, 128), 1)
        top = top_rows(top_ref, code_ref[8:9, :])
        for r in range(2):
            rows = jnp.where((lane >= 60) & (lane < 64), top, state[r * 4:r * 4 + 4, :])
            out_ref[r * 64:(r + 1) * 64] = jnp.broadcast_to(rows[None], (64, 4, 128))


def leaf_call(cap, kernel, name, out_shape, place, pieces, small, w, scratch):
    n = len(pieces)
    fixed = lambda shape: pl.BlockSpec(shape, lambda c, p: (0,) * len(shape))
    return pl.pallas_call(
        functools.partial(kernel, cap),
        out_shape=jax.ShapeDtypeStruct(out_shape, F32),
        grid_spec=pltpu.PrefetchScalarGridSpec(
            num_scalar_prefetch=1,
            grid=(4,),
            in_specs=[pl.BlockSpec((4, cap, 512), lambda c, p: (c, 0, 0))] * n
            + [fixed(a.shape) for a in small]
            + [pl.BlockSpec((LOCAL, 2048, 128), lambda c, p: (0, c, 0))],
            out_specs=fixed(out_shape),
            scratch_shapes=[pltpu.VMEM((n * cap, LOCAL * 128), F32), pltpu.VMEM((8, 128), F32)] + scratch,
        ),
        cost_estimate=pl.CostEstimate(flops=2 * n * cap * 8192 * 640, bytes_accessed=11_000_000, transcendentals=0),
        name=name,
    )(place, *pieces, *small, w)


def final_kernel(place_ref, heard_ref, gp_ref, out_ref):
    blocks = [heard_ref[d * 16:(d + 1) * 16] for d in range(8)]
    peak = functools.reduce(jnp.maximum, blocks)
    mass = functools.reduce(jnp.add, [jnp.exp(b - peak) for b in blocks])
    picked = functools.reduce(jnp.add, blocks)
    leaf = pltpu.roll(picked, 64, 2) - (peak + jnp.log(mass))
    lane = lax.broadcasted_iota(jnp.int32, (16, 128), 1)
    row = lax.broadcasted_iota(jnp.int32, (16, 128), 0)

    def column(at):
        wide = jnp.broadcast_to(gp_ref[at:at + 1, :], (16, 128))
        return jnp.sum(jnp.where(lane == row, wide, 0.0), axis=1, keepdims=True).astype(jnp.int32)

    for s in range(4):
        g = jnp.broadcast_to(column(s), (16, 128))
        at = lane == column(4 + s)
        tops = heard_ref[place_ref[0] * 64 + s * 16 + place_ref[1]]
        found = jnp.where(lane == 60 + (row >> 2), jnp.concatenate([tops] * 4, axis=0), 0.0)
        for c in range(16):
            found = found + jnp.where(at & (g == c), leaf[c, s:s + 1], 0.0)
        total = jnp.sum(found, axis=1, keepdims=True)
        out_ref[s:s + 1, :] = jnp.sum(jnp.where(lane == row, total, 0.0), axis=0, keepdims=True)[:, 0:16]


def small_call(kernel, name, out_shape, *args, smem=0):
    many = isinstance(out_shape[0], tuple)
    shapes = out_shape if many else (out_shape,)
    shapes = tuple(jax.ShapeDtypeStruct(s, F32) for s in shapes)
    return pl.pallas_call(
        kernel,
        out_shape=shapes if many else shapes[0],
        in_specs=[SMEM] * smem + [VMEM] * (len(args) - smem),
        out_specs=(VMEM,) * len(shapes) if many else VMEM,
        name=name,
    )(*args)


def from_cluster(x, dy, dz):
    pairs = []
    for c in range(16):
        pairs.append(((c // 4 + dy) % 4 * 4 + (c % 4 + dz) % 4, c))
    return lax.ppermute(x, "cluster", pairs)


def from_split(x, dy, dz):
    pairs = []
    for c in range(16):
        for r in range(2):
            sign = 1 - 2 * r
            source = (c // 4 + sign * dy) % 4 * 4 + (c % 4 + sign * dz) % 4
            pairs.append((r * 16 + source, r * 16 + c))
    return lax.ppermute(x, ("rows", "cluster"), pairs)


def from_split_x(x, d):
    pairs = [(r * 4 + (h + (1 - 2 * r) * d) % 4, r * 4 + h) for r in range(2) for h in range(4)]
    return lax.ppermute(x, ("rows", "head"), pairs)


def to_x(x, d):
    return lax.ppermute(x, "head", [(h, (h + d) % 4) for h in range(4)])


def swap(x):
    return lax.ppermute(x, "rows", [(0, 1), (1, 0)])


def tail(cap, parts, residual, gain, topw, places, gp, code, gp_rows, leaf_weight):
    place, near_place, far_place, end_place = places
    outgoing, top = post(cap, place, parts, residual, gain, topw, gp)
    own = lax.all_to_all(outgoing.reshape(16, cap, 512), "cluster", 0, 0, tiled=True)
    first, second = from_split_x(own, 1), from_split_x(own, 3)
    top = lax.all_to_all(top, "cluster", 0, 0, tiled=True)
    first, second, top = lax.optimization_barrier((first, second, top))
    far = from_split_x(first, 1)
    near = leaf_call(cap, near_kernel, "near", (8, 128), near_place, [own, first, second, swap(own), swap(first), swap(second)], [code], leaf_weight, [])
    far, near = lax.optimization_barrier((far, near))
    heard = leaf_call(cap, far_kernel, "far", (128, 4, 128), far_place, [far, swap(far)], [code, near, top], leaf_weight, [pltpu.VMEM((8, 128), F32)])
    heard = lax.all_to_all(heard, ("rows", "head", "cluster"), 0, 0, tiled=True)
    return small_call(final_kernel, "final", (4, 16), end_place, heard, gp_rows, smem=1)


def shards(queries, new_keys, new_values, key_cache, value_cache, lengths, residual_in, out_weight, norm_gain, top_weight, leaf_weight, cluster_ids, targets):
    my_cluster = lax.axis_index("cluster").astype(jnp.int32)
    my_row = lax.axis_index("rows").astype(jnp.int32)
    my_head = lax.axis_index("head").astype(jnp.int32)
    my_y, my_z = my_cluster // SIDE, my_cluster % SIDE

    att_a, att_b = attend(lengths, queries, new_keys, new_values, key_cache, value_cache)
    za = jnp.stack([att_a] + [from_cluster(att_a, 0, d) for d in OFFS[1:]])
    yb = jnp.stack([att_b] + [from_cluster(att_b, d, 0) for d in OFFS[1:]])
    a1, a3 = from_split(za, 1, 0), from_split(za, 3, 0)
    b1, b3 = from_split(yb, 0, 1), from_split(yb, 0, 3)
    a2, b2 = from_split(a1, 1, 0), from_split(b1, 0, 1)
    head_place = my_head[None]
    near_sums = project("project_near", head_place, [za, a1, yb, b1], out_weight)
    near_parts = [near_sums[0]] + [to_x(near_sums[k], OFFS[k]) for k in (1, 2, 3)]
    far_sums = project("project_far", head_place, [a3, a2, b3, b2], out_weight)
    far_parts = [far_sums[0]] + [to_x(far_sums[k], OFFS[k]) for k in (1, 2, 3)]
    parts = near_parts + far_parts

    ids8 = cluster_ids[:, :, 0].reshape(STEPS, 2, 256).transpose(1, 0, 2).reshape(8, 256)
    tg8 = targets.reshape(STEPS, 2, 256).transpose(1, 0, 2).reshape(8, 256)
    g8 = ids8 // LOCAL
    index = jnp.arange(256)
    earlier = (g8[:, :, None] == g8[:, None, :]) & (index[None, None, :] < index[None, :, None])
    p8 = jnp.sum(earlier.astype(jnp.int32), axis=2)
    own_block = my_row * 4 + my_head
    sign = 1 - 2 * my_row
    offs = jnp.array(OFFS, jnp.int32)
    major, minor = jnp.repeat(offs * sign, 4), jnp.tile(offs, 4)
    first = my_head < 2
    cabs = ((my_y + jnp.where(first, major, minor)) & 3) * 4 + ((my_z + jnp.where(first, minor, major)) & 3)
    place = jnp.concatenate([my_head[None], cabs])
    own_g = lax.dynamic_index_in_dim(g8, own_block, 0, False).reshape(16, 16)
    own_p = lax.dynamic_index_in_dim(p8, own_block, 0, False).reshape(16, 16)
    gp = jnp.stack([own_g[cabs].reshape(256), own_p[cabs].reshape(256)])
    own_ids = lax.dynamic_slice(ids8, (own_block, my_cluster * 16), (1, 16))
    g_rows = lax.dynamic_slice(g8, (my_row * 4, my_cluster * 16), (4, 16))
    p_rows = lax.dynamic_slice(p8, (my_row * 4, my_cluster * 16), (4, 16))
    gp_rows = jnp.pad(jnp.concatenate([g_rows, p_rows]), ((0, 0), (0, 112))).astype(F32)
    land = (g8 == my_cluster)[:, None, :] & (p8[:, None, :] == jnp.arange(128)[None, :, None])
    value = (ids8 % LOCAL * 1024 + tg8).astype(F32)
    code = jnp.sum(jnp.where(land, value[:, None, :], 0.0), axis=2)
    code = jnp.concatenate([code, jnp.pad(own_ids, ((0, 7), (0, 112))).astype(F32)])
    block = lambda flip, d: (my_row ^ flip) * 4 + ((my_head + d) & 3)
    start = (my_row * 4 + my_head) * LEAF_COLS
    near_place = jnp.stack([block(0, 0), block(0, sign), block(0, -sign), block(1, 0), block(1, -sign), block(1, sign), start])
    far_place = jnp.stack([block(0, 2), block(1, 2), start])
    end_place = jnp.stack([my_row, my_cluster])
    load = jnp.max(p8)
    level = sum((load >= size - 1).astype(jnp.int32) for size in SIZES[:-1])
    places = (place, near_place, far_place, end_place)
    places, gp, code, gp_rows, level = lax.optimization_barrier((places, gp, code, gp_rows, level))

    args = (parts, residual_in.reshape(4, 16, 16, 512), norm_gain[None, :], top_weight.T, places, gp, code, gp_rows, leaf_weight)
    return lax.switch(level, [functools.partial(tail, size) for size in SIZES], *args)


def solution(mesh):
    placed = (
        P(None, ("rows", "cluster"), "head"),
        P(None, ("rows", "cluster"), "head"),
        P(None, ("rows", "cluster"), "head"),
        P(("rows", "cluster"), "head", None, None),
        P(("rows", "cluster"), "head", None, None),
        P(("rows", "cluster")),
        P(None, "rows", "cluster"),
        P("head", "cluster"),
        P("cluster"),
        P("cluster", None),
        P("cluster", None, ("rows", "head")),
        P(),
        P(),
    )
    return jax.shard_map(
        shards, mesh=mesh, in_specs=placed, out_specs=P(None, ("rows", "cluster")), check_vma=False
    )
```

```python
import functools
import jax
import jax.numpy as jnp
from jax import lax
from jax.experimental import pallas as pl
from jax.experimental.pallas import tpu as pltpu
from jax.sharding import PartitionSpec as P


D = 8192
CLUSTERS = 80
STEPS = 4
LOCAL = 5
LEAF_COLS = 128
SIDE = 4
OFFS = (0, 1, 3, 2)
SIZES = (32, 40, 64)
F32 = jnp.float32
BF16 = jnp.bfloat16
VMEM = pl.BlockSpec(memory_space=pltpu.VMEM)
SMEM = pl.BlockSpec(memory_space=pltpu.SMEM)
GRANT = pltpu.CompilerParams(vmem_limit_bytes=24 * 1024 * 1024)


def dot_nt(a, b):
    return lax.dot_general(a, b, (((1,), (1,)), ((), ())), preferred_element_type=F32)


def dot_nn(a, b):
    return lax.dot_general(a, b, (((1,), (0,)), ((), ())), preferred_element_type=F32)


def attend_kernel(len_ref, q_ref, nk_ref, nv_ref, k_ref, v_ref, oa_ref, ob_ref, q_scr, o_scr, q2_scr, o2_scr):
    step = pl.program_id(0)
    heads = 16
    scale = 128 ** (-0.5)

    @pl.when(step == 0)
    def _():
        for head in range(heads):
            part = q_ref[:, :, head * 128:(head + 1) * 128]
            q_scr[head] = part.reshape(64, 128).astype(F32)

    row0 = step * 4
    m_col = lax.broadcasted_iota(jnp.int32, (128, 64), 0)
    n_row = lax.broadcasted_iota(jnp.int32, (128, 64), 1)
    recent_ok = ((n_row & 15) == row0 + (m_col >> 5)) & ((n_row >> 4) <= (m_col & 3))
    lane = lax.broadcasted_iota(jnp.int32, (32, 256), 1)
    for kv in range(2):
        for rr in range(4):
            for g in range(8):
                q2_scr[kv, rr * 32 + g * 4:rr * 32 + g * 4 + 4, :] = q_scr[kv * 8 + g, pl.ds(row0 + rr, 4, stride=16), :]
        q2 = q2_scr[kv].astype(BF16)
        cached = []
        for rr in range(4):
            s = dot_nt(q2[rr * 32:(rr + 1) * 32], k_ref[rr, kv]) * scale
            cached.append(jnp.where(lane < len_ref[row0 + rr], s, -jnp.inf))
        cached = jnp.concatenate(cached, axis=0)
        nk = nk_ref[:, :, kv * 128:(kv + 1) * 128].reshape(64, 128)
        nv = nv_ref[:, :, kv * 128:(kv + 1) * 128].reshape(64, 128)
        recent = jnp.where(recent_ok, dot_nt(q2, nk) * scale, -jnp.inf)
        peak = jnp.maximum(jnp.max(cached, axis=1, keepdims=True), jnp.max(recent, axis=1, keepdims=True))
        ec = jnp.exp(cached - peak)
        er = jnp.exp(recent - peak)
        inv = 1.0 / (jnp.sum(ec, axis=1, keepdims=True) + jnp.sum(er, axis=1, keepdims=True))
        wc = (ec * inv).astype(BF16)
        wr = (er * inv).astype(BF16)
        out = []
        for rr in range(4):
            out.append(dot_nn(wc[rr * 32:(rr + 1) * 32], v_ref[rr, kv]))
        o2_scr[kv] = jnp.concatenate(out, axis=0) + dot_nn(wr, nv)
        for rr in range(4):
            for g in range(8):
                o_scr[kv * 8 + g, pl.ds(row0 + rr, 4, stride=16), :] = o2_scr[kv, rr * 32 + g * 4:rr * 32 + g * 4 + 4, :]

    @pl.when(step == pl.num_programs(0) - 1)
    def _():
        for head in range(heads):
            cols = slice(head * 128, (head + 1) * 128)
            oa_ref[:, :, cols] = o_scr[head, 0:32].reshape(2, 16, 128).astype(BF16)
            ob_ref[:, :, cols] = o_scr[head, 32:64].reshape(2, 16, 128).astype(BF16)


def attend(lengths, q, nk, nv, k, v):
    whole = lambda shape: pl.BlockSpec(shape, lambda i, *_: (0,) * len(shape))
    block = pl.BlockSpec((4, 2, 256, 128), lambda i, *_: (i, 0, 0, 0))
    return pl.pallas_call(
        attend_kernel,
        out_shape=(jax.ShapeDtypeStruct((2, 16, 2048), BF16),) * 2,
        grid_spec=pltpu.PrefetchScalarGridSpec(
            num_scalar_prefetch=1,
            grid=(4,),
            in_specs=[whole((4, 16, 2048)), whole((4, 16, 256)), whole((4, 16, 256)), block, block],
            out_specs=(whole((2, 16, 2048)),) * 2,
            scratch_shapes=[
                pltpu.VMEM((16, 64, 128), F32),
                pltpu.VMEM((16, 64, 128), F32),
                pltpu.VMEM((2, 128, 128), F32),
                pltpu.VMEM((2, 128, 128), F32),
            ],
        ),
        cost_estimate=pl.CostEstimate(flops=300_000_000, bytes_accessed=5_000_000, transcendentals=400_000),
        name="attend",
    )(lengths, q, nk, nv, k, v)


def project_rows(pieces, lhs, w_ref, store):
    for s in range(4):
        for i in range(2):
            for j in range(4):
                at = s * 128 + (i * 4 + j) * 16
                lhs[at:at + 16, :] = pieces[s // 2][i][j, s % 2]
    for n in range(2):
        cols = slice(n * 256, (n + 1) * 256)
        rows = dot_nn(lhs[...], w_ref[:, cols]).astype(BF16)
        for s in range(4):
            store[s, :, cols] = rows[s * 128:(s + 1) * 128]


def project_kernel(place_ref, a0, a1, b0, b1, w_ref, *refs):
    outs, (lhs, all_rows) = refs[:4], refs[4:]
    project_rows(((a0, a1), (b0, b1)), lhs, w_ref, all_rows)
    for out, d in zip(outs, OFFS):
        out[...] = all_rows[(place_ref[0] + d) & 3]


def project(name, place, pieces, w):
    return pl.pallas_call(
        project_kernel,
        out_shape=(jax.ShapeDtypeStruct((128, 512), BF16),) * 4,
        in_specs=[SMEM] + [VMEM] * 5,
        out_specs=(VMEM,) * 4,
        scratch_shapes=[pltpu.VMEM((512, 2048), BF16), pltpu.VMEM((4, 128, 512), BF16)],
        cost_estimate=pl.CostEstimate(flops=1_100_000_000, bytes_accessed=6_000_000, transcendentals=0),
        compiler_params=GRANT,
        name=name,
    )(place, *pieces, w)


def post_kernel(cap, place_ref, *refs):
    parts, (res_ref, gain_ref, topw_ref, gp_ref, out_ref, top_ref, top_scr) = refs[:8], refs[8:]
    res = jnp.concatenate([res_ref[0, place_ref[k + 1]] for k in range(16)], axis=0).astype(F32)
    wide_parts = [p[...].astype(F32) for p in parts]
    near = (wide_parts[0] + wide_parts[1]) + (wide_parts[2] + wide_parts[3])
    far = (wide_parts[4] + wide_parts[5]) + (wide_parts[6] + wide_parts[7])
    mixed = jnp.concatenate([near, far], axis=0)
    hidden = mixed + res
    squares = jnp.sum(hidden * hidden, axis=1, keepdims=True)
    gated = (hidden * gain_ref[...]).astype(BF16)
    wide = jnp.broadcast_to(squares, (256, 128))
    top_scr[...] = wide
    top_scr[:, 0:CLUSTERS] = dot_nt(gated, topw_ref[...])
    for k in range(16):
        top_ref[place_ref[k + 1]] = top_scr[k * 16:(k + 1) * 16]
    dest = gp_ref[0:1, :]
    rank = gp_ref[1:2, :]
    rows = lax.broadcasted_iota(jnp.int32, (16, 256), 0)
    sq_row = wide.T[0:16]
    spread = jnp.where(rows == dest, sq_row, 0.0)
    hi = spread.astype(BF16)
    rest = spread - hi.astype(F32)
    mid = rest.astype(BF16)
    low = (rest - mid.astype(F32)).astype(BF16)
    by_rank = (lax.broadcasted_iota(jnp.int32, (128, 256), 0) == rank).astype(F32).astype(BF16)
    code = jnp.concatenate([dot_nt(hi, by_rank), dot_nt(mid, by_rank), dot_nt(low, by_rank), jnp.zeros((16, 128), F32)], axis=1).astype(BF16)
    slot = dest * cap + rank
    pick = (lax.broadcasted_iota(jnp.int32, (16 * cap, 256), 0) == slot).astype(F32).astype(BF16)
    srow = lax.broadcasted_iota(jnp.int32, (16 * cap, 16), 0)
    scol = lax.broadcasted_iota(jnp.int32, (16 * cap, 16), 1)
    last = (srow == scol * cap + cap - 1).astype(F32).astype(BF16)
    out_ref[...] = (dot_nn(pick, gated) + dot_nn(last, code)).astype(BF16)


def post(cap, place, parts, residual, gain, topw, gp):
    return pl.pallas_call(
        functools.partial(post_kernel, cap),
        out_shape=(jax.ShapeDtypeStruct((16 * cap, 512), BF16), jax.ShapeDtypeStruct((16, 16, 128), F32)),
        grid_spec=pltpu.PrefetchScalarGridSpec(
            num_scalar_prefetch=1,
            grid=(1,),
            in_specs=[
                *[pl.BlockSpec((128, 512), lambda i, p: (0, 0))] * 8,
                pl.BlockSpec((1, 16, 16, 512), lambda i, p: (p[0], 0, 0, 0)),
                pl.BlockSpec((1, 512), lambda i, p: (0, 0)),
                pl.BlockSpec((CLUSTERS, 512), lambda i, p: (0, 0)),
                pl.BlockSpec((2, 256), lambda i, p: (0, 0)),
            ],
            out_specs=(
                pl.BlockSpec((16 * cap, 512), lambda i, p: (0, 0)),
                pl.BlockSpec((16, 16, 128), lambda i, p: (0, 0, 0)),
            ),
            scratch_shapes=[pltpu.VMEM((256, 128), F32)],
        ),
        cost_estimate=pl.CostEstimate(flops=300_000_000, bytes_accessed=3_000_000, transcendentals=0),
        compiler_params=GRANT,
        name="post",
    )(place, *parts, residual, gain, topw, gp)


def stack_rows(cap, blocks):
    if cap % 16 == 0:
        return jnp.concatenate(blocks, axis=0)
    return jnp.concatenate([b.astype(F32) for b in blocks], axis=0).astype(BF16)


def leaf_accumulate(cap, pieces, w_ref, acc, sq_acc):
    @pl.when(pl.program_id(0) == 0)
    def _():
        acc[...] = jnp.zeros_like(acc)
        sq_acc[...] = jnp.zeros_like(sq_acc)

    lhs = []
    for c in range(4):
        blocks = [ref[c] for ref in pieces]
        for k, block in enumerate(blocks):
            spare = block[cap - 8:cap].astype(F32)[7:8]
            sq_acc[k:k + 1] += spare[:, 0:128] + spare[:, 128:256] + spare[:, 256:384]
        lhs.append(stack_rows(cap, blocks))
    lhs = jnp.concatenate(lhs, axis=1)
    for first, width in ((0, 2), (2, 2), (4, 1)):
        part = [w_ref[first + k] for k in range(width)]
        rhs = part[0] if width == 1 else jnp.concatenate(part, axis=1)
        acc[:, first * 128:(first + width) * 128] += dot_nn(lhs, rhs)


def leaf_finish(cap, n, place_ref, code_ref, acc, sq_acc, out_ref):
    start = place_ref[n]
    r_i = lax.broadcasted_iota(jnp.int32, (cap, 128), 0)
    c_i = lax.broadcasted_iota(jnp.int32, (cap, 128), 1)
    diag = r_i == c_i
    shifted = r_i + 64 == c_i

    def column(row):
        return jnp.sum(jnp.where(diag, jnp.broadcast_to(row, (cap, 128)), 0.0), axis=1, keepdims=True)

    for k in range(n):
        b = place_ref[k]
        code = column(code_ref[pl.ds(b, 1), :]).astype(jnp.int32)
        local = code >> 10
        target = (code & 1023) - start
        logits = jnp.zeros((cap, 128), F32)
        for j in range(LOCAL):
            logits = jnp.where(local == j, acc[k * cap:(k + 1) * cap, j * 128:(j + 1) * 128], logits)
        logits = logits * lax.rsqrt(column(sq_acc[k:k + 1]) / D + 1e-05)
        peak = jnp.max(logits, axis=1, keepdims=True)
        lse = peak + jnp.log(jnp.sum(jnp.exp(logits - peak), axis=1, keepdims=True))
        hit = jnp.sum(jnp.where(c_i == target, logits, 0.0), axis=1, keepdims=True)
        row = jnp.where(diag, lse, 0.0) + jnp.where(shifted, hit, 0.0)
        out_ref[pl.ds(b, 1), :] = jnp.sum(row, axis=0, keepdims=True)


def top_rows(top_ref, ids):
    total = top_ref[0]
    for k in range(1, 16):
        total = total + top_ref[k]
    lane = lax.broadcasted_iota(jnp.int32, (16, 128), 1)
    row = lax.broadcasted_iota(jnp.int32, (16, 128), 0)
    own_id = jnp.sum(jnp.where(lane == row, jnp.broadcast_to(ids, (16, 128)), 0.0), axis=1, keepdims=True).astype(jnp.int32)
    logits = total * lax.rsqrt(total[:, CLUSTERS:CLUSTERS + 1] / D + 1e-05)
    logits = jnp.where(lane < CLUSTERS, logits, -jnp.inf)
    peak = jnp.max(logits, axis=1, keepdims=True)
    norm = peak + jnp.log(jnp.sum(jnp.exp(logits - peak), axis=1, keepdims=True))
    own = jnp.sum(jnp.where(lane == own_id, logits, 0.0), axis=1, keepdims=True) - norm
    small = lane[0:4]
    rows = jnp.zeros((4, 128), F32)
    for j in range(4):
        rows = jnp.where(small == 60 + j, own[4 * j:4 * j + 4], rows)
    return rows


def near_kernel(cap, place_ref, *refs):
    pieces, (code_ref, w_ref, out_ref, acc, sq_acc) = refs[:6], refs[6:]
    leaf_accumulate(cap, pieces, w_ref, acc, sq_acc)

    @pl.when(pl.program_id(0) == pl.num_programs(0) - 1)
    def _():
        out_ref[...] = jnp.zeros_like(out_ref)
        leaf_finish(cap, 6, place_ref, code_ref, acc, sq_acc, out_ref)


def far_kernel(cap, place_ref, *refs):
    pieces, (code_ref, near_ref, top_ref, w_ref, out_ref, acc, sq_acc, state) = refs[:2], refs[2:]
    leaf_accumulate(cap, pieces, w_ref, acc, sq_acc)

    @pl.when(pl.program_id(0) == pl.num_programs(0) - 1)
    def _():
        state[...] = near_ref[...]
        leaf_finish(cap, 2, place_ref, code_ref, acc, sq_acc, state)
        lane = lax.broadcasted_iota(jnp.int32, (4, 128), 1)
        top = top_rows(top_ref, code_ref[8:9, :])
        for r in range(2):
            rows = jnp.where((lane >= 60) & (lane < 64), top, state[r * 4:r * 4 + 4, :])
            out_ref[r * 64:(r + 1) * 64] = jnp.broadcast_to(rows[None], (64, 4, 128))


def leaf_call(cap, kernel, name, out_shape, place, pieces, small, w, scratch):
    n = len(pieces)
    fixed = lambda shape: pl.BlockSpec(shape, lambda c, p: (0,) * len(shape))
    return pl.pallas_call(
        functools.partial(kernel, cap),
        out_shape=jax.ShapeDtypeStruct(out_shape, F32),
        grid_spec=pltpu.PrefetchScalarGridSpec(
            num_scalar_prefetch=1,
            grid=(4,),
            in_specs=[pl.BlockSpec((4, cap, 512), lambda c, p: (c, 0, 0))] * n
            + [fixed(a.shape) for a in small]
            + [pl.BlockSpec((LOCAL, 2048, 128), lambda c, p: (0, c, 0))],
            out_specs=fixed(out_shape),
            scratch_shapes=[pltpu.VMEM((n * cap, LOCAL * 128), F32), pltpu.VMEM((8, 128), F32)] + scratch,
        ),
        cost_estimate=pl.CostEstimate(flops=2 * n * cap * 8192 * 640, bytes_accessed=11_000_000, transcendentals=0),
        compiler_params=GRANT,
        name=name,
    )(place, *pieces, *small, w)


def final_kernel(place_ref, heard_ref, gp_ref, out_ref):
    blocks = [heard_ref[d * 16:(d + 1) * 16] for d in range(8)]
    peak = functools.reduce(jnp.maximum, blocks)
    mass = functools.reduce(jnp.add, [jnp.exp(b - peak) for b in blocks])
    picked = functools.reduce(jnp.add, blocks)
    leaf = pltpu.roll(picked, 64, 2) - (peak + jnp.log(mass))
    lane = lax.broadcasted_iota(jnp.int32, (16, 128), 1)
    row = lax.broadcasted_iota(jnp.int32, (16, 128), 0)

    def column(at):
        wide = jnp.broadcast_to(gp_ref[at:at + 1, :], (16, 128))
        return jnp.sum(jnp.where(lane == row, wide, 0.0), axis=1, keepdims=True).astype(jnp.int32)

    for s in range(4):
        g = jnp.broadcast_to(column(s), (16, 128))
        at = lane == column(4 + s)
        tops = heard_ref[place_ref[0] * 64 + s * 16 + place_ref[1]]
        found = jnp.where(lane == 60 + (row >> 2), jnp.concatenate([tops] * 4, axis=0), 0.0)
        for c in range(16):
            found = found + jnp.where(at & (g == c), leaf[c, s:s + 1], 0.0)
        total = jnp.sum(found, axis=1, keepdims=True)
        out_ref[s:s + 1, :] = jnp.sum(jnp.where(lane == row, total, 0.0), axis=0, keepdims=True)[:, 0:16]


def small_call(kernel, name, out_shape, *args, smem=0):
    many = isinstance(out_shape[0], tuple)
    shapes = out_shape if many else (out_shape,)
    shapes = tuple(jax.ShapeDtypeStruct(s, F32) for s in shapes)
    return pl.pallas_call(
        kernel,
        out_shape=shapes if many else shapes[0],
        in_specs=[SMEM] * smem + [VMEM] * (len(args) - smem),
        out_specs=(VMEM,) * len(shapes) if many else VMEM,
        compiler_params=GRANT,
        name=name,
    )(*args)


def from_cluster(x, dy, dz):
    pairs = []
    for c in range(16):
        pairs.append(((c // 4 + dy) % 4 * 4 + (c % 4 + dz) % 4, c))
    return lax.ppermute(x, "cluster", pairs)


def from_split(x, dy, dz):
    pairs = []
    for c in range(16):
        for r in range(2):
            sign = 1 - 2 * r
            source = (c // 4 + sign * dy) % 4 * 4 + (c % 4 + sign * dz) % 4
            pairs.append((r * 16 + source, r * 16 + c))
    return lax.ppermute(x, ("rows", "cluster"), pairs)


def from_split_x(x, d):
    pairs = [(r * 4 + (h + (1 - 2 * r) * d) % 4, r * 4 + h) for r in range(2) for h in range(4)]
    return lax.ppermute(x, ("rows", "head"), pairs)


def to_x(x, d):
    return lax.ppermute(x, "head", [(h, (h + d) % 4) for h in range(4)])


def swap(x):
    return lax.ppermute(x, "rows", [(0, 1), (1, 0)])


def tail(cap, parts, residual, gain, topw, places, gp, code, gp_rows, leaf_weight):
    place, near_place, far_place, end_place = places
    outgoing, top = post(cap, place, parts, residual, gain, topw, gp)
    own = lax.all_to_all(outgoing.reshape(16, cap, 512), "cluster", 0, 0, tiled=True)
    first, second = from_split_x(own, 1), from_split_x(own, 3)
    top = lax.all_to_all(top, "cluster", 0, 0, tiled=True)
    first, second, top = lax.optimization_barrier((first, second, top))
    far = from_split_x(first, 1)
    near = leaf_call(cap, near_kernel, "near", (8, 128), near_place, [own, first, second, swap(own), swap(first), swap(second)], [code], leaf_weight, [])
    far, near = lax.optimization_barrier((far, near))
    heard = leaf_call(cap, far_kernel, "far", (128, 4, 128), far_place, [far, swap(far)], [code, near, top], leaf_weight, [pltpu.VMEM((8, 128), F32)])
    heard = lax.all_to_all(heard, ("rows", "head", "cluster"), 0, 0, tiled=True)
    return small_call(final_kernel, "final", (4, 16), end_place, heard, gp_rows, smem=1)


def shards(queries, new_keys, new_values, key_cache, value_cache, lengths, residual_in, out_weight, norm_gain, top_weight, leaf_weight, cluster_ids, targets):
    my_cluster = lax.axis_index("cluster").astype(jnp.int32)
    my_row = lax.axis_index("rows").astype(jnp.int32)
    my_head = lax.axis_index("head").astype(jnp.int32)
    my_y, my_z = my_cluster // SIDE, my_cluster % SIDE

    att_a, att_b = attend(lengths, queries, new_keys, new_values, key_cache, value_cache)
    za = jnp.stack([att_a] + [from_cluster(att_a, 0, d) for d in OFFS[1:]])
    yb = jnp.stack([att_b] + [from_cluster(att_b, d, 0) for d in OFFS[1:]])
    a1, a3 = from_split(za, 1, 0), from_split(za, 3, 0)
    b1, b3 = from_split(yb, 0, 1), from_split(yb, 0, 3)
    a2, b2 = from_split(a1, 1, 0), from_split(b1, 0, 1)
    head_place = my_head[None]
    near_sums = project("project_near", head_place, [za, a1, yb, b1], out_weight)
    near_parts = [near_sums[0]] + [to_x(near_sums[k], OFFS[k]) for k in (1, 2, 3)]
    far_sums = project("project_far", head_place, [a3, a2, b3, b2], out_weight)
    far_parts = [far_sums[0]] + [to_x(far_sums[k], OFFS[k]) for k in (1, 2, 3)]
    parts = near_parts + far_parts

    ids8 = cluster_ids[:, :, 0].reshape(STEPS, 2, 256).transpose(1, 0, 2).reshape(8, 256)
    tg8 = targets.reshape(STEPS, 2, 256).transpose(1, 0, 2).reshape(8, 256)
    g8 = ids8 // LOCAL
    index = jnp.arange(256)
    earlier = (g8[:, :, None] == g8[:, None, :]) & (index[None, None, :] < index[None, :, None])
    p8 = jnp.sum(earlier.astype(jnp.int32), axis=2)
    own_block = my_row * 4 + my_head
    sign = 1 - 2 * my_row
    offs = jnp.array(OFFS, jnp.int32)
    major, minor = jnp.repeat(offs * sign, 4), jnp.tile(offs, 4)
    first = my_head < 2
    cabs = ((my_y + jnp.where(first, major, minor)) & 3) * 4 + ((my_z + jnp.where(first, minor, major)) & 3)
    place = jnp.concatenate([my_head[None], cabs])
    own_g = lax.dynamic_index_in_dim(g8, own_block, 0, False).reshape(16, 16)
    own_p = lax.dynamic_index_in_dim(p8, own_block, 0, False).reshape(16, 16)
    gp = jnp.stack([own_g[cabs].reshape(256), own_p[cabs].reshape(256)])
    own_ids = lax.dynamic_slice(ids8, (own_block, my_cluster * 16), (1, 16))
    g_rows = lax.dynamic_slice(g8, (my_row * 4, my_cluster * 16), (4, 16))
    p_rows = lax.dynamic_slice(p8, (my_row * 4, my_cluster * 16), (4, 16))
    gp_rows = jnp.pad(jnp.concatenate([g_rows, p_rows]), ((0, 0), (0, 112))).astype(F32)
    land = (g8 == my_cluster)[:, None, :] & (p8[:, None, :] == jnp.arange(128)[None, :, None])
    value = (ids8 % LOCAL * 1024 + tg8).astype(F32)
    code = jnp.sum(jnp.where(land, value[:, None, :], 0.0), axis=2)
    code = jnp.concatenate([code, jnp.pad(own_ids, ((0, 7), (0, 112))).astype(F32)])
    block = lambda flip, d: (my_row ^ flip) * 4 + ((my_head + d) & 3)
    start = (my_row * 4 + my_head) * LEAF_COLS
    near_place = jnp.stack([block(0, 0), block(0, sign), block(0, -sign), block(1, 0), block(1, -sign), block(1, sign), start])
    far_place = jnp.stack([block(0, 2), block(1, 2), start])
    end_place = jnp.stack([my_row, my_cluster])
    load = jnp.max(p8)
    level = sum((load >= size - 1).astype(jnp.int32) for size in SIZES[:-1])
    places = (place, near_place, far_place, end_place)
    places, gp, code, gp_rows, level = lax.optimization_barrier((places, gp, code, gp_rows, level))

    args = (parts, residual_in.reshape(4, 16, 16, 512), norm_gain[None, :], top_weight.T, places, gp, code, gp_rows, leaf_weight)
    return lax.switch(level, [functools.partial(tail, size) for size in SIZES], *args)


def solution(mesh):
    placed = (
        P(None, ("rows", "cluster"), "head"),
        P(None, ("rows", "cluster"), "head"),
        P(None, ("rows", "cluster"), "head"),
        P(("rows", "cluster"), "head", None, None),
        P(("rows", "cluster"), "head", None, None),
        P(("rows", "cluster")),
        P(None, "rows", "cluster"),
        P("head", "cluster"),
        P("cluster"),
        P("cluster", None),
        P("cluster", None, ("rows", "head")),
        P(),
        P(),
    )
    return jax.shard_map(
        shards, mesh=mesh, in_specs=placed, out_specs=P(None, ("rows", "cluster")), check_vma=False
    )
```
